32 devices in a mesh: dp: 8 (over z, x), mp: 4 (over y, core).
Axes of the slice: x: 2, y: 2, z: 4, core: 2. Of those that a mesh axis runs over, the one named last changes fastest.
Arguments:
- token_ids: int32 [8, 1024], P('dp'), may hold values from 0 to 50687
- target_ids: int32 [8, 1024], P('dp'), may hold values from 0 to 50687
- loss_mask: int32 [8, 1024], P('dp'), may hold values from 0 to 1, as said below
- lengths: int32 [8], P('dp'), may hold values from 128 to 1024, as said below
- step_count: int32 [1], replicated, may hold values from 2 to 20
- table: float32 [50688, 1024], P(('dp', 'mp')), may hold values from -1 to 1
- positions: float32 [1024, 1024], P('dp'), may hold values from -1 to 1
- attn_in: float32 [3, 1024, 1024], P(None, 'dp', 'mp'), may hold values from -0.1875 to 0.1875
- attn_out: float32 [1024, 1024], P('dp', 'mp'), may hold values from -0.1875 to 0.1875
- mlp_in: float32 [1024, 4096], P('dp', 'mp'), may hold values from -0.1875 to 0.1875
- mlp_out: float32 [1024, 4096], P('dp', 'mp'), may hold values from -0.0234375 to 0.0234375
- norms: float32 [6, 1024], P(None, 'dp'), may hold values from -1.2 to 1.6, as said below
- table_first: float32 [50688, 1024], P(('dp', 'mp')), may hold values from -8.34465e-07 to 8.34465e-07
- positions_first: float32 [1024, 1024], P('dp'), may hold values from -8.34465e-07 to 8.34465e-07
- attn_in_first: float32 [3, 1024, 1024], P(None, 'dp', 'mp'), may hold values from -8.34465e-07 to 8.34465e-07
- attn_out_first: float32 [1024, 1024], P('dp', 'mp'), may hold values from -8.34465e-07 to 8.34465e-07
- mlp_in_first: float32 [1024, 4096], P('dp', 'mp'), may hold values from -8.34465e-07 to 8.34465e-07
- mlp_out_first: float32 [1024, 4096], P('dp', 'mp'), may hold values from -8.34465e-07 to 8.34465e-07
- norms_first: float32 [6, 1024], P(None, 'dp'), may hold values from -2.3841858e-06 to 2.3841858e-06
- table_second: float32 [50688, 1024], P(('dp', 'mp')), may hold values from 1.5257359e-15 to 6.1029435e-15
- positions_second: float32 [1024, 1024], P('dp'), may hold values from 1.5257359e-15 to 6.1029435e-15
- attn_in_second: float32 [3, 1024, 1024], P(None, 'dp', 'mp'), may hold values from 1.5257359e-15 to 6.1029435e-15
- attn_out_second: float32 [1024, 1024], P('dp', 'mp'), may hold values from 1.5257359e-15 to 6.1029435e-15
- mlp_in_second: float32 [1024, 4096], P('dp', 'mp'), may hold values from 1.5257359e-15 to 6.1029435e-15
- mlp_out_second: float32 [1024, 4096], P('dp', 'mp'), may hold values from 1.5257359e-15 to 6.1029435e-15
- norms_second: float32 [6, 1024], P(None, 'dp'), may hold values from 1.5257359e-14 to 6.1029435e-14
Outputs:
- loss: float32 [], replicated
- grad_norm: float32 [], replicated
- table_new: float32 [50688, 1024], P(('dp', 'mp'))
- positions_new: float32 [1024, 1024], P('dp')
- attn_in_new: float32 [3, 1024, 1024], P(None, 'dp', 'mp')
- attn_out_new: float32 [1024, 1024], P('dp', 'mp')
- mlp_in_new: float32 [1024, 4096], P('dp', 'mp')
- mlp_out_new: float32 [1024, 4096], P('dp', 'mp')
- norms_new: float32 [6, 1024], P(None, 'dp')
- table_first_new: float32 [50688, 1024], P(('dp', 'mp'))
- positions_first_new: float32 [1024, 1024], P('dp')
- attn_in_first_new: float32 [3, 1024, 1024], P(None, 'dp', 'mp')
- attn_out_first_new: float32 [1024, 1024], P('dp', 'mp')
- mlp_in_first_new: float32 [1024, 4096], P('dp', 'mp')
- mlp_out_first_new: float32 [1024, 4096], P('dp', 'mp')
- norms_first_new: float32 [6, 1024], P(None, 'dp')
- table_second_new: float32 [50688, 1024], P(('dp', 'mp'))
- positions_second_new: float32 [1024, 1024], P('dp')
- attn_in_second_new: float32 [3, 1024, 1024], P(None, 'dp', 'mp')
- attn_out_second_new: float32 [1024, 1024], P('dp', 'mp')
- mlp_in_second_new: float32 [1024, 4096], P('dp', 'mp')
- mlp_out_second_new: float32 [1024, 4096], P('dp', 'mp')
- norms_second_new: float32 [6, 1024], P(None, 'dp')
The draws below stay inside these ranges and needn't reach their ends.
Inputs may be any that keep to these rules, and one draw needn't show every extreme that they name: `lengths`: one sequence of every draw has length 1024. `loss_mask`: zero at positions at or past a slot's length; one at position 0. `norms`: rows 0, 2, 4 are gains, rows 1, 3, 5 shifts.
All inputs are finite; a program needn't handle non-finite values.
Results may differ from the reference program's by a relative error of at most 0.012.
Values may be sent and summed in bfloat16 or wider, within the bound.
A program may use at most 224 MiB of HBM per device.

```python
import math
import jax
import jax.numpy as jnp
import numpy as np
from jax import lax

D = 1024
HEADS = 16
HD = 64
FF = 4096
VOCAB = 50688
SEQ_LEN = 1024
MIN_LEN = 128
SEQS = 8


def draw_shared(key):
    length_key = jax.random.fold_in(key, 11)
    spot_key = jax.random.fold_in(key, 12)
    mask_key = jax.random.fold_in(key, 13)
    raw_draw = jax.random.randint(length_key, (SEQS,), 0, 1000)
    extra_len = (SEQ_LEN - MIN_LEN) * (raw_draw * raw_draw // 1000) * raw_draw // 1000000
    seq_lengths = MIN_LEN + extra_len
    spot_index = jax.random.randint(spot_key, (), 0, SEQS)
    seq_lengths = jnp.where(jnp.arange(SEQS) == spot_index, SEQ_LEN, seq_lengths).astype(jnp.int32)
    keep_draw = jax.random.randint(mask_key, (SEQS, SEQ_LEN), 0, 20) < 17
    place_index = jnp.arange(SEQ_LEN)[None, :]
    mask_bits = (place_index < seq_lengths[:, None]) & keep_draw | (place_index == 0)
    return (seq_lengths, mask_bits.astype(jnp.int32))


def draw_lengths(key, part):
    return draw_shared(key)[0]


def draw_loss_mask(key, part):
    return draw_shared(key)[1]


def draw_norms(key, part):
    noise_draw = jnp.clip(jax.random.normal(key, (6, D), jnp.float32), -4.0, 4.0)
    is_gain = (jnp.arange(6) % 2 == 0)[:, None]
    return jnp.where(is_gain, 1.0 + 0.15 * noise_draw, 0.3 * noise_draw)


def set_ends(result, key, least, largest):
    index_at = [jax.random.randint(jax.random.fold_in(key, axis), (), 0, length) for axis, length in enumerate(result.shape)]
    main_axis = result.shape.index(max(result.shape))
    neighbour = index_at[:main_axis] + [(index_at[main_axis] + 1) % result.shape[main_axis]] + index_at[main_axis + 1:]
    return result.at[tuple(index_at)].set(least).at[tuple(neighbour)].set(largest)


def steps_of(key, extent, pieces, least, top_value):
    gain, own = 1.0, jax.random.fold_in(key, 6)
    for axis_at, blocks in pieces:
        steps = jnp.exp(jax.random.uniform(jax.random.fold_in(own, axis_at), (blocks,), jnp.float32, least / len(pieces), top_value / len(pieces)))
        gain = gain * jnp.repeat(steps, extent[axis_at] // blocks).reshape([-1 if axis == axis_at else 1 for axis in range(len(extent))])
    return gain


def rank_bounds(count, skew):
    loads = [(1 << 20) // math.isqrt(rank ** skew) + 1 for rank in range(1, count + 1)]
    scale = 1 + sum(loads) // (1 << 30)
    return np.cumsum(np.array([max(1, weight // scale) for weight in loads]))


def ranked_ids(key, dims, count, slope):
    grid = rank_bounds(count, slope)
    pick = jax.random.randint(jax.random.fold_in(key, 1), dims, 0, int(grid[count - 1]))
    standing = jnp.searchsorted(jnp.asarray(grid, jnp.int32), pick, side="right")
    return jax.random.permutation(jax.random.fold_in(key, 2), count)[standing].astype(jnp.int32)


def noise(key, shape, deviation, reach, split=(), dtype=jnp.bfloat16):
    result = jax.random.normal(key, shape, jnp.float32) * deviation
    if len(split) > 0:
        result = steps_of(key, shape, split, -0.22, 0.18) * result
    return jnp.clip(result, min=-reach, max=reach).astype(dtype)


def setup_inputs(seed: int = 0) -> dict:
    splits = jax.random.split(jax.random.key(seed), 27)
    return {
        "token_ids": set_ends(ranked_ids(splits[0], (SEQS, SEQ_LEN), VOCAB, 2), jax.random.fold_in(splits[0], 3), 0, VOCAB - 1).astype(jnp.int32),
        "target_ids": set_ends(ranked_ids(splits[1], (SEQS, SEQ_LEN), VOCAB, 2), jax.random.fold_in(splits[1], 3), 0, VOCAB - 1).astype(jnp.int32),
        "loss_mask": draw_loss_mask(jax.random.fold_in(splits[26], 71), 0),
        "lengths": draw_lengths(jax.random.fold_in(splits[26], 71), 0),
        "step_count": jax.random.randint(splits[4], (1,), 2, 21).astype(jnp.int32),
        "table": noise(splits[5], (VOCAB, D), (2.0 * D ** -0.5), 1.0, ((0, 32),), jnp.float32),
        "positions": noise(splits[6], (SEQ_LEN, D), (2.0 * D ** -0.5), 1.0, ((0, 8),), jnp.float32),
        "attn_in": noise(splits[7], (3, D, D), D ** -0.5, 0.1875, ((1, 8), (2, 4)), jnp.float32),
        "attn_out": noise(splits[8], (D, D), D ** -0.5, 0.1875, ((0, 8), (1, 4)), jnp.float32),
        "mlp_in": noise(splits[9], (D, FF), D ** -0.5, 0.1875, ((0, 8), (1, 4)), jnp.float32),
        "mlp_out": noise(splits[10], (D, FF), (16 * FF) ** -0.5, 0.0234375, ((0, 8), (1, 4)), jnp.float32),
        "norms": draw_norms(jax.random.fold_in(splits[26], 71), 0),
        "table_first": noise(splits[12], (VOCAB, D), (0.0011 * (VOCAB * D + SEQ_LEN * D + 4 * D * D + 2 * D * FF + 6 * D) ** -0.5), 8.344650268554688e-07, ((0, 32),), jnp.float32),
        "positions_first": noise(splits[13], (SEQ_LEN, D), (0.0011 * (VOCAB * D + SEQ_LEN * D + 4 * D * D + 2 * D * FF + 6 * D) ** -0.5), 8.344650268554688e-07, ((0, 8),), jnp.float32),
        "attn_in_first": noise(splits[14], (3, D, D), (0.0011 * (VOCAB * D + SEQ_LEN * D + 4 * D * D + 2 * D * FF + 6 * D) ** -0.5), 8.344650268554688e-07, ((1, 8), (2, 4)), jnp.float32),
        "attn_out_first": noise(splits[15], (D, D), (0.0011 * (VOCAB * D + SEQ_LEN * D + 4 * D * D + 2 * D * FF + 6 * D) ** -0.5), 8.344650268554688e-07, ((0, 8), (1, 4)), jnp.float32),
        "mlp_in_first": noise(splits[16], (D, FF), (0.0011 * (VOCAB * D + SEQ_LEN * D + 4 * D * D + 2 * D * FF + 6 * D) ** -0.5), 8.344650268554688e-07, ((0, 8), (1, 4)), jnp.float32),
        "mlp_out_first": noise(splits[17], (D, FF), (0.0011 * (VOCAB * D + SEQ_LEN * D + 4 * D * D + 2 * D * FF + 6 * D) ** -0.5), 8.344650268554688e-07, ((0, 8), (1, 4)), jnp.float32),
        "norms_first": noise(splits[18], (6, D), (0.0033 * (VOCAB * D + SEQ_LEN * D + 4 * D * D + 2 * D * FF + 6 * D) ** -0.5), 2.384185791015625e-06, ((1, 8),), jnp.float32),
        "table_second": jnp.clip(jnp.exp(math.log(6.102943535734803e-15) - 1.3862944 * jax.random.uniform(splits[19], (VOCAB, D), jnp.float32) ** steps_of(splits[19], (VOCAB, D), ((0, 32),), -0.2, 0.2)), 1.5257358839337008e-15, 6.102943535734803e-15),
        "positions_second": jnp.clip(jnp.exp(math.log(6.102943535734803e-15) - 1.3862944 * jax.random.uniform(splits[20], (SEQ_LEN, D), jnp.float32) ** steps_of(splits[20], (SEQ_LEN, D), ((0, 8),), -0.2, 0.2)), 1.5257358839337008e-15, 6.102943535734803e-15),
        "attn_in_second": jnp.clip(jnp.exp(math.log(6.102943535734803e-15) - 1.3862944 * jax.random.uniform(splits[21], (3, D, D), jnp.float32) ** steps_of(splits[21], (3, D, D), ((1, 8), (2, 4)), -0.2, 0.2)), 1.5257358839337008e-15, 6.102943535734803e-15),
        "attn_out_second": jnp.clip(jnp.exp(math.log(6.102943535734803e-15) - 1.3862944 * jax.random.uniform(splits[22], (D, D), jnp.float32) ** steps_of(splits[22], (D, D), ((0, 8), (1, 4)), -0.2, 0.2)), 1.5257358839337008e-15, 6.102943535734803e-15),
        "mlp_in_second": jnp.clip(jnp.exp(math.log(6.102943535734803e-15) - 1.3862944 * jax.random.uniform(splits[23], (D, FF), jnp.float32) ** steps_of(splits[23], (D, FF), ((0, 8), (1, 4)), -0.2, 0.2)), 1.5257358839337008e-15, 6.102943535734803e-15),
        "mlp_out_second": jnp.clip(jnp.exp(math.log(6.102943535734803e-15) - 1.3862944 * jax.random.uniform(splits[24], (D, FF), jnp.float32) ** steps_of(splits[24], (D, FF), ((0, 8), (1, 4)), -0.2, 0.2)), 1.5257358839337008e-15, 6.102943535734803e-15),
        "norms_second": jnp.clip(jnp.exp(math.log(6.102943535734803e-14) - 1.3862944 * jax.random.uniform(splits[25], (6, D), jnp.float32) ** steps_of(splits[25], (6, D), ((1, 8),), -0.2, 0.2)), 1.5257358839337008e-14, 6.102943535734803e-14),
    }


@jax.custom_vjp
def low(v):
    return lax.optimization_barrier(v.astype(jnp.bfloat16)).astype(jnp.float32)

@jax.custom_vjp
def low_back(v):
    return v

def low_keep(v):
    return (low(v), None)

def low_pass(kept, grad):
    return (grad,)

def back_keep(v):
    return (v, None)

def back_low(kept, grad):
    return (low(grad),)
low.defvjp(low_keep, low_pass)
low_back.defvjp(back_keep, back_low)
highest = lax.Precision.HIGHEST
smoothing = 0.1
clip_norm = 0.01
beta_one = 0.9
beta_two = 0.999
adam_eps = 1e-08
learn_rates = (0.06, 0.06, 0.03, 0.03, 0.03, 0.004, 0.3)
decay_rates = (0.1, 0.0, 0.1, 0.1, 0.1, 0.1, 0.0)

def layer_norm(values, gain_row, shift_row):
    centered = values - lax.optimization_barrier(jnp.mean(values, axis=-1, keepdims=True))
    spread = lax.optimization_barrier(jnp.mean(centered * centered, axis=-1, keepdims=True))
    return centered * lax.rsqrt(spread + 1e-05) * gain_row + shift_row

def adam_update(weight, first_moment, second, grad_item, rate, decay, step_float):
    first_new = beta_one * first_moment + (1.0 - beta_one) * grad_item
    second_new = beta_two * second + (1.0 - beta_two) * grad_item * grad_item
    first_hat = first_new / (1.0 - beta_one ** step_float)
    second_hat = second_new / (1.0 - beta_two ** step_float)
    weight_new = weight - rate * (first_hat / (jnp.sqrt(second_hat) + adam_eps) + decay * weight)
    return (weight_new, first_new, second_new)

def attend_sequence(normed, attn_in_low, length):
    project = jnp.einsum('td,kde->kte', normed, attn_in_low, precision=highest)
    project = low_back(low(project))
    queries = project[0].reshape(SEQ_LEN, HEADS, HD)
    keys_all = project[1].reshape(SEQ_LEN, HEADS, HD)
    values_all = project[2].reshape(SEQ_LEN, HEADS, HD)
    scores = jnp.einsum('qhe,khe->hqk', queries, keys_all, precision=highest) * HD ** (-0.5)
    scores = low_back(scores)
    place = jnp.arange(SEQ_LEN)
    allowed = (place[None, :] <= place[:, None]) & (place[None, :] < length)
    scores = jnp.where(allowed[None], scores, -1e+30)
    weights = low(jax.nn.softmax(scores, axis=-1))
    mixed = jnp.einsum('hqk,khe->qhe', weights, values_all, precision=highest)
    return low_back(low(mixed.reshape(SEQ_LEN, D)))

def head_sequence(hidden, targets, mask_row, table_low):
    logits = low_back(jnp.dot(hidden, table_low.T, precision=highest))
    log_total = jax.nn.logsumexp(logits, axis=-1)
    picked = jnp.take_along_axis(logits, targets[:, None], axis=1)[:, 0]
    losses = log_total - (1.0 - smoothing) * picked - smoothing * lax.optimization_barrier(jnp.mean(logits, axis=-1))
    return jnp.sum(losses * mask_row)

def forward(table, positions, attn_in, attn_out, mlp_in, mlp_out, norms, token_ids, target_ids, mask_float, lengths):
    table_low = low(table)
    positions_low = low(positions)
    attn_in_low = low(attn_in)
    attn_out_low = low(attn_out)
    mlp_in_low = low(mlp_in)
    mlp_out_low = low(mlp_out)
    gain_rows = low(norms)
    start_rows = table_low[token_ids] + positions_low[None]
    normed_one = low(layer_norm(start_rows, gain_rows[0], gain_rows[1]))

    def attend_one(packed):
        return attend_sequence(packed[0], attn_in_low, packed[1])
    attended = lax.map(jax.checkpoint(attend_one), (normed_one, lengths))
    attn_branch = low_back(jnp.einsum('std,ed->ste', attended, attn_out_low, precision=highest))
    middle = start_rows + attn_branch
    normed_two = low(layer_norm(middle, gain_rows[2], gain_rows[3]))
    pre_gelu = low_back(jnp.einsum('std,df->stf', normed_two, mlp_in_low, precision=highest))
    activated = low(jax.nn.gelu(pre_gelu, approximate=True))
    mlp_branch = low_back(jnp.einsum('stf,df->std', activated, mlp_out_low, precision=highest))
    last_rows = middle + mlp_branch
    hidden = low(layer_norm(last_rows, gain_rows[4], gain_rows[5]))

    def head_one(packed):
        return head_sequence(packed[0], packed[1], packed[2], table_low)
    sums = lax.map(jax.checkpoint(head_one), (hidden, target_ids, mask_float))
    return jnp.sum(sums)

def reference(token_ids, target_ids, loss_mask, lengths, step_count, table, positions, attn_in, attn_out, mlp_in, mlp_out, norms, table_first, positions_first, attn_in_first, attn_out_first, mlp_in_first, mlp_out_first, norms_first, table_second, positions_second, attn_in_second, attn_out_second, mlp_in_second, mlp_out_second, norms_second):
    mask_float = loss_mask.astype(jnp.float32)
    token_total = jnp.sum(mask_float)

    def loss_of(table_w, positions_w, attn_in_w, attn_out_w, mlp_in_w, mlp_out_w, norms_w):
        summed = forward(table_w, positions_w, attn_in_w, attn_out_w, mlp_in_w, mlp_out_w, norms_w, token_ids, target_ids, mask_float, lengths)
        return summed / token_total
    loss, pullback = jax.vjp(loss_of, table, positions, attn_in, attn_out, mlp_in, mlp_out, norms)
    grads = pullback(jnp.ones_like(loss))
    masters = (table, positions, attn_in, attn_out, mlp_in, mlp_out, norms)
    firsts = (table_first, positions_first, attn_in_first, attn_out_first, mlp_in_first, mlp_out_first, norms_first)
    seconds = (table_second, positions_second, attn_in_second, attn_out_second, mlp_in_second, mlp_out_second, norms_second)
    square_sum = sum((jnp.sum(grad_item * grad_item) for grad_item in grads))
    grad_norm = jnp.sqrt(square_sum)
    factor = jnp.minimum(1.0, clip_norm / (grad_norm + 1e-06))
    step_float = step_count[0].astype(jnp.float32)
    updated = [adam_update(masters[number], firsts[number], seconds[number], factor * grads[number], learn_rates[number], decay_rates[number], step_float) for number in range(7)]
    return (loss, grad_norm, updated[0][0], updated[1][0], updated[2][0], updated[3][0], updated[4][0], updated[5][0], updated[6][0], updated[0][1], updated[1][1], updated[2][1], updated[3][1], updated[4][1], updated[5][1], updated[6][1], updated[0][2], updated[1][2], updated[2][2], updated[3][2], updated[4][2], updated[5][2], updated[6][2])
```

```python
import functools

import jax
import jax.numpy as jnp
from jax import lax
from jax.experimental import pallas as pl
from jax.experimental.pallas import tpu as pltpu
from jax.sharding import PartitionSpec as P

HD = 64
VOCAB = 50688
MESH = pl.DeviceIdType.MESH
ANY = pl.ANY
VMEM = pltpu.VMEM
BF = jnp.bfloat16
F32 = jnp.float32

smoothing = 0.1
clip_norm = 0.01
beta_one = 0.9
beta_two = 0.999
adam_eps = 1e-08
learn_rates = (0.06, 0.06, 0.03, 0.03, 0.03, 0.004, 0.3)
decay_rates = (0.1, 0.0, 0.1, 0.1, 0.1, 0.1, 0.0)


def layer_norm(values, gain_row, shift_row):
    centered = values - jnp.mean(values, axis=-1, keepdims=True)
    spread = jnp.mean(centered * centered, axis=-1, keepdims=True)
    return centered * lax.rsqrt(spread + 1e-05) * gain_row + shift_row


def gelu_tanh(values):
    return jax.nn.gelu(values, approximate=True)


def adam_update(weight, first_moment, second, grad_item, rate, decay, step_float):
    first_new = beta_one * first_moment + (1.0 - beta_one) * grad_item
    second_new = beta_two * second + (1.0 - beta_two) * grad_item * grad_item
    first_hat = first_new / (1.0 - beta_one**step_float)
    second_hat = second_new / (1.0 - beta_two**step_float)
    weight_new = weight - rate * (first_hat / (jnp.sqrt(second_hat) + adam_eps) + decay * weight)
    return (weight_new, first_new, second_new)


def contract_rows(left, right):
    return lax.dot_general(
        left, right, (((0,), (0,)), ((), ())), preferred_element_type=F32
    )


def contract_cols(left, right):
    return lax.dot_general(
        left, right, (((1,), (1,)), ((), ())), preferred_element_type=F32
    )


def dot_nn(left, right):
    return lax.dot_general(
        left, right, (((1,), (0,)), ((), ())), preferred_element_type=F32
    )


def place():
    dp = lax.axis_index("dp")
    mp = lax.axis_index("mp")
    return dp // 2, dp % 2, mp // 2, mp % 2


def device(z, x, y, c):
    return (z * 2 + x, y * 2 + c)


def block_index(z, x, y, c):
    return ((z * 2 + x) * 2 + y) * 2 + c


def flip(bit, by):
    return bit + by - 2 * bit * by


def flipped(x, y, core, j):
    first, second = j % 2, j // 2
    by_x = first * (1 - core) + second * core
    by_y = second * (1 - core) + first * core
    return flip(x, by_x), flip(y, by_y)


def greet(peers):
    barrier = pltpu.get_barrier_semaphore()
    for peer in peers:
        pl.semaphore_signal(barrier, inc=1, device_id=peer, device_id_type=MESH)
    pl.semaphore_wait(barrier, len(peers))


def remote(src, dst, send_sem, recv_sem, peer):
    return pltpu.make_async_remote_copy(
        src_ref=src,
        dst_ref=dst,
        send_sem=send_sem,
        recv_sem=recv_sem,
        device_id=peer,
        device_id_type=MESH,
    )


def to_column(row):
    wide = jnp.broadcast_to(row, (128, row.shape[1]))
    return jnp.transpose(wide)[:, :1]


def to_row(column):
    wide = jnp.broadcast_to(column, (column.shape[0], 128))
    return jnp.transpose(wide)[:1, :]


def gather_scratch(depth):
    return [
        pltpu.SemaphoreType.DMA((1,)),
        pltpu.SemaphoreType.DMA((depth - 1,)),
        pltpu.SemaphoreType.DMA((depth - 1,)),
        pltpu.SemaphoreType.DMA((depth,)),
        pltpu.SemaphoreType.DMA((depth,)),
        pltpu.SemaphoreType.DMA((2 * depth,)),
        pltpu.SemaphoreType.DMA((2 * depth,)),
        pltpu.SemaphoreType.DMA((4 * depth,)),
        pltpu.SemaphoreType.DMA((4 * depth,)),
    ]


def gather_blocks(depth, own_ref, land, sems, consume):
    lsem, zs, zr, ps, pr, qs, qr, cs, cr = sems
    z, x, y, c = place()
    other = 1 - c
    p_peer = device(z, flip(x, 1 - c), flip(y, c), c)
    q_peer = device(z, flip(x, c), flip(y, 1 - c), c)
    c_peer = device(z, x, y, other)

    def z_peer(k):
        return device((z + k) % depth, x, y, c)

    def block(k, j, core):
        bx, by = flipped(x, y, core, j)
        return block_index((z + depth - k) % depth, bx, by, core)

    def copy(index, send_sem, recv_sem, peer):
        return remote(land.at[index], land.at[index], send_sem, recv_sem, peer)

    greet([z_peer(k) for k in range(1, depth)] + [p_peer, q_peer, c_peer])
    own = block_index(z, x, y, c)
    local = pltpu.make_async_copy(own_ref, land.at[own], lsem.at[0])
    local.start()
    local.wait()
    for k in range(1, depth):
        copy(own, zs.at[k - 1], zr.at[k - 1], z_peer(k)).start()

    def first(k):
        index = block(k, 0, c)
        copy(index, ps.at[k], pr.at[k], p_peer).start()
        copy(index, qs.at[2 * k], qr.at[2 * k], q_peer).start()
        copy(index, cs.at[4 * k], cr.at[4 * k], c_peer).start()

    first(0)

    def both(k, j):
        def one(i, inner):
            index = block(k, j, flip(c, i))

            @pl.when(i == 1)
            def _():
                copy(index, cs.at[4 * k + j], cr.at[4 * k + j], c_peer).wait_recv()

            consume(index, (4 * k + j) * 2 + i)
            return inner

        lax.fori_loop(0, 2, one, 0)

    def step(k, carry):
        index = block(k, 1, c)
        copy(index, ps.at[k], pr.at[k], p_peer).wait_recv()
        copy(index, qs.at[2 * k + 1], qr.at[2 * k + 1], q_peer).start()
        copy(index, cs.at[4 * k + 1], cr.at[4 * k + 1], c_peer).start()

        @pl.when(k < depth - 1)
        def _():
            copy(block(k + 1, 0, c), zs.at[k], zr.at[k], c_peer).wait_recv()
            first(k + 1)

        def stage(j, inner):
            @pl.when(j >= 2)
            def _():
                arrived = block(k, j, c)
                copy(arrived, qs.at[2 * k + j - 2], qr.at[2 * k + j - 2], q_peer).wait_recv()
                copy(arrived, cs.at[4 * k + j], cr.at[4 * k + j], c_peer).start()

            both(k, j)
            return inner

        lax.fori_loop(0, 4, stage, 0)
        return carry

    lax.fori_loop(0, depth, step, 0)

    for k in range(1, depth):
        copy(own, zs.at[k - 1], zr.at[k - 1], c_peer).wait_send()

    def drain(k, carry):
        copy(own, ps.at[k], pr.at[k], p_peer).wait_send()
        for j in range(2):
            copy(own, qs.at[2 * k + j], qr.at[2 * k + j], q_peer).wait_send()
        for j in range(4):
            copy(own, cs.at[4 * k + j], cr.at[4 * k + j], c_peer).wait_send()
        return carry

    lax.fori_loop(0, depth, drain, 0)


def reduce_scratch(depth, rows, width):
    return [
        VMEM((4 * depth, rows, width), BF),
        VMEM((4 * depth, rows, width), BF),
        VMEM((4 * depth, rows, width), BF),
        VMEM((2 * depth, rows, width), BF),
        VMEM((depth, rows, width), BF),
        VMEM((depth - 1, rows, width), BF),
        pltpu.SemaphoreType.DMA((depth - 1,)),
        pltpu.SemaphoreType.DMA((depth - 1,)),
        pltpu.SemaphoreType.DMA((depth,)),
        pltpu.SemaphoreType.DMA((depth,)),
        pltpu.SemaphoreType.DMA((2 * depth,)),
        pltpu.SemaphoreType.DMA((2 * depth,)),
        pltpu.SemaphoreType.DMA((4 * depth,)),
        pltpu.SemaphoreType.DMA((4 * depth,)),
    ]


def reduce_blocks(depth, out_ref, scratch, produce, start=None):
    own, oth, cbuf, qbuf, pbuf, zbuf, zs, zr, ps, pr, qs, qr, cs, cr = scratch
    z, x, y, c = place()
    other = 1 - c
    p_peer = device(z, flip(x, 1 - c), flip(y, c), c)
    q_peer = device(z, flip(x, c), flip(y, 1 - c), c)
    c_peer = device(z, x, y, other)

    def z_peer(s):
        return device((z + s + 1) % depth, x, y, c)

    def c_copy(slot):
        return remote(oth.at[slot], cbuf.at[slot], cs.at[slot], cr.at[slot], c_peer)

    def q_copy(s, jp):
        return remote(
            own.at[4 * s + 2 + jp], qbuf.at[2 * s + jp], qs.at[2 * s + jp], qr.at[2 * s + jp], q_peer
        )

    def p_copy(s):
        return remote(own.at[4 * s + 1], pbuf.at[s], ps.at[s], pr.at[s], p_peer)

    def z_copy(s):
        return remote(own.at[4 * s], zbuf.at[s], zs.at[s], zr.at[s], z_peer(s))

    def target(n):
        s, i = n // 8, n % 8
        j = (i // 2 + 2) % 4
        to_other = 1 - i % 2
        core = flip(c, to_other)
        bx, by = flipped(x, y, core, j)
        return block_index((z + s + 1) % depth, bx, by, core)

    greet([z_peer(s) for s in range(depth - 1)] + [p_peer, q_peer, c_peer])
    if start is not None:
        start(target)

    def add(slot, ref):
        own[slot] = (own[slot].astype(F32) + ref.astype(F32)).astype(BF)

    def make(s):
        def one(i, carry):
            n = s * 8 + i
            j = (i // 2 + 2) % 4
            value = produce(n, target(n))

            @pl.when(i % 2 == 0)
            def _():
                oth[4 * s + j] = value
                c_copy(4 * s + j).start()

            @pl.when(i % 2 == 1)
            def _():
                own[4 * s + j] = value

            return carry

        lax.fori_loop(0, 8, one, 0)

    def pair(s):
        for j in (2, 3, 0, 1):
            c_copy(4 * s + j).wait_recv()
            add(4 * s + j, cbuf[4 * s + j])
            if j >= 2:
                q_copy(s, j - 2).start()

    def second(s):
        q_copy(s, 1).wait_recv()
        add(4 * s + 1, qbuf[2 * s + 1])
        p_copy(s).start()
        q_copy(s, 0).wait_recv()
        add(4 * s, qbuf[2 * s])

    def third(s):
        p_copy(s).wait_recv()
        add(4 * s, pbuf[s])

        @pl.when(s < depth - 1)
        def _():
            z_copy(s).start()

    def step(t, carry):
        @pl.when(t < depth)
        def _():
            make(t)
            pair(t)

        @pl.when((t >= 1) & (t <= depth))
        def _():
            second(t - 1)

        @pl.when(t >= 2)
        def _():
            third(t - 2)

        return carry

    lax.fori_loop(0, depth + 2, step, 0)
    total = own[4 * (depth - 1)].astype(F32)
    for s in range(depth - 1):
        z_copy(s).wait_recv()
        total = total + zbuf[s].astype(F32)
    out_ref[...] = total.astype(out_ref.dtype)
    for s in range(depth - 1):
        z_copy(s).wait_send()

    def drain(s, carry):
        p_copy(s).wait_send()
        for j in range(2):
            q_copy(s, j).wait_send()
        for j in range(4):
            c_copy(4 * s + j).wait_send()
        return carry

    lax.fori_loop(0, depth, drain, 0)


def comm_params(number, limit_mib=60):
    return pltpu.CompilerParams(
        collective_id=number, has_side_effects=True, vmem_limit_bytes=limit_mib << 20
    )


def vspec():
    return pl.BlockSpec(memory_space=VMEM)


def aspec():
    return pl.BlockSpec(memory_space=ANY)


def embed_kernel(depth, table_ref, ids_ref, out_ref, *scratch):
    def produce(n, block):
        wanted = to_column(ids_ref[block])
        rows = wanted.shape[0]
        vocab = lax.broadcasted_iota(jnp.int32, (rows, table_ref.shape[0]), 1).astype(F32)
        onehot = (vocab == wanted).astype(F32).astype(BF)
        return dot_nn(onehot, table_ref[...]).astype(BF)

    reduce_blocks(depth, out_ref, scratch, produce)


def embed_call(depth, table_low, local_ids):
    blocks, unused, rows = local_ids.shape
    width = table_low.shape[1]
    return pl.pallas_call(
        functools.partial(embed_kernel, depth),
        out_shape=jax.ShapeDtypeStruct((rows, width), BF),
        in_specs=[vspec(), vspec()],
        out_specs=vspec(),
        scratch_shapes=reduce_scratch(depth, rows, width),
        compiler_params=comm_params(1),
        name="embed_exchange",
    )(table_low, local_ids)


def combine_logs(first, second):
    top = jnp.maximum(first, second)
    return top + jnp.log(jnp.exp(first - top) + jnp.exp(second - top))


def logits_kernel(
    depth, hidden_ref, table_ref, targets_ref, all_ref, expo_ref, top_ref, total_ref, picked_ref,
    land, stage, snap, got, out_sem, all_sem, xs, xr, *sems
):
    z, x, y, c = place()
    blocks = land.shape[0]

    def out_copy(slot, block):
        return pltpu.make_async_copy(stage.at[slot], expo_ref.at[block], out_sem.at[slot])

    def keep(block):
        return pltpu.make_async_copy(land.at[block], all_ref.at[block], all_sem.at[block])

    def consume(block, number):
        slot = number % 2
        keep(block).start()
        logits = contract_cols(land[block], table_ref[...])
        top = jnp.max(logits, axis=1, keepdims=True)
        expo = jnp.exp(logits - top)
        total = jnp.sum(expo, axis=1, keepdims=True)
        wanted = to_column(targets_ref[block])
        vocab = lax.broadcasted_iota(jnp.int32, logits.shape, 1).astype(F32)
        picked = jnp.sum(jnp.where(vocab == wanted, logits, 0.0), axis=1, keepdims=True)
        top_row = to_row(top)
        top_ref[block] = top_row
        picked_ref[block] = to_row(picked)
        total_ref[block] = top_row + jnp.log(to_row(total))

        @pl.when(number >= 2)
        def _():
            out_copy(slot, block).wait()

        stage[slot] = expo.astype(BF)
        out_copy(slot, block).start()

    gather_blocks(depth, hidden_ref, land, sems, consume)
    peers = [device(z, x, y, 1 - c), device(z, x, 1 - y, c), device(z, 1 - x, y, c)]
    for number, peer in enumerate(peers):
        snap[number] = total_ref[...]
        copy = remote(snap.at[number], got.at[number], xs.at[number], xr.at[number], peer)
        copy.start()
        copy.wait()
        total_ref[...] = combine_logs(snap[number], got[number])
    snap[3] = total_ref[...]
    copies = [
        remote(
            snap.at[3], got.at[2 + k], xs.at[2 + k], xr.at[2 + k], device((z + k) % depth, x, y, c)
        )
        for k in range(1, depth)
    ]
    for copy in copies:
        copy.start()
    for k, copy in enumerate(copies):
        copy.wait()
        total_ref[...] = combine_logs(total_ref[...], got[3 + k])
    for slot in range(2):
        out_copy(slot, 0).wait()

    def kept(block, carry):
        keep(block).wait()
        return carry

    lax.fori_loop(0, blocks, kept, 0)


def logits_call(depth, hidden, table_low, targets):
    blocks, unused, rows = targets.shape
    shard, width = table_low.shape
    row_shape = jax.ShapeDtypeStruct((blocks, 1, rows), F32)
    return pl.pallas_call(
        functools.partial(logits_kernel, depth),
        out_shape=(
            jax.ShapeDtypeStruct((blocks, rows, width), BF),
            jax.ShapeDtypeStruct((blocks, rows, shard), BF),
            row_shape,
            row_shape,
            row_shape,
        ),
        in_specs=[vspec(), vspec(), vspec()],
        out_specs=(aspec(), aspec(), vspec(), vspec(), vspec()),
        scratch_shapes=[
            VMEM((blocks, rows, width), BF),
            VMEM((2, rows, shard), BF),
            VMEM((4, blocks, 1, rows), F32),
            VMEM((2 + depth, blocks, 1, rows), F32),
            pltpu.SemaphoreType.DMA((2,)),
            pltpu.SemaphoreType.DMA((blocks,)),
            pltpu.SemaphoreType.DMA((2 + depth,)),
            pltpu.SemaphoreType.DMA((2 + depth,)),
        ]
        + gather_scratch(depth),
        compiler_params=comm_params(2),
        name="logits_exchange",
    )(hidden, table_low, targets)


def grads_kernel(
    depth, vocab_size, table_ref, targets_ref, weights_ref, top_ref, total_ref, expo_ref, out_ref, grad_ref,
    inbox, outbox, in_sem, out_sem, *scratch
):
    steps = 8 * depth

    def fetch(slot, block):
        return pltpu.make_async_copy(expo_ref.at[block], inbox.at[slot], in_sem.at[slot])

    def store(slot, block):
        return pltpu.make_async_copy(outbox.at[slot], grad_ref.at[block], out_sem.at[slot])

    targets = []

    def start(target):
        targets.append(target)
        fetch(0, target(0)).start()

    def produce(n, block):
        slot = n % 2
        fetch(slot, block).wait()

        @pl.when(n + 1 < steps)
        def _():
            fetch(1 - slot, targets[0](n + 1)).start()

        weight = weights_ref[block]
        scale = to_column(jnp.exp(top_ref[block] - total_ref[block]) * weight)
        wanted = to_column(targets_ref[block])
        weight = to_column(weight)
        vocab = lax.broadcasted_iota(jnp.int32, inbox.shape[1:], 1).astype(F32)
        low = -(smoothing / vocab_size) * weight
        hit = low - (1.0 - smoothing) * weight
        grad = inbox[slot].astype(F32) * scale + jnp.where(vocab == wanted, hit, low)
        grad = grad.astype(BF)

        @pl.when(n >= 2)
        def _():
            store(slot, block).wait()

        outbox[slot] = grad
        store(slot, block).start()
        return dot_nn(grad, table_ref[...]).astype(BF)

    reduce_blocks(depth, out_ref, scratch, produce, start)
    for slot in range(2):
        store(slot, 0).wait()


def grads_call(depth, vocab_size, table_low, targets, weights, top, total, expo):
    blocks, rows, shard = expo.shape
    width = table_low.shape[1]
    return pl.pallas_call(
        functools.partial(grads_kernel, depth, vocab_size),
        out_shape=(
            jax.ShapeDtypeStruct((rows, width), F32),
            jax.ShapeDtypeStruct((blocks, rows, shard), BF),
        ),
        in_specs=[vspec(), vspec(), vspec(), vspec(), vspec(), aspec()],
        out_specs=(vspec(), aspec()),
        scratch_shapes=[
            VMEM((2, rows, shard), BF),
            VMEM((2, rows, shard), BF),
            pltpu.SemaphoreType.DMA((2,)),
            pltpu.SemaphoreType.DMA((2,)),
        ]
        + reduce_scratch(depth, rows, width),
        compiler_params=comm_params(3),
        name="grads_exchange",
    )(table_low, targets, weights, top, total, expo)


def scatter_kernel(depth, rows, sent_ref, ids_ref, grad_ref, out_ref, pos_ref, rest_ref, land, *sems):
    out_ref[...] = grad_ref[...]
    shard = grad_ref.shape[0]

    def consume(block, number):
        vocab = lax.broadcasted_iota(jnp.int32, (shard, rows), 0).astype(F32)
        onehot = (vocab == ids_ref[block]).astype(F32).astype(BF)
        out_ref[...] += dot_nn(onehot, land[block, :rows, :])

    gather_blocks(depth, sent_ref, land, sems, consume)
    dp = lax.axis_index("dp")
    slots = 2 * depth
    span = pos_ref.shape[0]
    per = rows // span
    total = jnp.zeros(pos_ref.shape, F32)
    rest = jnp.zeros(rest_ref.shape, F32)
    first = pl.multiple_of((dp % per) * span, span)
    for slot in range(slots):
        total = total + land[slot * 4 + dp // per, pl.ds(first, span), :].astype(F32)
    pos_ref[...] = total
    for block in range(land.shape[0]):
        rest = rest + land[block, rows:, :].astype(F32)
    rest_ref[...] = rest


def scatter_call(depth, sent, ids, table_grad, span):
    blocks, unused, rows = ids.shape
    extended, width = sent.shape
    return pl.pallas_call(
        functools.partial(scatter_kernel, depth, rows),
        out_shape=(
            jax.ShapeDtypeStruct(table_grad.shape, F32),
            jax.ShapeDtypeStruct((span, width), F32),
            jax.ShapeDtypeStruct((extended - rows, width), F32),
        ),
        in_specs=[vspec(), vspec(), vspec()],
        out_specs=(vspec(), vspec(), vspec()),
        scratch_shapes=[VMEM((blocks, extended, width), BF)] + gather_scratch(depth),
        compiler_params=comm_params(4),
        name="rows_exchange",
    )(sent, ids, table_grad)


def group_gather_kernel(own_ref, out_ref, local_sem, send_sem, recv_sem):
    z, x, y, c = place()
    y_peer, c_peer = device(z, x, 1 - y, c), device(z, x, y, 1 - c)
    greet([y_peer, c_peer])
    own, across = y * 2 + c, (1 - y) * 2 + c
    to_y = remote(own_ref, out_ref.at[own], send_sem.at[0], recv_sem.at[0], y_peer)
    to_c = remote(own_ref, out_ref.at[own], send_sem.at[1], recv_sem.at[1], c_peer)
    on = remote(out_ref.at[across], out_ref.at[across], send_sem.at[2], recv_sem.at[2], c_peer)
    to_y.start()
    to_c.start()
    local = pltpu.make_async_copy(own_ref, out_ref.at[own], local_sem.at[0])
    local.start()
    to_y.wait_recv()
    on.start()
    local.wait()
    to_c.wait_recv()
    on.wait_recv()
    to_y.wait_send()
    to_c.wait_send()
    on.wait_send()


def group_gather(own, number):
    rows, width = own.shape
    out = pl.pallas_call(
        group_gather_kernel,
        out_shape=jax.ShapeDtypeStruct((4, rows, width), own.dtype),
        in_specs=[vspec()],
        out_specs=aspec(),
        scratch_shapes=[
            pltpu.SemaphoreType.DMA((1,)),
            pltpu.SemaphoreType.DMA((3,)),
            pltpu.SemaphoreType.DMA((3,)),
        ],
        compiler_params=comm_params(number),
        name="group_gather",
    )(own)
    return out.reshape(4 * rows, width)


def group_sum_kernel(parts_ref, out_ref, cbuf, ybuf, mixed, send_sem, recv_sem):
    z, x, y, c = place()
    y_peer, c_peer = device(z, x, 1 - y, c), device(z, x, y, 1 - c)
    greet([y_peer, c_peer])
    copies = [
        remote(parts_ref.at[row * 2 + 1 - c], cbuf.at[i], send_sem.at[i], recv_sem.at[i], c_peer)
        for i, row in enumerate((1 - y, y))
    ]
    for copy in copies:
        copy.start()
    copies[0].wait_recv()
    mixed[...] = (parts_ref[(1 - y) * 2 + c].astype(F32) + cbuf[0].astype(F32)).astype(BF)
    across = remote(mixed, ybuf, send_sem.at[2], recv_sem.at[2], y_peer)
    across.start()
    copies[1].wait_recv()
    out_ref[...] = parts_ref[y * 2 + c].astype(F32) + cbuf[1].astype(F32)
    across.wait_recv()
    out_ref[...] += ybuf[...].astype(F32)
    for copy in copies:
        copy.wait_send()
    across.wait_send()


def group_sum(parts, number):
    rows, width = parts.shape[0] // 4, parts.shape[1]
    return pl.pallas_call(
        group_sum_kernel,
        out_shape=jax.ShapeDtypeStruct((rows, width), F32),
        in_specs=[vspec()],
        out_specs=vspec(),
        scratch_shapes=[
            VMEM((2, rows, width), BF),
            VMEM((rows, width), BF),
            VMEM((rows, width), BF),
            pltpu.SemaphoreType.DMA((3,)),
            pltpu.SemaphoreType.DMA((3,)),
        ],
        compiler_params=comm_params(number),
        name="group_sum",
    )(parts.astype(BF).reshape(4, rows, width))


def small_gather_kernel(depth, ints_ref, norms_ref, ints_out, norms_out, ss, rs, ns, nr):
    z, x, y, c = place()
    dp = lax.axis_index("dp")
    mp = lax.axis_index("mp")
    count = 2 * depth
    peers = [((dp + k) % count, mp) for k in range(1, count)]
    greet(peers)
    ints_out[dp] = ints_ref[...]
    norms_out[dp] = norms_ref[...]
    copies = []
    for k, peer in enumerate(peers):
        copies.append(remote(ints_ref, ints_out.at[dp], ss.at[k], rs.at[k], peer))
        copies.append(remote(norms_ref, norms_out.at[dp], ns.at[k], nr.at[k], peer))
    for copy in copies:
        copy.start()
    for copy in copies:
        copy.wait()


def small_gather(depth, ints, norms):
    count = 2 * depth
    return pl.pallas_call(
        functools.partial(small_gather_kernel, depth),
        out_shape=(
            jax.ShapeDtypeStruct((count, *ints.shape), ints.dtype),
            jax.ShapeDtypeStruct((count, *norms.shape), norms.dtype),
        ),
        in_specs=[vspec(), vspec()],
        out_specs=(vspec(), vspec()),
        scratch_shapes=[pltpu.SemaphoreType.DMA((count - 1,))] * 4,
        compiler_params=comm_params(5, 8),
        name="small_gather",
    )(ints, norms)


def scalar_sum_kernel(depth, own_ref, out_ref, snap, got, ss, rs):
    z, x, y, c = place()
    peers = [device(z, x, y, 1 - c), device(z, x, 1 - y, c), device(z, 1 - x, y, c)]
    z_peers = [device((z + k) % depth, x, y, c) for k in range(1, depth)]
    greet(peers + z_peers)
    snap[0] = own_ref[...]
    for number, peer in enumerate(peers):
        copy = remote(snap.at[number], got.at[depth + number], ss.at[number], rs.at[number], peer)
        copy.start()
        copy.wait()
        snap[number + 1] = snap[number] + got[depth + number]
    copies = [
        remote(snap.at[3], got.at[z], ss.at[2 + k], rs.at[2 + k], z_peers[k - 1])
        for k in range(1, depth)
    ]
    for copy in copies:
        copy.start()
    got[z] = snap[3]
    for copy in copies:
        copy.wait()
    total = got[0]
    for k in range(1, depth):
        total = total + got[k]
    out_ref[...] = total


def scalar_sum(depth, values):
    return pl.pallas_call(
        functools.partial(scalar_sum_kernel, depth),
        out_shape=jax.ShapeDtypeStruct(values.shape, F32),
        in_specs=[vspec()],
        out_specs=vspec(),
        scratch_shapes=[
            VMEM((4, *values.shape), F32),
            VMEM((depth + 3, *values.shape), F32),
            pltpu.SemaphoreType.DMA((depth + 2,)),
            pltpu.SemaphoreType.DMA((depth + 2,)),
        ],
        compiler_params=comm_params(6, 8),
        name="scalar_sum",
    )(values)


class KernelMoves:
    def __init__(self, depth):
        self.depth = depth
        self.number = 10

    def next(self):
        self.number += 1
        return self.number

    def small(self, token_ids, target_ids, mask, norms):
        packed = jnp.concatenate([v.reshape(-1, 128) for v in (token_ids, target_ids, mask)], axis=0)
        each = packed.shape[0] // 3
        low = jnp.pad(norms.astype(BF), ((0, 16 - norms.shape[0]), (0, 0)))
        ints, norms_all = small_gather(self.depth, packed, low)
        norms_all = jnp.transpose(norms_all, (1, 0, 2)).reshape(16, -1)[: norms.shape[0]]
        return [ints[:, i * each : (i + 1) * each].reshape(-1) for i in range(3)] + [norms_all]

    def embed(self, table_low, local_ids, rows):
        return embed_call(self.depth, table_low, local_ids.astype(F32).reshape(-1, 1, rows))

    def gather_group(self, own):
        return group_gather(own, self.next())

    def sum_group(self, parts):
        return group_sum(parts, self.next())

    def head(self, hidden, table_low, targets, weights, vocab_size):
        rows = hidden.shape[0]
        targets = targets.astype(F32).reshape(-1, 1, rows)
        weights = weights.reshape(-1, 1, rows)
        hidden_all, expo, top, total, picked = logits_call(self.depth, hidden, table_low, targets)
        grad_hidden, grads = grads_call(
            self.depth, vocab_size, table_low, targets, weights, top, total, expo
        )
        shard, width = table_low.shape
        hidden_all = hidden_all.reshape(-1, width)
        table_grad = contract_rows(grads.reshape(-1, shard), hidden_all)
        weights = weights.reshape(-1)
        counted = (weights > 0.0).astype(F32).astype(BF)
        hidden_sum = dot_nn(counted[None], hidden_all)[0] * jnp.max(weights)
        first = (lax.axis_index("dp") * lax.axis_size("mp") + lax.axis_index("mp")) * rows
        own_logs = lax.dynamic_slice(total.reshape(-1), (first,), (rows,))
        log_sum = jnp.sum(own_logs * lax.dynamic_slice(weights, (first,), (rows,)))
        picked_sum = jnp.sum(picked.reshape(-1) * weights)
        return grad_hidden, table_grad, log_sum, picked_sum, hidden_sum

    def scatter(self, grad_start, norms_grad, local_ids, table_grad, span):
        rows = grad_start.shape[0]
        count = norms_grad.shape[0]
        rest = jnp.pad(norms_grad, ((0, 16 - count), (0, 0)))
        sent = jnp.concatenate([grad_start, rest], axis=0).astype(BF)
        ids = local_ids.astype(F32).reshape(-1, 1, rows)
        table_grad, positions_grad, rest = scatter_call(self.depth, sent, ids, table_grad, span)
        dp = lax.axis_index("dp")
        part = rest.shape[1] // lax.axis_size("dp")
        norms_part = lax.dynamic_slice(rest, (0, dp * part), (16, part))[:count]
        return table_grad, positions_grad, norms_part

    def total(self, scalars):
        row = jnp.concatenate([jnp.full((1, 128), value, F32) for value in scalars], axis=0)
        row = jnp.pad(row, ((0, 8 - len(scalars)), (0, 0)))
        summed = scalar_sum(self.depth, row)
        return [summed[i, 0] for i in range(len(scalars))]


class PlainMoves:
    parts = 4

    def split(self, values, rows):
        piece = rows // self.parts
        return jnp.swapaxes(values.reshape(-1, self.parts, piece), 0, 1).reshape(self.parts, -1)

    def small(self, token_ids, target_ids, mask, norms):
        found = [lax.all_gather(v.reshape(-1), "dp", tiled=True) for v in (token_ids, target_ids, mask)]
        return found + [lax.all_gather(norms.astype(BF), "dp", axis=1, tiled=True)]

    def embed(self, table_low, local_ids, rows):
        def one(ids):
            looked = jnp.take(table_low, jnp.maximum(ids, 0), axis=0)
            looked = jnp.where(ids[:, None] >= 0, looked, jnp.zeros((), BF))
            return lax.psum_scatter(looked, ("dp", "mp"), tiled=True)

        return lax.map(one, self.split(local_ids, rows)).reshape(rows, -1)

    def gather_group(self, own):
        return lax.all_gather(own, "mp", tiled=True)

    def sum_group(self, parts):
        return lax.psum_scatter(parts, "mp", tiled=True)

    def head(self, hidden, table_low, targets, weights, vocab_size):
        rows, width = hidden.shape
        shard = table_low.shape[0]

        def one(carried, packed):
            own, ids, weight = packed
            table_grad, log_sum, picked_sum, hidden_sum = carried
            hidden_all = lax.all_gather(own, ("dp", "mp"), tiled=True)
            logits = contract_cols(hidden_all, table_low)
            top = lax.pmax(jnp.max(logits, axis=1), ("dp", "mp"))
            onehot = jnp.arange(shard)[None, :] == ids[:, None]
            picked = jnp.sum(jnp.where(onehot, logits, 0.0), axis=1)
            total = lax.psum(jnp.sum(jnp.exp(logits - top[:, None]), axis=1), ("dp", "mp"))
            total = top + jnp.log(total)
            grads = jnp.exp(logits - total[:, None]) - jnp.where(onehot, 1.0 - smoothing, 0.0)
            grads = ((grads - smoothing / vocab_size) * weight[:, None]).astype(BF)
            partial = dot_nn(grads, table_low).astype(BF)
            grad_hidden = lax.psum_scatter(partial, ("dp", "mp"), tiled=True).astype(F32)
            hidden_sum = hidden_sum + jnp.sum(weight[:, None] * hidden_all.astype(F32), axis=0)
            carried = (
                table_grad + contract_rows(grads, hidden_all),
                log_sum + jnp.sum(total * weight),
                picked_sum + jnp.sum(picked * weight),
                hidden_sum,
            )
            return carried, grad_hidden

        zero = jnp.zeros((), F32)
        first = (jnp.zeros((shard, width), F32), zero, zero, jnp.zeros((width,), F32))
        own = hidden.reshape(self.parts, rows // self.parts, width)
        carried, grad_hidden = lax.scan(
            one, first, (own, self.split(targets, rows), self.split(weights, rows))
        )
        table_grad, log_sum, picked_sum, hidden_sum = carried
        devices = lax.axis_size("dp") * lax.axis_size("mp")
        return grad_hidden.reshape(rows, width), table_grad, log_sum / devices, picked_sum, hidden_sum

    def scatter(self, grad_start, norms_grad, local_ids, table_grad, span):
        shard = table_grad.shape[0]
        rows, width = grad_start.shape

        def one(carried, packed):
            own, ids = packed
            everything = lax.all_gather(own, ("dp", "mp"), tiled=True).astype(F32)
            safe = jnp.where(ids >= 0, ids, shard)
            return carried + jax.ops.segment_sum(everything, safe, num_segments=shard), None

        own = grad_start.astype(BF).reshape(self.parts, rows // self.parts, width)
        table_grad, unused = lax.scan(one, table_grad, (own, self.split(local_ids, rows)))
        spread = jnp.zeros((lax.axis_size("mp") * rows, width), F32)
        spread = lax.dynamic_update_slice(spread, grad_start, (lax.axis_index("mp") * rows, 0))
        positions_grad = lax.psum(lax.psum_scatter(spread, "dp", tiled=True), "mp")
        norms_part = lax.psum(
            lax.psum_scatter(norms_grad, "dp", scatter_dimension=1, tiled=True), "mp"
        )
        return table_grad, positions_grad, norms_part

    def total(self, scalars):
        return list(lax.psum(tuple(scalars), ("dp", "mp")))


def attend_scores(queries, keys, length):
    scores = jnp.einsum("qhe,khe->hqk", queries, keys, preferred_element_type=F32) * HD ** (-0.5)
    place_at = jnp.arange(queries.shape[0])
    allowed = (place_at[None, :] <= place_at[:, None]) & (place_at[None, :] < length)
    return jnp.where(allowed[None], scores, -1e30)


def attend_forward(queries, keys, values, length):
    scores = attend_scores(queries, keys, length)
    top = jnp.max(scores, axis=-1, keepdims=True)
    log_total = jnp.log(jnp.sum(jnp.exp(scores - top), axis=-1, keepdims=True)) + top
    probs = jnp.exp(scores - log_total).astype(BF)
    attended = jnp.einsum("hqk,khe->qhe", probs, values, preferred_element_type=F32)
    return attended.astype(BF), log_total


def attend_backward(queries, keys, values, length, log_total, grad):
    probs = jnp.exp(attend_scores(queries, keys, length) - log_total)
    grad_values = jnp.einsum("hqk,qhe->khe", probs.astype(BF), grad, preferred_element_type=F32)
    grad_probs = jnp.einsum("qhe,khe->hqk", grad, values, preferred_element_type=F32)
    inner = jnp.sum(grad_probs * probs, axis=-1, keepdims=True)
    grad_scores = (probs * (grad_probs - inner)).astype(BF)
    scale = HD ** (-0.5)
    grad_queries = jnp.einsum("hqk,khe->qhe", grad_scores, keys, preferred_element_type=F32) * scale
    grad_keys = jnp.einsum("hqk,qhe->khe", grad_scores, queries, preferred_element_type=F32) * scale
    return grad_queries.astype(BF), grad_keys.astype(BF), grad_values.astype(BF)


def local(
    moves,
    token_ids,
    target_ids,
    loss_mask,
    lengths,
    step_count,
    *weights,
):
    masters, firsts, seconds = weights[:7], weights[7:14], weights[14:]
    table, positions, attn_in, attn_out, mlp_in, mlp_out, norms = masters
    shard = table.shape[0]
    width = table.shape[1]
    dp, mp = lax.axis_index("dp"), lax.axis_index("mp")
    dp_count, mp_count = lax.axis_size("dp"), lax.axis_size("mp")
    vocab_size = shard * dp_count * mp_count
    seq_len = token_ids.shape[1]
    rows = token_ids.size // mp_count
    table_low = table.astype(BF)
    ids_all, targets_all, mask_all, norms_all = moves.small(token_ids, target_ids, loss_mask, norms)
    gains = norms_all.astype(F32)
    mask_all = mask_all.astype(F32)
    token_total = jnp.sum(mask_all)
    row_weights = mask_all / token_total
    base = (dp * mp_count + mp) * shard

    def local_of(ids):
        inside = (ids >= base) & (ids < base + shard)
        return jnp.where(inside, ids - base, -1)

    local_ids, local_targets = local_of(ids_all), local_of(targets_all)
    attn_pack = jnp.concatenate([attn_in, attn_out[None]], axis=0).astype(BF)
    mlp_pack = jnp.stack([mlp_in, mlp_out]).astype(BF)
    positions_all = lax.all_gather(positions.astype(BF), "dp", axis=0, tiled=True)
    attn_all = lax.all_gather(attn_pack, "dp", axis=1, tiled=True)
    mlp_all = lax.all_gather(mlp_pack, "dp", axis=1, tiled=True)

    embedded = moves.embed(table_low, local_ids, rows)
    first_row = (mp * rows) % seq_len
    own_positions = lax.dynamic_slice(positions_all, (first_row, 0), (rows, width))
    start_rows = embedded.astype(F32) + own_positions.astype(F32)
    normed_one = moves.gather_group(layer_norm(start_rows, gains[0], gains[1]).astype(BF))
    head_shape = (seq_len, attn_all.shape[2] // HD, HD)
    queries, keys, values = (dot_nn(normed_one, attn_all[i]).astype(BF) for i in range(3))
    heads = [v.reshape(head_shape) for v in (queries, keys, values)]
    attended, log_total = attend_forward(*heads, lengths[0])
    attended = attended.reshape(seq_len, -1)
    middle = start_rows + moves.sum_group(contract_cols(attended, attn_all[3]))
    normed_two = moves.gather_group(layer_norm(middle, gains[2], gains[3]).astype(BF))
    pre_gelu = dot_nn(normed_two, mlp_all[0])
    activated = gelu_tanh(pre_gelu).astype(BF)
    last_rows = middle + moves.sum_group(contract_cols(activated, mlp_all[1]))
    hidden = layer_norm(last_rows, gains[4], gains[5]).astype(BF)

    grad_hidden, table_grad, log_sum, picked_sum, hidden_sum = moves.head(
        hidden, table_low, local_targets, row_weights, vocab_size
    )
    column_sum = jnp.sum(table_low.astype(F32), axis=0)
    loss_part = (
        log_sum
        - (1.0 - smoothing) * picked_sum
        - smoothing / vocab_size * jnp.sum(hidden_sum * column_sum)
    )

    unused, norm_three_back = jax.vjp(layer_norm, last_rows, gains[4], gains[5])
    grad_last, gain_three, shift_three = norm_three_back(grad_hidden)
    grad_last_low = moves.gather_group(grad_last.astype(BF))
    mlp_out_grad = contract_rows(grad_last_low, activated)
    grad_activated = dot_nn(grad_last_low, mlp_all[1])
    unused, gelu_back = jax.vjp(gelu_tanh, pre_gelu)
    grad_pre = gelu_back(grad_activated)[0].astype(BF)
    mlp_in_grad = contract_rows(normed_two, grad_pre)
    grad_normed_two = moves.sum_group(contract_cols(grad_pre, mlp_all[0]))
    mlp_share = lax.psum_scatter(
        jnp.stack([mlp_in_grad, mlp_out_grad]).astype(BF), "dp", scatter_dimension=1, tiled=True
    ).astype(F32)
    unused, norm_two_back = jax.vjp(layer_norm, middle, gains[2], gains[3])
    grad_from_two, gain_two, shift_two = norm_two_back(grad_normed_two)
    grad_middle = grad_last + grad_from_two
    grad_middle_low = moves.gather_group(grad_middle.astype(BF))
    attn_out_grad = contract_rows(grad_middle_low, attended)
    grad_attended = dot_nn(grad_middle_low, attn_all[3]).astype(BF).reshape(head_shape)
    members = [
        v.reshape(seq_len, -1)
        for v in attend_backward(*heads, lengths[0], log_total, grad_attended)
    ]
    attn_grads = [contract_rows(normed_one, v) for v in members] + [attn_out_grad]
    grad_normed_one = moves.sum_group(
        sum(contract_cols(members[i], attn_all[i]) for i in range(3))
    )
    attn_share = lax.psum_scatter(
        jnp.stack(attn_grads).astype(BF), "dp", scatter_dimension=1, tiled=True
    ).astype(F32)
    unused, norm_one_back = jax.vjp(layer_norm, start_rows, gains[0], gains[1])
    grad_from_one, gain_one, shift_one = norm_one_back(grad_normed_one)
    grad_start = grad_middle + grad_from_one
    norms_grad = jnp.stack([gain_one, shift_one, gain_two, shift_two, gain_three, shift_three])
    table_grad, positions_grad, norms_part = moves.scatter(
        grad_start, norms_grad, local_ids, table_grad, positions.shape[0]
    )
    shares = (
        table_grad,
        positions_grad,
        attn_share[:3],
        attn_share[3],
        mlp_share[0],
        mlp_share[1],
        norms_part,
    )
    copies = (1.0, mp_count, 1.0, 1.0, 1.0, 1.0, mp_count)
    squares = sum(jnp.sum(v * v) / n for v, n in zip(shares, copies))
    total_square, loss = moves.total([squares, loss_part])
    grad_norm = jnp.sqrt(total_square)
    factor = jnp.minimum(1.0, clip_norm / (grad_norm + 1e-06))
    step_float = step_count[0].astype(F32)
    updated = [
        adam_update(
            masters[i],
            firsts[i],
            seconds[i],
            factor * shares[i],
            learn_rates[i],
            decay_rates[i],
            step_float,
        )
        for i in range(7)
    ]
    return (loss, grad_norm) + tuple(updated[i][part] for part in range(3) for i in range(7))


def fits_kernels(mesh):
    if mesh.shape["mp"] != 4 or mesh.shape["dp"] != 8:
        return False
    for (dp, mp), item in zip(
        ((i, j) for i in range(8) for j in range(4)), mesh.devices.reshape(-1)
    ):
        coords = getattr(item, "coords", None)
        if coords is not None and (tuple(coords), item.core_on_chip) != (
            (dp % 2, mp // 2, dp // 2),
            mp % 2,
        ):
            return False
    return True


def solution(mesh):
    table, rows, heads, grid, norms = (
        P(("dp", "mp"), None),
        P("dp", None),
        P(None, "dp", "mp"),
        P("dp", "mp"),
        P(None, "dp"),
    )
    each = (table, rows, heads, grid, grid, grid, norms)
    in_specs = (rows, rows, rows, P("dp"), P()) + each * 3
    out_specs = (P(), P()) + each * 3
    moves = KernelMoves(mesh.shape["dp"] // 2) if fits_kernels(mesh) else PlainMoves()
    return jax.shard_map(
        functools.partial(local, moves),
        mesh=mesh,
        in_specs=in_specs,
        out_specs=out_specs,
        check_vma=False,
    )
```

```python
import functools

import jax
import jax.numpy as jnp
from jax import lax
from jax.experimental import pallas as pl
from jax.experimental.pallas import tpu as pltpu
from jax.sharding import PartitionSpec as P

HD = 64
VOCAB = 50688
MESH = pl.DeviceIdType.MESH
ANY = pl.ANY
VMEM = pltpu.VMEM
BF = jnp.bfloat16
F32 = jnp.float32

smoothing = 0.1
clip_norm = 0.01
beta_one = 0.9
beta_two = 0.999
adam_eps = 1e-08
learn_rates = (0.06, 0.06, 0.03, 0.03, 0.03, 0.004, 0.3)
decay_rates = (0.1, 0.0, 0.1, 0.1, 0.1, 0.1, 0.0)


def layer_norm(values, gain_row, shift_row):
    centered = values - jnp.mean(values, axis=-1, keepdims=True)
    spread = jnp.mean(centered * centered, axis=-1, keepdims=True)
    return centered * lax.rsqrt(spread + 1e-05) * gain_row + shift_row


def gelu_tanh(values):
    return jax.nn.gelu(values, approximate=True)


def adam_update(weight, first_moment, second, grad_item, rate, decay, step_float):
    first_new = beta_one * first_moment + (1.0 - beta_one) * grad_item
    second_new = beta_two * second + (1.0 - beta_two) * grad_item * grad_item
    first_hat = first_new / (1.0 - beta_one**step_float)
    second_hat = second_new / (1.0 - beta_two**step_float)
    weight_new = weight - rate * (first_hat / (jnp.sqrt(second_hat) + adam_eps) + decay * weight)
    return (weight_new, first_new, second_new)


def contract_rows(left, right):
    return lax.dot_general(
        left, right, (((0,), (0,)), ((), ())), preferred_element_type=F32
    )


def contract_cols(left, right):
    return lax.dot_general(
        left, right, (((1,), (1,)), ((), ())), preferred_element_type=F32
    )


def dot_nn(left, right):
    return lax.dot_general(
        left, right, (((1,), (0,)), ((), ())), preferred_element_type=F32
    )


def place():
    dp = lax.axis_index("dp")
    mp = lax.axis_index("mp")
    return dp // 2, dp % 2, mp // 2, mp % 2


def device(z, x, y, c):
    return (z * 2 + x, y * 2 + c)


def flip(bit, by):
    return bit + by - 2 * bit * by


def greet(peers):
    barrier = pltpu.get_barrier_semaphore()
    for peer in peers:
        pl.semaphore_signal(barrier, inc=1, device_id=peer, device_id_type=MESH)
    pl.semaphore_wait(barrier, len(peers))


def remote(src, dst, send_sem, recv_sem, peer):
    return pltpu.make_async_remote_copy(
        src_ref=src,
        dst_ref=dst,
        send_sem=send_sem,
        recv_sem=recv_sem,
        device_id=peer,
        device_id_type=MESH,
    )


def to_column(row):
    wide = jnp.broadcast_to(row, (128, row.shape[1]))
    return jnp.transpose(wide)[:, :1]


def to_row(column):
    wide = jnp.broadcast_to(column, (column.shape[0], 128))
    return jnp.transpose(wide)[:1, :]


ARRIVALS = (
    "000o 010p 100d 001q 200d 110p 011q 101q 201q 300d 210p 111q 310d 301q 211q 311q",
    "100o 000u 200d 010u 300d 110p 201q 310d 001q 301q 210p 111q 011q 101q 211q 311q",
)
DEPTH = 4
EVENTS = 16


def sent_on(z, source, kind):
    up = ["u"] if z < DEPTH - 1 else []
    down = ["d"] if z > 0 else []
    if source in (1, 2):
        return {"o": up + down + ["p", "q"], "u": up + ["p", "q"], "d": down + ["p", "q"]}.get(
            kind, ["q"] if kind == "p" else []
        )
    return {
        "o": ["p"] + up + down + ["q"],
        "p": up + down + ["q"],
        "u": up + ["q"],
        "d": down + ["q"],
    }.get(kind, [])


@functools.lru_cache
def route_tables():
    mirror = {"u": "d", "d": "u"}
    events = {}
    for z in range(DEPTH):
        rows = []
        for item in ARRIVALS[min(z, DEPTH - 1 - z)].split():
            source, first, second, kind = int(item[0]), int(item[1]), int(item[2]), item[3]
            if z >= 2:
                source, kind = DEPTH - 1 - source, mirror.get(kind, kind)
            rows.append((source, first, second, kind))
        events[z] = rows
    order = ("p", "q", "u", "d")
    slots, firsts, flags = {}, {}, {}
    for z in range(DEPTH):
        count = 0
        turned = ("p", "q", "u", "d") if z < 2 else ("p", "q", "d", "u")
        for n, (source, first, second, kind) in enumerate(events[z]):
            sends = sent_on(z, source, kind)
            firsts[z, n] = count
            flags[z, n] = sum(1 << i for i, k in enumerate(turned) if k in sends)
            for k in turned:
                if k in sends:
                    slots[z, source, first, second, k] = count
                    count += 1
    tables = []
    most = 1 + max(slots.values())
    for z in range(2):
        rows = []
        for n, (source, first, second, kind) in enumerate(events[z]):
            if kind == "o":
                slot, origin = 0, 0
            else:
                at = z - 1 if kind == "u" else z + 1 if kind == "d" else z
                up_first = 1 - first if kind == "p" else first
                up_second = 1 - second if kind == "q" else second
                slot = slots[at, source, up_first, up_second, kind]
                origin = order.index(kind)
            rows.append((source, 2 * first + second, flags[z, n], slot, firsts[z, n], origin))
        tables.append(rows)
    return tables, most


RADIX = 1024


class Route:
    def __init__(self):
        self.z, self.x, self.y, self.c = place()
        tables, self.slots = route_tables()
        kind = flip(self.z % 2, self.z // 2)
        self.mirrored = self.z // 2
        self.packed = []
        for digits in (
            lambda row: row[0] + 4 * row[1] + 16 * row[2] + 256 * row[5],
            lambda row: row[3] + 32 * row[4],
        ):
            low, high = (
                [digits(rows[n]) + RADIX * digits(rows[n + 1]) for n in range(0, EVENTS, 2)]
                for rows in tables
            )
            self.packed.append([a + kind * (b - a) for a, b in zip(low, high)])
        sign = 1 - 2 * self.mirrored
        z, x, y, c = self.z, self.x, self.y, self.c
        self.c_peer = device(z, x, y, 1 - c)
        self.peers = (
            device(z, flip(x, 1 - c), flip(y, c), c),
            device(z, flip(x, c), flip(y, 1 - c), c),
            device(z + sign, x, y, c),
            device(z - sign * kind, x, y, c),
        )

    def greet(self):
        z, x, y, c = self.z, self.x, self.y, self.c
        along = [device((z + k) % DEPTH, x, y, c) for k in range(1, DEPTH)]
        greet(along + [self.peers[0], self.peers[1], self.c_peer])

    def digits(self, which, n):
        pair = n // 2
        bits = (pair % 2, pair // 2 % 2, pair // 4)
        total = 0
        for number, value in enumerate(self.packed[which]):
            chosen = value
            for i, bit in enumerate(bits):
                chosen = chosen * (bit if number >> i & 1 else 1 - bit)
            total = total + chosen
        return total // (1 + (RADIX - 1) * (n % 2)) % RADIX

    def flags(self, n):
        return self.digits(0, n) // 16 % 16

    def origin(self, n):
        return self.digits(0, n) // 256

    def parent_slot(self, n):
        return self.digits(1, n) % 32

    def first_slot(self, n):
        return self.digits(1, n) // 32

    def family(self, n, core):
        digits = self.digits(0, n)
        source = digits % 4
        source = source + self.mirrored * (DEPTH - 1 - 2 * source)
        first, second = digits // 8 % 2, digits // 4 % 2
        by_x = first * (1 - core) + second * core
        by_y = second * (1 - core) + first * core
        return (source * 2 + flip(self.x, by_x)) * 2 + flip(self.y, by_y)

    def sends(self, n, act):
        flags = self.flags(n)
        for i in range(4):

            @pl.when((flags // (1 << i)) % 2 == 1)
            def _():
                act(i)


def gather_scratch():
    return [
        pltpu.SemaphoreType.DMA((1,)),
        pltpu.SemaphoreType.DMA((4 * EVENTS,)),
        pltpu.SemaphoreType.DMA((EVENTS,)),
        pltpu.SemaphoreType.DMA((EVENTS,)),
        pltpu.SemaphoreType.DMA((EVENTS,)),
    ]


def gather_blocks(own_ref, land, scratch, consume):
    lsem, ss, rs, cs, cr = scratch
    route = Route()
    c = route.c
    route.greet()
    own = route.family(0, c) * 2 + c
    local = pltpu.make_async_copy(own_ref, land.at[own], lsem.at[0])
    local.start()
    local.wait()

    def copy(family, i):
        block = land.at[family * 2 + c]
        return remote(block, block, ss.at[i * EVENTS + family], rs.at[family], route.peers[i])

    def c_copy(family, core):
        block = land.at[family * 2 + core]
        return remote(block, block, cs.at[family], cr.at[family], route.c_peer)

    def event(n, carry):
        @pl.when(n < EVENTS)
        def _():
            family = route.family(n, c)

            @pl.when(n >= 1)
            def _():
                copy(family, 0).wait_recv()

            route.sends(n, lambda i: copy(family, i).start())
            c_copy(family, c).start()

        def one(i, inner):
            at = n - i

            @pl.when((at >= 0) & (at < EVENTS))
            def _():
                core = flip(c, i)
                family = route.family(at, core)

                @pl.when(i == 1)
                def _():
                    c_copy(family, core).wait_recv()

                consume(family * 2 + core, 2 * n - i)

            return inner

        lax.fori_loop(0, 2, one, 0)
        return carry

    lax.fori_loop(0, EVENTS + 1, event, 0)

    def drain(n, carry):
        family = route.family(n, c)
        route.sends(n, lambda i: copy(family, i).wait_send())
        c_copy(family, c).wait_send()
        return carry

    lax.fori_loop(0, EVENTS, drain, 0)


def reduce_scratch(rows, width):
    slots = route_tables()[1]
    return [
        VMEM((2, rows, width), F32),
        VMEM((EVENTS, rows, width), BF),
        VMEM((EVENTS, rows, width), BF),
        VMEM((EVENTS, rows, width), BF),
        VMEM((slots, rows, width), BF),
        pltpu.SemaphoreType.DMA((EVENTS,)),
        pltpu.SemaphoreType.DMA((slots,)),
        pltpu.SemaphoreType.DMA((EVENTS,)),
        pltpu.SemaphoreType.DMA((EVENTS,)),
    ]


def reduce_blocks(out_ref, scratch, produce, start=None):
    own, oth, cbuf, sbuf, rbuf, ss, rs, cs, cr = scratch
    route = Route()
    c = route.c

    def target(k):
        core = flip(c, 1 - k % 2)
        return route.family(EVENTS - 1 - k // 2, core) * 2 + core

    route.greet()
    if start is not None:
        start(target)

    def c_copy(n):
        return remote(oth.at[n], cbuf.at[n], cs.at[n], cr.at[n], route.c_peer)

    def copy(n, slot, i):
        return remote(sbuf.at[n], rbuf.at[slot], ss.at[n], rs.at[slot], route.peers[i])

    def finish(n):
        half = n % 2
        c_copy(n).wait_recv()
        own[half] += cbuf[n].astype(F32)
        flags, base = route.flags(n), route.first_slot(n)

        def arrived(i):
            slot = base
            for lower in range(i):
                slot = slot + (flags // (1 << lower)) % 2
            copy(n, slot, 0).wait_recv()
            own[half] += rbuf[slot].astype(F32)

        route.sends(n, arrived)

        @pl.when(n > 0)
        def _():
            sbuf[n] = own[half].astype(BF)
            for i, back in enumerate((0, 1, 3, 2)):

                @pl.when(route.origin(n) == i)
                def _():
                    copy(n, route.parent_slot(n), back).start()

    def step(m, carry):
        n = EVENTS - 1 - m

        def one(i, inner):
            @pl.when(m < EVENTS)
            def _():
                value = produce(2 * m + i, target(2 * m + i))

                @pl.when(i == 0)
                def _():
                    oth[n] = value.astype(BF)
                    c_copy(n).start()

                @pl.when(i == 1)
                def _():
                    own[n % 2] = value

            @pl.when((i == 0) & (m >= 1))
            def _():
                finish(n + 1)

            return inner

        lax.fori_loop(0, 2, one, 0)
        return carry

    lax.fori_loop(0, EVENTS + 1, step, 0)
    out_ref[...] = own[0].astype(out_ref.dtype)

    def drain(n, carry):
        c_copy(n).wait_send()

        @pl.when(n > 0)
        def _():
            copy(n, 0, 0).wait_send()

        return carry

    lax.fori_loop(0, EVENTS, drain, 0)


def comm_params(number, limit_mib=60):
    return pltpu.CompilerParams(
        collective_id=number, has_side_effects=True, vmem_limit_bytes=limit_mib << 20
    )


def vspec():
    return pl.BlockSpec(memory_space=VMEM)


def aspec():
    return pl.BlockSpec(memory_space=ANY)


def embed_kernel(depth, table_ref, ids_ref, out_ref, *scratch):
    def produce(n, block):
        wanted = to_column(ids_ref[block])
        rows = wanted.shape[0]
        vocab = lax.broadcasted_iota(jnp.int32, (rows, table_ref.shape[0]), 1).astype(F32)
        onehot = (vocab == wanted).astype(F32).astype(BF)
        return dot_nn(onehot, table_ref[...])

    reduce_blocks(out_ref, scratch, produce)


def embed_call(depth, table_low, local_ids):
    blocks, unused, rows = local_ids.shape
    width = table_low.shape[1]
    return pl.pallas_call(
        functools.partial(embed_kernel, depth),
        out_shape=jax.ShapeDtypeStruct((rows, width), BF),
        in_specs=[vspec(), vspec()],
        out_specs=vspec(),
        scratch_shapes=reduce_scratch(rows, width),
        compiler_params=comm_params(1),
        name="embed_exchange",
    )(table_low, local_ids)


def combine_logs(first, second):
    top = jnp.maximum(first, second)
    return top + jnp.log(jnp.exp(first - top) + jnp.exp(second - top))


def logits_kernel(
    depth, hidden_ref, table_ref, targets_ref, all_ref, expo_ref, top_ref, total_ref, picked_ref,
    land, stage, snap, got, out_sem, all_sem, xs, xr, *sems
):
    z, x, y, c = place()
    blocks = land.shape[0]

    def out_copy(slot, block):
        return pltpu.make_async_copy(stage.at[slot], expo_ref.at[block], out_sem.at[slot])

    def keep(block):
        return pltpu.make_async_copy(land.at[block], all_ref.at[block], all_sem.at[block])

    def consume(block, number):
        slot = number % 2
        keep(block).start()
        logits = contract_cols(land[block], table_ref[...])
        top = jnp.max(logits, axis=1, keepdims=True)
        expo = jnp.exp(logits - top)
        total = jnp.sum(expo, axis=1, keepdims=True)
        wanted = to_column(targets_ref[block])
        vocab = lax.broadcasted_iota(jnp.int32, logits.shape, 1).astype(F32)
        picked = jnp.sum(jnp.where(vocab == wanted, logits, 0.0), axis=1, keepdims=True)
        top_row = to_row(top)
        top_ref[block] = top_row
        picked_ref[block] = to_row(picked)
        total_ref[block] = top_row + jnp.log(to_row(total))

        @pl.when(number >= 2)
        def _():
            out_copy(slot, block).wait()

        stage[slot] = expo.astype(BF)
        out_copy(slot, block).start()

    gather_blocks(hidden_ref, land, sems, consume)
    peers = [device(z, x, y, 1 - c), device(z, x, 1 - y, c), device(z, 1 - x, y, c)]
    for number, peer in enumerate(peers):
        snap[number] = total_ref[...]
        copy = remote(snap.at[number], got.at[number], xs.at[number], xr.at[number], peer)
        copy.start()
        copy.wait()
        total_ref[...] = combine_logs(snap[number], got[number])
    snap[3] = total_ref[...]
    copies = [
        remote(
            snap.at[3], got.at[2 + k], xs.at[2 + k], xr.at[2 + k], device((z + k) % depth, x, y, c)
        )
        for k in range(1, depth)
    ]
    for copy in copies:
        copy.start()
    for k, copy in enumerate(copies):
        copy.wait()
        total_ref[...] = combine_logs(total_ref[...], got[3 + k])
    for slot in range(2):
        out_copy(slot, 0).wait()

    def kept(block, carry):
        keep(block).wait()
        return carry

    lax.fori_loop(0, blocks, kept, 0)


def logits_call(depth, hidden, table_low, targets):
    blocks, unused, rows = targets.shape
    shard, width = table_low.shape
    row_shape = jax.ShapeDtypeStruct((blocks, 1, rows), F32)
    return pl.pallas_call(
        functools.partial(logits_kernel, depth),
        out_shape=(
            jax.ShapeDtypeStruct((blocks, rows, width), BF),
            jax.ShapeDtypeStruct((blocks, rows, shard), BF),
            row_shape,
            row_shape,
            row_shape,
        ),
        in_specs=[vspec(), vspec(), vspec()],
        out_specs=(aspec(), aspec(), vspec(), vspec(), vspec()),
        scratch_shapes=[
            VMEM((blocks, rows, width), BF),
            VMEM((2, rows, shard), BF),
            VMEM((4, blocks, 1, rows), F32),
            VMEM((2 + depth, blocks, 1, rows), F32),
            pltpu.SemaphoreType.DMA((2,)),
            pltpu.SemaphoreType.DMA((blocks,)),
            pltpu.SemaphoreType.DMA((2 + depth,)),
            pltpu.SemaphoreType.DMA((2 + depth,)),
        ]
        + gather_scratch(),
        compiler_params=comm_params(2),
        name="logits_exchange",
    )(hidden, table_low, targets)


def grads_kernel(
    depth, vocab_size, table_ref, targets_ref, weights_ref, top_ref, total_ref, expo_ref, out_ref, grad_ref,
    inbox, outbox, in_sem, out_sem, *scratch
):
    steps = 2 * EVENTS

    def fetch(slot, block):
        return pltpu.make_async_copy(expo_ref.at[block], inbox.at[slot], in_sem.at[slot])

    def store(slot, block):
        return pltpu.make_async_copy(outbox.at[slot], grad_ref.at[block], out_sem.at[slot])

    targets = []

    def start(target):
        targets.append(target)
        fetch(0, target(0)).start()

    def produce(n, block):
        slot = n % 2
        fetch(slot, block).wait()

        @pl.when(n + 1 < steps)
        def _():
            fetch(1 - slot, targets[0](n + 1)).start()

        weight = weights_ref[block]
        scale = to_column(jnp.exp(top_ref[block] - total_ref[block]) * weight)
        wanted = to_column(targets_ref[block])
        weight = to_column(weight)
        vocab = lax.broadcasted_iota(jnp.int32, inbox.shape[1:], 1).astype(F32)
        low = -(smoothing / vocab_size) * weight
        hit = low - (1.0 - smoothing) * weight
        grad = inbox[slot].astype(F32) * scale + jnp.where(vocab == wanted, hit, low)
        grad = grad.astype(BF)

        @pl.when(n >= 2)
        def _():
            store(slot, block).wait()

        outbox[slot] = grad
        store(slot, block).start()
        return dot_nn(grad, table_ref[...])

    reduce_blocks(out_ref, scratch, produce, start)
    for slot in range(2):
        store(slot, 0).wait()


def grads_call(depth, vocab_size, table_low, targets, weights, top, total, expo):
    blocks, rows, shard = expo.shape
    width = table_low.shape[1]
    return pl.pallas_call(
        functools.partial(grads_kernel, depth, vocab_size),
        out_shape=(
            jax.ShapeDtypeStruct((rows, width), F32),
            jax.ShapeDtypeStruct((blocks, rows, shard), BF),
        ),
        in_specs=[vspec(), vspec(), vspec(), vspec(), vspec(), aspec()],
        out_specs=(vspec(), aspec()),
        scratch_shapes=[
            VMEM((2, rows, shard), BF),
            VMEM((2, rows, shard), BF),
            pltpu.SemaphoreType.DMA((2,)),
            pltpu.SemaphoreType.DMA((2,)),
        ]
        + reduce_scratch(rows, width),
        compiler_params=comm_params(3),
        name="grads_exchange",
    )(table_low, targets, weights, top, total, expo)


def scatter_kernel(depth, rows, sent_ref, ids_ref, grad_ref, out_ref, pos_ref, rest_ref, land, *sems):
    out_ref[...] = grad_ref[...]
    shard = grad_ref.shape[0]

    def consume(block, number):
        vocab = lax.broadcasted_iota(jnp.int32, (shard, rows), 0).astype(F32)
        onehot = (vocab == ids_ref[block]).astype(F32).astype(BF)
        out_ref[...] += dot_nn(onehot, land[block, :rows, :])

    gather_blocks(sent_ref, land, sems, consume)
    dp = lax.axis_index("dp")
    slots = 2 * depth
    span = pos_ref.shape[0]
    per = rows // span
    total = jnp.zeros(pos_ref.shape, F32)
    rest = jnp.zeros(rest_ref.shape, F32)
    first = pl.multiple_of((dp % per) * span, span)
    for slot in range(slots):
        total = total + land[slot * 4 + dp // per, pl.ds(first, span), :].astype(F32)
    pos_ref[...] = total
    for block in range(land.shape[0]):
        rest = rest + land[block, rows:, :].astype(F32)
    rest_ref[...] = rest


def scatter_call(depth, sent, ids, table_grad, span):
    blocks, unused, rows = ids.shape
    extended, width = sent.shape
    return pl.pallas_call(
        functools.partial(scatter_kernel, depth, rows),
        out_shape=(
            jax.ShapeDtypeStruct(table_grad.shape, F32),
            jax.ShapeDtypeStruct((span, width), F32),
            jax.ShapeDtypeStruct((extended - rows, width), F32),
        ),
        in_specs=[vspec(), vspec(), vspec()],
        out_specs=(vspec(), vspec(), vspec()),
        scratch_shapes=[VMEM((blocks, extended, width), BF)] + gather_scratch(),
        compiler_params=comm_params(4),
        name="rows_exchange",
    )(sent, ids, table_grad)


def group_gather_kernel(own_ref, out_ref, local_sem, send_sem, recv_sem):
    z, x, y, c = place()
    y_peer, c_peer = device(z, x, 1 - y, c), device(z, x, y, 1 - c)
    greet([y_peer, c_peer])
    own, across = y * 2 + c, (1 - y) * 2 + c
    to_y = remote(own_ref, out_ref.at[own], send_sem.at[0], recv_sem.at[0], y_peer)
    to_c = remote(own_ref, out_ref.at[own], send_sem.at[1], recv_sem.at[1], c_peer)
    on = remote(out_ref.at[across], out_ref.at[across], send_sem.at[2], recv_sem.at[2], c_peer)
    to_y.start()
    to_c.start()
    local = pltpu.make_async_copy(own_ref, out_ref.at[own], local_sem.at[0])
    local.start()
    to_y.wait_recv()
    on.start()
    local.wait()
    to_c.wait_recv()
    on.wait_recv()
    to_y.wait_send()
    to_c.wait_send()
    on.wait_send()


def group_gather(own, number):
    rows, width = own.shape
    out = pl.pallas_call(
        group_gather_kernel,
        out_shape=jax.ShapeDtypeStruct((4, rows, width), own.dtype),
        in_specs=[vspec()],
        out_specs=aspec(),
        scratch_shapes=[
            pltpu.SemaphoreType.DMA((1,)),
            pltpu.SemaphoreType.DMA((3,)),
            pltpu.SemaphoreType.DMA((3,)),
        ],
        compiler_params=comm_params(number),
        name="group_gather",
    )(own)
    return out.reshape(4 * rows, width)


def group_sum_kernel(parts_ref, out_ref, cbuf, ybuf, mixed, send_sem, recv_sem):
    z, x, y, c = place()
    y_peer, c_peer = device(z, x, 1 - y, c), device(z, x, y, 1 - c)
    greet([y_peer, c_peer])
    copies = [
        remote(parts_ref.at[row * 2 + 1 - c], cbuf.at[i], send_sem.at[i], recv_sem.at[i], c_peer)
        for i, row in enumerate((1 - y, y))
    ]
    for copy in copies:
        copy.start()
    copies[0].wait_recv()
    mixed[...] = (parts_ref[(1 - y) * 2 + c].astype(F32) + cbuf[0].astype(F32)).astype(BF)
    across = remote(mixed, ybuf, send_sem.at[2], recv_sem.at[2], y_peer)
    across.start()
    copies[1].wait_recv()
    out_ref[...] = parts_ref[y * 2 + c].astype(F32) + cbuf[1].astype(F32)
    across.wait_recv()
    out_ref[...] += ybuf[...].astype(F32)
    for copy in copies:
        copy.wait_send()
    across.wait_send()


def group_sum(parts, number):
    rows, width = parts.shape[0] // 4, parts.shape[1]
    return pl.pallas_call(
        group_sum_kernel,
        out_shape=jax.ShapeDtypeStruct((rows, width), F32),
        in_specs=[vspec()],
        out_specs=vspec(),
        scratch_shapes=[
            VMEM((2, rows, width), BF),
            VMEM((rows, width), BF),
            VMEM((rows, width), BF),
            pltpu.SemaphoreType.DMA((3,)),
            pltpu.SemaphoreType.DMA((3,)),
        ],
        compiler_params=comm_params(number),
        name="group_sum",
    )(parts.astype(BF).reshape(4, rows, width))


def small_gather_kernel(depth, ints_ref, norms_ref, ints_out, norms_out, ss, rs, ns, nr):
    z, x, y, c = place()
    dp = lax.axis_index("dp")
    mp = lax.axis_index("mp")
    count = 2 * depth
    peers = [((dp + k) % count, mp) for k in range(1, count)]
    greet(peers)
    ints_out[dp] = ints_ref[...]
    norms_out[dp] = norms_ref[...]
    copies = []
    for k, peer in enumerate(peers):
        copies.append(remote(ints_ref, ints_out.at[dp], ss.at[k], rs.at[k], peer))
        copies.append(remote(norms_ref, norms_out.at[dp], ns.at[k], nr.at[k], peer))
    for copy in copies:
        copy.start()
    for copy in copies:
        copy.wait()


def small_gather(depth, ints, norms):
    count = 2 * depth
    return pl.pallas_call(
        functools.partial(small_gather_kernel, depth),
        out_shape=(
            jax.ShapeDtypeStruct((count, *ints.shape), ints.dtype),
            jax.ShapeDtypeStruct((count, *norms.shape), norms.dtype),
        ),
        in_specs=[vspec(), vspec()],
        out_specs=(vspec(), vspec()),
        scratch_shapes=[pltpu.SemaphoreType.DMA((count - 1,))] * 4,
        compiler_params=comm_params(5, 8),
        name="small_gather",
    )(ints, norms)


def scalar_sum_kernel(depth, own_ref, out_ref, snap, got, ss, rs):
    z, x, y, c = place()
    peers = [device(z, x, y, 1 - c), device(z, x, 1 - y, c), device(z, 1 - x, y, c)]
    z_peers = [device((z + k) % depth, x, y, c) for k in range(1, depth)]
    greet(peers + z_peers)
    snap[0] = own_ref[...]
    for number, peer in enumerate(peers):
        copy = remote(snap.at[number], got.at[depth + number], ss.at[number], rs.at[number], peer)
        copy.start()
        copy.wait()
        snap[number + 1] = snap[number] + got[depth + number]
    copies = [
        remote(snap.at[3], got.at[z], ss.at[2 + k], rs.at[2 + k], z_peers[k - 1])
        for k in range(1, depth)
    ]
    for copy in copies:
        copy.start()
    got[z] = snap[3]
    for copy in copies:
        copy.wait()
    total = got[0]
    for k in range(1, depth):
        total = total + got[k]
    out_ref[...] = total


def scalar_sum(depth, values):
    return pl.pallas_call(
        functools.partial(scalar_sum_kernel, depth),
        out_shape=jax.ShapeDtypeStruct(values.shape, F32),
        in_specs=[vspec()],
        out_specs=vspec(),
        scratch_shapes=[
            VMEM((4, *values.shape), F32),
            VMEM((depth + 3, *values.shape), F32),
            pltpu.SemaphoreType.DMA((depth + 2,)),
            pltpu.SemaphoreType.DMA((depth + 2,)),
        ],
        compiler_params=comm_params(6, 8),
        name="scalar_sum",
    )(values)


class KernelMoves:
    def __init__(self, depth):
        self.depth = depth
        self.number = 10

    def next(self):
        self.number += 1
        return self.number

    def small(self, token_ids, target_ids, mask, norms):
        packed = jnp.concatenate([v.reshape(-1, 128) for v in (token_ids, target_ids, mask)], axis=0)
        each = packed.shape[0] // 3
        low = jnp.pad(norms.astype(BF), ((0, 16 - norms.shape[0]), (0, 0)))
        ints, norms_all = small_gather(self.depth, packed, low)
        norms_all = jnp.transpose(norms_all, (1, 0, 2)).reshape(16, -1)[: norms.shape[0]]
        return [ints[:, i * each : (i + 1) * each].reshape(-1) for i in range(3)] + [norms_all]

    def embed(self, table_low, local_ids, rows):
        return embed_call(self.depth, table_low, local_ids.astype(F32).reshape(-1, 1, rows))

    def gather_group(self, own):
        return group_gather(own, self.next())

    def sum_group(self, parts):
        return group_sum(parts, self.next())

    def head(self, hidden, table_low, targets, weights, vocab_size):
        rows = hidden.shape[0]
        targets = targets.astype(F32).reshape(-1, 1, rows)
        weights = weights.reshape(-1, 1, rows)
        hidden_all, expo, top, total, picked = logits_call(self.depth, hidden, table_low, targets)
        grad_hidden, grads = grads_call(
            self.depth, vocab_size, table_low, targets, weights, top, total, expo
        )
        shard, width = table_low.shape
        hidden_all = hidden_all.reshape(-1, width)
        table_grad = contract_rows(grads.reshape(-1, shard), hidden_all)
        weights = weights.reshape(-1)
        counted = (weights > 0.0).astype(F32).astype(BF)
        hidden_sum = dot_nn(counted[None], hidden_all)[0] * jnp.max(weights)
        first = (lax.axis_index("dp") * lax.axis_size("mp") + lax.axis_index("mp")) * rows
        own_logs = lax.dynamic_slice(total.reshape(-1), (first,), (rows,))
        log_sum = jnp.sum(own_logs * lax.dynamic_slice(weights, (first,), (rows,)))
        picked_sum = jnp.sum(picked.reshape(-1) * weights)
        return grad_hidden, table_grad, log_sum, picked_sum, hidden_sum

    def scatter(self, grad_start, norms_grad, local_ids, table_grad, span):
        rows = grad_start.shape[0]
        count = norms_grad.shape[0]
        rest = jnp.pad(norms_grad, ((0, 16 - count), (0, 0)))
        sent = jnp.concatenate([grad_start, rest], axis=0).astype(BF)
        ids = local_ids.astype(F32).reshape(-1, 1, rows)
        table_grad, positions_grad, rest = scatter_call(self.depth, sent, ids, table_grad, span)
        dp = lax.axis_index("dp")
        part = rest.shape[1] // lax.axis_size("dp")
        norms_part = lax.dynamic_slice(rest, (0, dp * part), (16, part))[:count]
        return table_grad, positions_grad, norms_part

    def total(self, scalars):
        row = jnp.concatenate([jnp.full((1, 128), value, F32) for value in scalars], axis=0)
        row = jnp.pad(row, ((0, 8 - len(scalars)), (0, 0)))
        summed = scalar_sum(self.depth, row)
        return [summed[i, 0] for i in range(len(scalars))]


class PlainMoves:
    parts = 4

    def split(self, values, rows):
        piece = rows // self.parts
        return jnp.swapaxes(values.reshape(-1, self.parts, piece), 0, 1).reshape(self.parts, -1)

    def small(self, token_ids, target_ids, mask, norms):
        found = [lax.all_gather(v.reshape(-1), "dp", tiled=True) for v in (token_ids, target_ids, mask)]
        return found + [lax.all_gather(norms.astype(BF), "dp", axis=1, tiled=True)]

    def embed(self, table_low, local_ids, rows):
        def one(ids):
            looked = jnp.take(table_low, jnp.maximum(ids, 0), axis=0)
            looked = jnp.where(ids[:, None] >= 0, looked, jnp.zeros((), BF))
            return lax.psum_scatter(looked, ("dp", "mp"), tiled=True)

        return lax.map(one, self.split(local_ids, rows)).reshape(rows, -1)

    def gather_group(self, own):
        return lax.all_gather(own, "mp", tiled=True)

    def sum_group(self, parts):
        return lax.psum_scatter(parts, "mp", tiled=True)

    def head(self, hidden, table_low, targets, weights, vocab_size):
        rows, width = hidden.shape
        shard = table_low.shape[0]

        def one(carried, packed):
            own, ids, weight = packed
            table_grad, log_sum, picked_sum, hidden_sum = carried
            hidden_all = lax.all_gather(own, ("dp", "mp"), tiled=True)
            logits = contract_cols(hidden_all, table_low)
            top = lax.pmax(jnp.max(logits, axis=1), ("dp", "mp"))
            onehot = jnp.arange(shard)[None, :] == ids[:, None]
            picked = jnp.sum(jnp.where(onehot, logits, 0.0), axis=1)
            total = lax.psum(jnp.sum(jnp.exp(logits - top[:, None]), axis=1), ("dp", "mp"))
            total = top + jnp.log(total)
            grads = jnp.exp(logits - total[:, None]) - jnp.where(onehot, 1.0 - smoothing, 0.0)
            grads = ((grads - smoothing / vocab_size) * weight[:, None]).astype(BF)
            partial = dot_nn(grads, table_low).astype(BF)
            grad_hidden = lax.psum_scatter(partial, ("dp", "mp"), tiled=True).astype(F32)
            hidden_sum = hidden_sum + jnp.sum(weight[:, None] * hidden_all.astype(F32), axis=0)
            carried = (
                table_grad + contract_rows(grads, hidden_all),
                log_sum + jnp.sum(total * weight),
                picked_sum + jnp.sum(picked * weight),
                hidden_sum,
            )
            return carried, grad_hidden

        zero = jnp.zeros((), F32)
        first = (jnp.zeros((shard, width), F32), zero, zero, jnp.zeros((width,), F32))
        own = hidden.reshape(self.parts, rows // self.parts, width)
        carried, grad_hidden = lax.scan(
            one, first, (own, self.split(targets, rows), self.split(weights, rows))
        )
        table_grad, log_sum, picked_sum, hidden_sum = carried
        devices = lax.axis_size("dp") * lax.axis_size("mp")
        return grad_hidden.reshape(rows, width), table_grad, log_sum / devices, picked_sum, hidden_sum

    def scatter(self, grad_start, norms_grad, local_ids, table_grad, span):
        shard = table_grad.shape[0]
        rows, width = grad_start.shape

        def one(carried, packed):
            own, ids = packed
            everything = lax.all_gather(own, ("dp", "mp"), tiled=True).astype(F32)
            safe = jnp.where(ids >= 0, ids, shard)
            return carried + jax.ops.segment_sum(everything, safe, num_segments=shard), None

        own = grad_start.astype(BF).reshape(self.parts, rows // self.parts, width)
        table_grad, unused = lax.scan(one, table_grad, (own, self.split(local_ids, rows)))
        spread = jnp.zeros((lax.axis_size("mp") * rows, width), F32)
        spread = lax.dynamic_update_slice(spread, grad_start, (lax.axis_index("mp") * rows, 0))
        positions_grad = lax.psum(lax.psum_scatter(spread, "dp", tiled=True), "mp")
        norms_part = lax.psum(
            lax.psum_scatter(norms_grad, "dp", scatter_dimension=1, tiled=True), "mp"
        )
        return table_grad, positions_grad, norms_part

    def total(self, scalars):
        return list(lax.psum(tuple(scalars), ("dp", "mp")))


def attend_scores(queries, keys, length):
    scores = jnp.einsum("qhe,khe->hqk", queries, keys, preferred_element_type=F32) * HD ** (-0.5)
    place_at = jnp.arange(queries.shape[0])
    allowed = (place_at[None, :] <= place_at[:, None]) & (place_at[None, :] < length)
    return jnp.where(allowed[None], scores, -1e30)


def attend_forward(queries, keys, values, length):
    scores = attend_scores(queries, keys, length)
    top = jnp.max(scores, axis=-1, keepdims=True)
    log_total = jnp.log(jnp.sum(jnp.exp(scores - top), axis=-1, keepdims=True)) + top
    probs = jnp.exp(scores - log_total).astype(BF)
    attended = jnp.einsum("hqk,khe->qhe", probs, values, preferred_element_type=F32)
    return attended.astype(BF), log_total


def attend_backward(queries, keys, values, length, log_total, grad):
    probs = jnp.exp(attend_scores(queries, keys, length) - log_total)
    grad_values = jnp.einsum("hqk,qhe->khe", probs.astype(BF), grad, preferred_element_type=F32)
    grad_probs = jnp.einsum("qhe,khe->hqk", grad, values, preferred_element_type=F32)
    inner = jnp.sum(grad_probs * probs, axis=-1, keepdims=True)
    grad_scores = (probs * (grad_probs - inner)).astype(BF)
    scale = HD ** (-0.5)
    grad_queries = jnp.einsum("hqk,khe->qhe", grad_scores, keys, preferred_element_type=F32) * scale
    grad_keys = jnp.einsum("hqk,qhe->khe", grad_scores, queries, preferred_element_type=F32) * scale
    return grad_queries.astype(BF), grad_keys.astype(BF), grad_values.astype(BF)


def local(
    moves,
    token_ids,
    target_ids,
    loss_mask,
    lengths,
    step_count,
    *weights,
):
    masters, firsts, seconds = weights[:7], weights[7:14], weights[14:]
    table, positions, attn_in, attn_out, mlp_in, mlp_out, norms = masters
    shard = table.shape[0]
    width = table.shape[1]
    dp, mp = lax.axis_index("dp"), lax.axis_index("mp")
    dp_count, mp_count = lax.axis_size("dp"), lax.axis_size("mp")
    vocab_size = shard * dp_count * mp_count
    seq_len = token_ids.shape[1]
    rows = token_ids.size // mp_count
    table_low = table.astype(BF)
    ids_all, targets_all, mask_all, norms_all = moves.small(token_ids, target_ids, loss_mask, norms)
    gains = norms_all.astype(F32)
    mask_all = mask_all.astype(F32)
    token_total = jnp.sum(mask_all)
    row_weights = mask_all / token_total
    base = (dp * mp_count + mp) * shard

    def local_of(ids):
        inside = (ids >= base) & (ids < base + shard)
        return jnp.where(inside, ids - base, -1)

    local_ids, local_targets = local_of(ids_all), local_of(targets_all)
    attn_pack = jnp.concatenate([attn_in, attn_out[None]], axis=0).astype(BF)
    mlp_pack = jnp.stack([mlp_in, mlp_out]).astype(BF)
    positions_all = lax.all_gather(positions.astype(BF), "dp", axis=0, tiled=True)
    attn_all = lax.all_gather(attn_pack, "dp", axis=1, tiled=True)
    mlp_all = lax.all_gather(mlp_pack, "dp", axis=1, tiled=True)

    embedded = moves.embed(table_low, local_ids, rows)
    first_row = (mp * rows) % seq_len
    own_positions = lax.dynamic_slice(positions_all, (first_row, 0), (rows, width))
    start_rows = embedded.astype(F32) + own_positions.astype(F32)
    normed_one = moves.gather_group(layer_norm(start_rows, gains[0], gains[1]).astype(BF))
    head_shape = (seq_len, attn_all.shape[2] // HD, HD)
    queries, keys, values = (dot_nn(normed_one, attn_all[i]).astype(BF) for i in range(3))
    heads = [v.reshape(head_shape) for v in (queries, keys, values)]
    attended, log_total = attend_forward(*heads, lengths[0])
    attended = attended.reshape(seq_len, -1)
    middle = start_rows + moves.sum_group(contract_cols(attended, attn_all[3]))
    normed_two = moves.gather_group(layer_norm(middle, gains[2], gains[3]).astype(BF))
    pre_gelu = dot_nn(normed_two, mlp_all[0])
    activated = gelu_tanh(pre_gelu).astype(BF)
    last_rows = middle + moves.sum_group(contract_cols(activated, mlp_all[1]))
    hidden = layer_norm(last_rows, gains[4], gains[5]).astype(BF)

    grad_hidden, table_grad, log_sum, picked_sum, hidden_sum = moves.head(
        hidden, table_low, local_targets, row_weights, vocab_size
    )
    column_sum = jnp.sum(table_low.astype(F32), axis=0)
    loss_part = (
        log_sum
        - (1.0 - smoothing) * picked_sum
        - smoothing / vocab_size * jnp.sum(hidden_sum * column_sum)
    )

    unused, norm_three_back = jax.vjp(layer_norm, last_rows, gains[4], gains[5])
    grad_last, gain_three, shift_three = norm_three_back(grad_hidden)
    grad_last_low = moves.gather_group(grad_last.astype(BF))
    mlp_out_grad = contract_rows(grad_last_low, activated)
    grad_activated = dot_nn(grad_last_low, mlp_all[1])
    unused, gelu_back = jax.vjp(gelu_tanh, pre_gelu)
    grad_pre = gelu_back(grad_activated)[0].astype(BF)
    mlp_in_grad = contract_rows(normed_two, grad_pre)
    grad_normed_two = moves.sum_group(contract_cols(grad_pre, mlp_all[0]))
    mlp_share = lax.psum_scatter(
        jnp.stack([mlp_in_grad, mlp_out_grad]).astype(BF), "dp", scatter_dimension=1, tiled=True
    ).astype(F32)
    unused, norm_two_back = jax.vjp(layer_norm, middle, gains[2], gains[3])
    grad_from_two, gain_two, shift_two = norm_two_back(grad_normed_two)
    grad_middle = grad_last + grad_from_two
    grad_middle_low = moves.gather_group(grad_middle.astype(BF))
    attn_out_grad = contract_rows(grad_middle_low, attended)
    grad_attended = dot_nn(grad_middle_low, attn_all[3]).astype(BF).reshape(head_shape)
    members = [
        v.reshape(seq_len, -1)
        for v in attend_backward(*heads, lengths[0], log_total, grad_attended)
    ]
    attn_grads = [contract_rows(normed_one, v) for v in members] + [attn_out_grad]
    grad_normed_one = moves.sum_group(
        sum(contract_cols(members[i], attn_all[i]) for i in range(3))
    )
    attn_share = lax.psum_scatter(
        jnp.stack(attn_grads).astype(BF), "dp", scatter_dimension=1, tiled=True
    ).astype(F32)
    unused, norm_one_back = jax.vjp(layer_norm, start_rows, gains[0], gains[1])
    grad_from_one, gain_one, shift_one = norm_one_back(grad_normed_one)
    grad_start = grad_middle + grad_from_one
    norms_grad = jnp.stack([gain_one, shift_one, gain_two, shift_two, gain_three, shift_three])
    table_grad, positions_grad, norms_part = moves.scatter(
        grad_start, norms_grad, local_ids, table_grad, positions.shape[0]
    )
    shares = (
        table_grad,
        positions_grad,
        attn_share[:3],
        attn_share[3],
        mlp_share[0],
        mlp_share[1],
        norms_part,
    )
    copies = (1.0, mp_count, 1.0, 1.0, 1.0, 1.0, mp_count)
    squares = sum(jnp.sum(v * v) / n for v, n in zip(shares, copies))
    total_square, loss = moves.total([squares, loss_part])
    grad_norm = jnp.sqrt(total_square)
    factor = jnp.minimum(1.0, clip_norm / (grad_norm + 1e-06))
    step_float = step_count[0].astype(F32)
    updated = [
        adam_update(
            masters[i],
            firsts[i],
            seconds[i],
            factor * shares[i],
            learn_rates[i],
            decay_rates[i],
            step_float,
        )
        for i in range(7)
    ]
    return (loss, grad_norm) + tuple(updated[i][part] for part in range(3) for i in range(7))


def fits_kernels(mesh):
    if mesh.shape["mp"] != 4 or mesh.shape["dp"] != 8:
        return False
    for (dp, mp), item in zip(
        ((i, j) for i in range(8) for j in range(4)), mesh.devices.reshape(-1)
    ):
        coords = getattr(item, "coords", None)
        if coords is not None and (tuple(coords), item.core_on_chip) != (
            (dp % 2, mp // 2, dp // 2),
            mp % 2,
        ):
            return False
    return True


def solution(mesh):
    table, rows, heads, grid, norms = (
        P(("dp", "mp"), None),
        P("dp", None),
        P(None, "dp", "mp"),
        P("dp", "mp"),
        P(None, "dp"),
    )
    each = (table, rows, heads, grid, grid, grid, norms)
    in_specs = (rows, rows, rows, P("dp"), P()) + each * 3
    out_specs = (P(), P()) + each * 3
    moves = KernelMoves(mesh.shape["dp"] // 2) if fits_kernels(mesh) else PlainMoves()
    return jax.shard_map(
        functools.partial(local, moves),
        mesh=mesh,
        in_specs=in_specs,
        out_specs=out_specs,
        check_vma=False,
    )
```

```python
import functools

import jax
import jax.numpy as jnp
from jax import lax
from jax.experimental import pallas as pl
from jax.experimental.pallas import tpu as pltpu
from jax.sharding import PartitionSpec as P

HD = 64
VOCAB = 50688
MESH = pl.DeviceIdType.MESH
ANY = pl.ANY
VMEM = pltpu.VMEM
BF = jnp.bfloat16
F32 = jnp.float32

smoothing = 0.1
clip_norm = 0.01
beta_one = 0.9
beta_two = 0.999
adam_eps = 1e-08
learn_rates = (0.06, 0.06, 0.03, 0.03, 0.03, 0.004, 0.3)
decay_rates = (0.1, 0.0, 0.1, 0.1, 0.1, 0.1, 0.0)


def layer_norm(values, gain_row, shift_row):
    centered = values - jnp.mean(values, axis=-1, keepdims=True)
    spread = jnp.mean(centered * centered, axis=-1, keepdims=True)
    return centered * lax.rsqrt(spread + 1e-05) * gain_row + shift_row


def gelu_tanh(values):
    return jax.nn.gelu(values, approximate=True)


def adam_update(weight, first_moment, second, grad_item, rate, decay, step_float):
    first_new = beta_one * first_moment + (1.0 - beta_one) * grad_item
    second_new = beta_two * second + (1.0 - beta_two) * grad_item * grad_item
    first_hat = first_new / (1.0 - beta_one**step_float)
    second_hat = second_new / (1.0 - beta_two**step_float)
    weight_new = weight - rate * (first_hat / (jnp.sqrt(second_hat) + adam_eps) + decay * weight)
    return (weight_new, first_new, second_new)


def contract_rows(left, right):
    return lax.dot_general(
        left, right, (((0,), (0,)), ((), ())), preferred_element_type=F32
    )


def contract_cols(left, right):
    return lax.dot_general(
        left, right, (((1,), (1,)), ((), ())), preferred_element_type=F32
    )


def dot_nn(left, right):
    return lax.dot_general(
        left, right, (((1,), (0,)), ((), ())), preferred_element_type=F32
    )


def place():
    dp = lax.axis_index("dp")
    mp = lax.axis_index("mp")
    return dp // 2, dp % 2, mp // 2, mp % 2


def device(z, x, y, c):
    return (z * 2 + x, y * 2 + c)


def flip(bit, by):
    return bit + by - 2 * bit * by


def greet(peers):
    barrier = pltpu.get_barrier_semaphore()
    for peer in peers:
        pl.semaphore_signal(barrier, inc=1, device_id=peer, device_id_type=MESH)
    pl.semaphore_wait(barrier, len(peers))


def remote(src, dst, send_sem, recv_sem, peer):
    return pltpu.make_async_remote_copy(
        src_ref=src,
        dst_ref=dst,
        send_sem=send_sem,
        recv_sem=recv_sem,
        device_id=peer,
        device_id_type=MESH,
    )


def to_column(row):
    wide = jnp.broadcast_to(row, (128, row.shape[1]))
    return jnp.transpose(wide)[:, :1]


def to_row(column):
    wide = jnp.broadcast_to(column, (column.shape[0], 128))
    return jnp.transpose(wide)[:1, :]


ARRIVALS = (
    "000o 010p 100d 001q 200d 110p 011q 101q 201q 300d 210p 111q 310d 301q 211q 311q",
    "100o 000u 200d 010u 300d 110p 201q 310d 001q 301q 210p 111q 011q 101q 211q 311q",
)
DEPTH = 4
EVENTS = 16


def sent_on(z, source, kind):
    up = ["u"] if z < DEPTH - 1 else []
    down = ["d"] if z > 0 else []
    if source in (1, 2):
        return {"o": up + down + ["p", "q"], "u": up + ["p", "q"], "d": down + ["p", "q"]}.get(
            kind, ["q"] if kind == "p" else []
        )
    return {
        "o": ["p"] + up + down + ["q"],
        "p": up + down + ["q"],
        "u": up + ["q"],
        "d": down + ["q"],
    }.get(kind, [])


@functools.lru_cache
def route_tables():
    mirror = {"u": "d", "d": "u"}
    events = {}
    for z in range(DEPTH):
        rows = []
        for item in ARRIVALS[min(z, DEPTH - 1 - z)].split():
            source, first, second, kind = int(item[0]), int(item[1]), int(item[2]), item[3]
            if z >= 2:
                source, kind = DEPTH - 1 - source, mirror.get(kind, kind)
            rows.append((source, first, second, kind))
        events[z] = rows
    order = ("p", "q", "u", "d")
    slots, firsts, flags = {}, {}, {}
    for z in range(DEPTH):
        count = 0
        turned = ("p", "q", "u", "d") if z < 2 else ("p", "q", "d", "u")
        for n, (source, first, second, kind) in enumerate(events[z]):
            sends = sent_on(z, source, kind)
            firsts[z, n] = count
            flags[z, n] = sum(1 << i for i, k in enumerate(turned) if k in sends)
            for k in turned:
                if k in sends:
                    slots[z, source, first, second, k] = count
                    count += 1
    tables = []
    most = 1 + max(slots.values())
    for z in range(2):
        rows = []
        for n, (source, first, second, kind) in enumerate(events[z]):
            if kind == "o":
                slot, origin = 0, 0
            else:
                at = z - 1 if kind == "u" else z + 1 if kind == "d" else z
                up_first = 1 - first if kind == "p" else first
                up_second = 1 - second if kind == "q" else second
                slot = slots[at, source, up_first, up_second, kind]
                origin = order.index(kind)
            rows.append((source, 2 * first + second, flags[z, n], slot, firsts[z, n], origin))
        tables.append(rows)
    return tables, most


RADIX = 1024


class Route:
    def __init__(self):
        self.z, self.x, self.y, self.c = place()
        tables, self.slots = route_tables()
        kind = flip(self.z % 2, self.z // 2)
        self.mirrored = self.z // 2
        self.packed = []
        for digits in (
            lambda row: row[0] + 4 * row[1] + 16 * row[2] + 256 * row[5],
            lambda row: row[3] + 32 * row[4],
        ):
            low, high = (
                [digits(rows[n]) + RADIX * digits(rows[n + 1]) for n in range(0, EVENTS, 2)]
                for rows in tables
            )
            self.packed.append([a + kind * (b - a) for a, b in zip(low, high)])
        sign = 1 - 2 * self.mirrored
        z, x, y, c = self.z, self.x, self.y, self.c
        self.c_peer = device(z, x, y, 1 - c)
        self.peers = (
            device(z, flip(x, 1 - c), flip(y, c), c),
            device(z, flip(x, c), flip(y, 1 - c), c),
            device(z + sign, x, y, c),
            device(z - sign * kind, x, y, c),
        )

    def greet(self):
        z, x, y, c = self.z, self.x, self.y, self.c
        along = [device((z + k) % DEPTH, x, y, c) for k in range(1, DEPTH)]
        greet(along + [self.peers[0], self.peers[1], self.c_peer])

    def digits(self, which, n):
        pair = n // 2
        bits = (pair % 2, pair // 2 % 2, pair // 4)
        total = 0
        for number, value in enumerate(self.packed[which]):
            chosen = value
            for i, bit in enumerate(bits):
                chosen = chosen * (bit if number >> i & 1 else 1 - bit)
            total = total + chosen
        return total // (1 + (RADIX - 1) * (n % 2)) % RADIX

    def flags(self, n):
        return self.digits(0, n) // 16 % 16

    def origin(self, n):
        return self.digits(0, n) // 256

    def parent_slot(self, n):
        return self.digits(1, n) % 32

    def first_slot(self, n):
        return self.digits(1, n) // 32

    def family(self, n, core):
        digits = self.digits(0, n)
        source = digits % 4
        source = source + self.mirrored * (DEPTH - 1 - 2 * source)
        first, second = digits // 8 % 2, digits // 4 % 2
        by_x = first * (1 - core) + second * core
        by_y = second * (1 - core) + first * core
        return (source * 2 + flip(self.x, by_x)) * 2 + flip(self.y, by_y)

    def sends(self, n, act):
        flags = self.flags(n)
        for i in range(4):

            @pl.when((flags // (1 << i)) % 2 == 1)
            def _():
                act(i)


def gather_scratch():
    return [
        pltpu.SemaphoreType.DMA((1,)),
        pltpu.SemaphoreType.DMA((4 * EVENTS,)),
        pltpu.SemaphoreType.DMA((EVENTS,)),
        pltpu.SemaphoreType.DMA((EVENTS,)),
        pltpu.SemaphoreType.DMA((EVENTS,)),
    ]


def gather_blocks(own_ref, land, scratch, consume):
    lsem, ss, rs, cs, cr = scratch
    route = Route()
    c = route.c
    route.greet()
    own = route.family(0, c) * 2 + c
    local = pltpu.make_async_copy(own_ref, land.at[own], lsem.at[0])
    local.start()
    local.wait()

    def copy(family, i):
        block = land.at[family * 2 + c]
        return remote(block, block, ss.at[i * EVENTS + family], rs.at[family], route.peers[i])

    def c_copy(family, core):
        block = land.at[family * 2 + core]
        return remote(block, block, cs.at[family], cr.at[family], route.c_peer)

    def event(n, carry):
        @pl.when(n < EVENTS)
        def _():
            family = route.family(n, c)

            @pl.when(n >= 1)
            def _():
                copy(family, 0).wait_recv()

            route.sends(n, lambda i: copy(family, i).start())
            c_copy(family, c).start()

        def one(i, inner):
            at = n - i

            @pl.when((at >= 0) & (at < EVENTS))
            def _():
                core = flip(c, i)
                family = route.family(at, core)

                @pl.when(i == 1)
                def _():
                    c_copy(family, core).wait_recv()

                consume(family * 2 + core, 2 * n - 1 + i + (EVENTS - n) // EVENTS - n // EVENTS)

            return inner

        lax.fori_loop(0, 2, one, 0)
        return carry

    lax.fori_loop(0, EVENTS + 1, event, 0)

    def drain(n, carry):
        family = route.family(n, c)
        route.sends(n, lambda i: copy(family, i).wait_send())
        c_copy(family, c).wait_send()
        return carry

    lax.fori_loop(0, EVENTS, drain, 0)


def reduce_scratch(rows, width):
    slots = route_tables()[1]
    return [
        VMEM((2, rows, width), F32),
        VMEM((EVENTS, rows, width), BF),
        VMEM((EVENTS, rows, width), BF),
        VMEM((EVENTS, rows, width), BF),
        VMEM((slots, rows, width), BF),
        pltpu.SemaphoreType.DMA((EVENTS,)),
        pltpu.SemaphoreType.DMA((slots,)),
        pltpu.SemaphoreType.DMA((EVENTS,)),
        pltpu.SemaphoreType.DMA((EVENTS,)),
    ]


def reduce_blocks(out_ref, scratch, produce, start=None):
    own, oth, cbuf, sbuf, rbuf, ss, rs, cs, cr = scratch
    route = Route()
    c = route.c

    def target(k):
        core = flip(c, 1 - k % 2)
        return route.family(EVENTS - 1 - k // 2, core) * 2 + core

    route.greet()
    if start is not None:
        start(target)

    def c_copy(n):
        return remote(oth.at[n], cbuf.at[n], cs.at[n], cr.at[n], route.c_peer)

    def copy(n, slot, i):
        return remote(sbuf.at[n], rbuf.at[slot], ss.at[n], rs.at[slot], route.peers[i])

    def finish(n):
        half = n % 2
        c_copy(n).wait_recv()
        own[half] += cbuf[n].astype(F32)
        flags, base = route.flags(n), route.first_slot(n)

        def arrived(i):
            slot = base
            for lower in range(i):
                slot = slot + (flags // (1 << lower)) % 2
            copy(n, slot, 0).wait_recv()
            own[half] += rbuf[slot].astype(F32)

        route.sends(n, arrived)

        @pl.when(n > 0)
        def _():
            sbuf[n] = own[half].astype(BF)
            for i, back in enumerate((0, 1, 3, 2)):

                @pl.when(route.origin(n) == i)
                def _():
                    copy(n, route.parent_slot(n), back).start()

    def step(m, carry):
        n = EVENTS - 1 - m

        def one(i, inner):
            @pl.when(m < EVENTS)
            def _():
                value = produce(2 * m + i, target(2 * m + i))

                @pl.when(i == 0)
                def _():
                    oth[n] = value.astype(BF)
                    c_copy(n).start()

                @pl.when(i == 1)
                def _():
                    own[n % 2] = value

            @pl.when((i == 0) & (m >= 1))
            def _():
                finish(n + 1)

            return inner

        lax.fori_loop(0, 2, one, 0)
        return carry

    lax.fori_loop(0, EVENTS + 1, step, 0)
    out_ref[...] = own[0].astype(out_ref.dtype)

    def drain(n, carry):
        c_copy(n).wait_send()

        @pl.when(n > 0)
        def _():
            copy(n, 0, 0).wait_send()

        return carry

    lax.fori_loop(0, EVENTS, drain, 0)


def comm_params(number, limit_mib=60):
    return pltpu.CompilerParams(
        collective_id=number, has_side_effects=True, vmem_limit_bytes=limit_mib << 20
    )


def vspec():
    return pl.BlockSpec(memory_space=VMEM)


def aspec():
    return pl.BlockSpec(memory_space=ANY)


def embed_kernel(depth, table_ref, ids_ref, out_ref, *scratch):
    def produce(n, block):
        wanted = to_column(ids_ref[block])
        rows = wanted.shape[0]
        vocab = lax.broadcasted_iota(jnp.int32, (rows, table_ref.shape[0]), 1).astype(F32)
        onehot = (vocab == wanted).astype(F32).astype(BF)
        return dot_nn(onehot, table_ref[...])

    reduce_blocks(out_ref, scratch, produce)


def embed_call(depth, table_low, local_ids):
    blocks, unused, rows = local_ids.shape
    width = table_low.shape[1]
    return pl.pallas_call(
        functools.partial(embed_kernel, depth),
        out_shape=jax.ShapeDtypeStruct((rows, width), BF),
        in_specs=[vspec(), vspec()],
        out_specs=vspec(),
        scratch_shapes=reduce_scratch(rows, width),
        compiler_params=comm_params(1),
        name="embed_exchange",
    )(table_low, local_ids)


def combine_logs(first, second):
    top = jnp.maximum(first, second)
    return top + jnp.log(jnp.exp(first - top) + jnp.exp(second - top))


def logits_kernel(
    depth, vocab_size, hidden_ref, table_ref, targets_ref, all_ref, expo_ref, top_ref, total_ref, picked_ref,
    land, stage, snap, got, out_sem, all_sem, xs, xr, *sems
):
    z, x, y, c = place()
    blocks = land.shape[0]
    even = smoothing / vocab_size

    def out_copy(slot, block):
        return pltpu.make_async_copy(stage.at[slot], expo_ref.at[block], out_sem.at[slot])

    def keep(block):
        return pltpu.make_async_copy(land.at[block], all_ref.at[block], all_sem.at[block])

    def consume(block, number):
        slot = number % 2
        keep(block).start()
        logits = contract_cols(land[block], table_ref[...])
        top = jnp.max(logits, axis=1, keepdims=True)
        expo = jnp.exp(logits - top)
        total = jnp.sum(expo, axis=1, keepdims=True)
        wanted = to_column(targets_ref[block])
        vocab = lax.broadcasted_iota(jnp.int32, logits.shape, 1).astype(F32)
        mixed = logits * jnp.where(vocab == wanted, 1.0 - smoothing + even, even)
        picked = jnp.sum(mixed, axis=1, keepdims=True)
        top_row = to_row(top)
        top_ref[block] = top_row
        picked_ref[block] = to_row(picked)
        total_ref[block] = top_row + jnp.log(to_row(total))

        @pl.when(number >= 2)
        def _():
            out_copy(slot, block).wait()

        stage[slot] = expo.astype(BF)
        out_copy(slot, block).start()

    gather_blocks(hidden_ref, land, sems, consume)
    peers = [device(z, x, y, 1 - c), device(z, x, 1 - y, c), device(z, 1 - x, y, c)]
    for number, peer in enumerate(peers):
        snap[number] = total_ref[...]
        copy = remote(snap.at[number], got.at[number], xs.at[number], xr.at[number], peer)
        copy.start()
        copy.wait()
        total_ref[...] = combine_logs(snap[number], got[number])
    snap[3] = total_ref[...]
    copies = [
        remote(
            snap.at[3], got.at[2 + k], xs.at[2 + k], xr.at[2 + k], device((z + k) % depth, x, y, c)
        )
        for k in range(1, depth)
    ]
    for copy in copies:
        copy.start()
    for k, copy in enumerate(copies):
        copy.wait()
        total_ref[...] = combine_logs(total_ref[...], got[3 + k])
    for slot in range(2):
        out_copy(slot, 0).wait()

    def kept(block, carry):
        keep(block).wait()
        return carry

    lax.fori_loop(0, blocks, kept, 0)


def logits_call(depth, vocab_size, hidden, table_low, targets):
    blocks, unused, rows = targets.shape
    shard, width = table_low.shape
    row_shape = jax.ShapeDtypeStruct((blocks, 1, rows), F32)
    return pl.pallas_call(
        functools.partial(logits_kernel, depth, vocab_size),
        out_shape=(
            jax.ShapeDtypeStruct((blocks, rows, width), BF),
            jax.ShapeDtypeStruct((blocks, rows, shard), BF),
            row_shape,
            row_shape,
            row_shape,
        ),
        in_specs=[vspec(), vspec(), vspec()],
        out_specs=(aspec(), aspec(), vspec(), vspec(), vspec()),
        scratch_shapes=[
            VMEM((blocks, rows, width), BF),
            VMEM((2, rows, shard), BF),
            VMEM((4, blocks, 1, rows), F32),
            VMEM((2 + depth, blocks, 1, rows), F32),
            pltpu.SemaphoreType.DMA((2,)),
            pltpu.SemaphoreType.DMA((blocks,)),
            pltpu.SemaphoreType.DMA((2 + depth,)),
            pltpu.SemaphoreType.DMA((2 + depth,)),
        ]
        + gather_scratch(),
        compiler_params=comm_params(2),
        name="logits_exchange",
    )(hidden, table_low, targets)


def grads_kernel(
    depth, vocab_size, table_ref, targets_ref, weights_ref, top_ref, total_ref, expo_ref, out_ref, grad_ref,
    inbox, outbox, in_sem, out_sem, *scratch
):
    steps = 2 * EVENTS

    def fetch(slot, block):
        return pltpu.make_async_copy(expo_ref.at[block], inbox.at[slot], in_sem.at[slot])

    def store(slot, block):
        return pltpu.make_async_copy(outbox.at[slot], grad_ref.at[block], out_sem.at[slot])

    targets = []

    def start(target):
        targets.append(target)
        fetch(0, target(0)).start()

    def produce(n, block):
        slot = n % 2
        fetch(slot, block).wait()

        @pl.when(n + 1 < steps)
        def _():
            fetch(1 - slot, targets[0](n + 1)).start()

        weight = weights_ref[block]
        scale = to_column(jnp.exp(top_ref[block] - total_ref[block]) * weight)
        wanted = to_column(targets_ref[block])
        weight = to_column(weight)
        vocab = lax.broadcasted_iota(jnp.int32, inbox.shape[1:], 1).astype(F32)
        low = -(smoothing / vocab_size) * weight
        hit = low - (1.0 - smoothing) * weight
        grad = inbox[slot].astype(F32) * scale + jnp.where(vocab == wanted, hit, low)
        grad = grad.astype(BF)

        @pl.when(n >= 2)
        def _():
            store(slot, block).wait()

        outbox[slot] = grad
        store(slot, block).start()
        return dot_nn(grad, table_ref[...])

    reduce_blocks(out_ref, scratch, produce, start)
    for slot in range(2):
        store(slot, 0).wait()


def grads_call(depth, vocab_size, table_low, targets, weights, top, total, expo):
    blocks, rows, shard = expo.shape
    width = table_low.shape[1]
    return pl.pallas_call(
        functools.partial(grads_kernel, depth, vocab_size),
        out_shape=(
            jax.ShapeDtypeStruct((rows, width), F32),
            jax.ShapeDtypeStruct((blocks, rows, shard), BF),
        ),
        in_specs=[vspec(), vspec(), vspec(), vspec(), vspec(), aspec()],
        out_specs=(vspec(), aspec()),
        scratch_shapes=[
            VMEM((2, rows, shard), BF),
            VMEM((2, rows, shard), BF),
            pltpu.SemaphoreType.DMA((2,)),
            pltpu.SemaphoreType.DMA((2,)),
        ]
        + reduce_scratch(rows, width),
        compiler_params=comm_params(3),
        name="grads_exchange",
    )(table_low, targets, weights, top, total, expo)


def scatter_kernel(
    depth, rows, sent_ref, ids_ref, grads_ref, hidden_ref, out_ref, pos_ref, rest_ref, square_ref,
    left, right, left_sem, right_sem, land, *scratch
):
    out_ref[...] = jnp.zeros(out_ref.shape, F32)
    shard = out_ref.shape[0]

    def fetch(slot, block):
        top = pl.ds(0, rows)
        return (
            pltpu.make_async_copy(grads_ref.at[block], left.at[slot, top, :], left_sem.at[slot]),
            pltpu.make_async_copy(hidden_ref.at[block], right.at[slot, top, :], right_sem.at[slot]),
        )

    for copy in fetch(0, 0):
        copy.start()

    def consume(block, number):
        slot = number % 2
        for copy in fetch(slot, number):
            copy.wait()

        @pl.when(number + 1 < land.shape[0])
        def _():
            for copy in fetch(1 - slot, number + 1):
                copy.start()

        vocab = lax.broadcasted_iota(jnp.int32, (rows, shard), 1).astype(F32)
        onehot = (vocab == to_column(ids_ref[block])).astype(F32).astype(BF)
        left[slot, rows:, :] = onehot
        right[slot, rows:, :] = land[block, :rows, :]
        out_ref[...] += contract_rows(left[slot], right[slot])

    gather_blocks(sent_ref, land, scratch, consume)
    dp = lax.axis_index("dp")
    slots = 2 * depth
    span = pos_ref.shape[0]
    per = rows // span
    total = jnp.zeros(pos_ref.shape, F32)
    rest = jnp.zeros(rest_ref.shape, F32)
    first = pl.multiple_of((dp % per) * span, span)
    for slot in range(slots):
        total = total + land[slot * 4 + dp // per, pl.ds(first, span), :].astype(F32)
    pos_ref[...] = total
    for block in range(land.shape[0]):
        rest = rest + land[block, rows:, :].astype(F32)
    rest_ref[...] = rest
    square_ref[...] = jnp.zeros(square_ref.shape, F32) + jnp.sum(out_ref[...] * out_ref[...])


def scatter_call(depth, sent, ids, grads, hidden_all, span):
    blocks, unused, rows = ids.shape
    extended, width = sent.shape
    shard = grads.shape[2]
    return pl.pallas_call(
        functools.partial(scatter_kernel, depth, rows),
        out_shape=(
            jax.ShapeDtypeStruct((shard, width), F32),
            jax.ShapeDtypeStruct((span, width), F32),
            jax.ShapeDtypeStruct((extended - rows, width), F32),
            jax.ShapeDtypeStruct((8, 128), F32),
        ),
        in_specs=[vspec(), vspec(), aspec(), aspec()],
        out_specs=(vspec(),) * 4,
        scratch_shapes=[
            VMEM((2, 2 * rows, shard), BF),
            VMEM((2, 2 * rows, width), BF),
            pltpu.SemaphoreType.DMA((2,)),
            pltpu.SemaphoreType.DMA((2,)),
            VMEM((blocks, extended, width), BF),
        ]
        + gather_scratch(),
        compiler_params=comm_params(4),
        name="rows_exchange",
    )(sent, ids, grads, hidden_all)


def group_gather_kernel(own_ref, out_ref, local_sem, send_sem, recv_sem):
    z, x, y, c = place()
    y_peer, c_peer = device(z, x, 1 - y, c), device(z, x, y, 1 - c)
    greet([y_peer, c_peer])
    own, across = y * 2 + c, (1 - y) * 2 + c
    to_y = remote(own_ref, out_ref.at[own], send_sem.at[0], recv_sem.at[0], y_peer)
    to_c = remote(own_ref, out_ref.at[own], send_sem.at[1], recv_sem.at[1], c_peer)
    on = remote(out_ref.at[across], out_ref.at[across], send_sem.at[2], recv_sem.at[2], c_peer)
    to_y.start()
    to_c.start()
    local = pltpu.make_async_copy(own_ref, out_ref.at[own], local_sem.at[0])
    local.start()
    to_y.wait_recv()
    on.start()
    local.wait()
    to_c.wait_recv()
    on.wait_recv()
    to_y.wait_send()
    to_c.wait_send()
    on.wait_send()


def group_gather(own, number):
    rows, width = own.shape
    out = pl.pallas_call(
        group_gather_kernel,
        out_shape=jax.ShapeDtypeStruct((4, rows, width), own.dtype),
        in_specs=[vspec()],
        out_specs=aspec(),
        scratch_shapes=[
            pltpu.SemaphoreType.DMA((1,)),
            pltpu.SemaphoreType.DMA((3,)),
            pltpu.SemaphoreType.DMA((3,)),
        ],
        compiler_params=comm_params(number),
        name="group_gather",
    )(own)
    return out.reshape(4 * rows, width)


def group_sum_kernel(parts_ref, out_ref, cbuf, ybuf, mixed, send_sem, recv_sem):
    z, x, y, c = place()
    y_peer, c_peer = device(z, x, 1 - y, c), device(z, x, y, 1 - c)
    greet([y_peer, c_peer])
    copies = [
        remote(parts_ref.at[row * 2 + 1 - c], cbuf.at[i], send_sem.at[i], recv_sem.at[i], c_peer)
        for i, row in enumerate((1 - y, y))
    ]
    for copy in copies:
        copy.start()
    copies[0].wait_recv()
    mixed[...] = (parts_ref[(1 - y) * 2 + c].astype(F32) + cbuf[0].astype(F32)).astype(BF)
    across = remote(mixed, ybuf, send_sem.at[2], recv_sem.at[2], y_peer)
    across.start()
    copies[1].wait_recv()
    out_ref[...] = parts_ref[y * 2 + c].astype(F32) + cbuf[1].astype(F32)
    across.wait_recv()
    out_ref[...] += ybuf[...].astype(F32)
    for copy in copies:
        copy.wait_send()
    across.wait_send()


def group_sum(parts, number):
    rows, width = parts.shape[0] // 4, parts.shape[1]
    return pl.pallas_call(
        group_sum_kernel,
        out_shape=jax.ShapeDtypeStruct((rows, width), F32),
        in_specs=[vspec()],
        out_specs=vspec(),
        scratch_shapes=[
            VMEM((2, rows, width), BF),
            VMEM((rows, width), BF),
            VMEM((rows, width), BF),
            pltpu.SemaphoreType.DMA((3,)),
            pltpu.SemaphoreType.DMA((3,)),
        ],
        compiler_params=comm_params(number),
        name="group_sum",
    )(parts.astype(BF).reshape(4, rows, width))


def small_gather_kernel(depth, ints_ref, norms_ref, ints_out, norms_out, ss, rs, ns, nr):
    z, x, y, c = place()
    dp = lax.axis_index("dp")
    mp = lax.axis_index("mp")
    count = 2 * depth
    peers = [((dp + k) % count, mp) for k in range(1, count)]
    greet(peers)
    ints_out[dp] = ints_ref[...]
    norms_out[dp] = norms_ref[...]
    copies = []
    for k, peer in enumerate(peers):
        copies.append(remote(ints_ref, ints_out.at[dp], ss.at[k], rs.at[k], peer))
        copies.append(remote(norms_ref, norms_out.at[dp], ns.at[k], nr.at[k], peer))
    for copy in copies:
        copy.start()
    for copy in copies:
        copy.wait()


def small_gather(depth, ints, norms):
    count = 2 * depth
    return pl.pallas_call(
        functools.partial(small_gather_kernel, depth),
        out_shape=(
            jax.ShapeDtypeStruct((count, *ints.shape), ints.dtype),
            jax.ShapeDtypeStruct((count, *norms.shape), norms.dtype),
        ),
        in_specs=[vspec(), vspec()],
        out_specs=(vspec(), vspec()),
        scratch_shapes=[pltpu.SemaphoreType.DMA((count - 1,))] * 4,
        compiler_params=comm_params(5, 8),
        name="small_gather",
    )(ints, norms)


def scalar_sum_kernel(depth, own_ref, out_ref, snap, got, ss, rs):
    z, x, y, c = place()
    peers = [device(z, x, y, 1 - c), device(z, x, 1 - y, c), device(z, 1 - x, y, c)]
    z_peers = [device((z + k) % depth, x, y, c) for k in range(1, depth)]
    greet(peers + z_peers)
    snap[0] = own_ref[...]
    for number, peer in enumerate(peers):
        copy = remote(snap.at[number], got.at[depth + number], ss.at[number], rs.at[number], peer)
        copy.start()
        copy.wait()
        snap[number + 1] = snap[number] + got[depth + number]
    copies = [
        remote(snap.at[3], got.at[z], ss.at[2 + k], rs.at[2 + k], z_peers[k - 1])
        for k in range(1, depth)
    ]
    for copy in copies:
        copy.start()
    got[z] = snap[3]
    for copy in copies:
        copy.wait()
    total = got[0]
    for k in range(1, depth):
        total = total + got[k]
    out_ref[...] = total


def scalar_sum(depth, values):
    return pl.pallas_call(
        functools.partial(scalar_sum_kernel, depth),
        out_shape=jax.ShapeDtypeStruct(values.shape, F32),
        in_specs=[vspec()],
        out_specs=vspec(),
        scratch_shapes=[
            VMEM((4, *values.shape), F32),
            VMEM((depth + 3, *values.shape), F32),
            pltpu.SemaphoreType.DMA((depth + 2,)),
            pltpu.SemaphoreType.DMA((depth + 2,)),
        ],
        compiler_params=comm_params(6, 8),
        name="scalar_sum",
    )(values)


class KernelMoves:
    def __init__(self, depth):
        self.depth = depth
        self.number = 10

    def next(self):
        self.number += 1
        return self.number

    def small(self, token_ids, target_ids, mask, norms):
        packed = jnp.concatenate([v.reshape(-1, 128) for v in (token_ids, target_ids, mask)], axis=0)
        each = packed.shape[0] // 3
        low = jnp.pad(norms.astype(BF), ((0, 16 - norms.shape[0]), (0, 0)))
        ints, norms_all = small_gather(self.depth, packed, low)
        norms_all = jnp.transpose(norms_all, (1, 0, 2)).reshape(16, -1)[: norms.shape[0]]
        return [ints[:, i * each : (i + 1) * each].reshape(-1) for i in range(3)] + [norms_all]

    def embed(self, table_low, local_ids, rows):
        return embed_call(self.depth, table_low, local_ids.astype(F32).reshape(-1, 1, rows))

    def gather_group(self, own):
        return group_gather(own, self.next())

    def sum_group(self, parts):
        return group_sum(parts, self.next())

    def head(self, hidden, table_low, targets, weights, vocab_size):
        rows = hidden.shape[0]
        targets = targets.astype(F32).reshape(-1, 1, rows)
        weights = weights.reshape(-1, 1, rows)
        hidden_all, expo, top, total, picked = logits_call(
            self.depth, vocab_size, hidden, table_low, targets
        )
        grad_hidden, grads = grads_call(
            self.depth, vocab_size, table_low, targets, weights, top, total, expo
        )
        weights = weights.reshape(-1)
        first = (lax.axis_index("dp") * lax.axis_size("mp") + lax.axis_index("mp")) * rows
        own_logs = lax.dynamic_slice(total.reshape(-1), (first,), (rows,))
        log_sum = jnp.sum(own_logs * lax.dynamic_slice(weights, (first,), (rows,)))
        loss_part = log_sum - jnp.sum(picked.reshape(-1) * weights)
        return grad_hidden, (grads, hidden_all), loss_part

    def scatter(self, grad_start, norms_grad, local_ids, table_grad, span):
        rows = grad_start.shape[0]
        count = norms_grad.shape[0]
        rest = jnp.pad(norms_grad, ((0, 16 - count), (0, 0)))
        sent = jnp.concatenate([grad_start, rest], axis=0).astype(BF)
        ids = local_ids.astype(F32).reshape(-1, 1, rows)
        grads, hidden_all = table_grad
        table_grad, positions_grad, rest, square = scatter_call(
            self.depth, sent, ids, grads, hidden_all, span
        )
        dp = lax.axis_index("dp")
        part = rest.shape[1] // lax.axis_size("dp")
        norms_part = lax.dynamic_slice(rest, (0, dp * part), (16, part))[:count]
        return table_grad, positions_grad, norms_part, square[0, 0]

    def total(self, scalars):
        row = jnp.concatenate([jnp.full((1, 128), value, F32) for value in scalars], axis=0)
        row = jnp.pad(row, ((0, 8 - len(scalars)), (0, 0)))
        summed = scalar_sum(self.depth, row)
        return [summed[i, 0] for i in range(len(scalars))]


class PlainMoves:
    parts = 4

    def split(self, values, rows):
        piece = rows // self.parts
        return jnp.swapaxes(values.reshape(-1, self.parts, piece), 0, 1).reshape(self.parts, -1)

    def small(self, token_ids, target_ids, mask, norms):
        found = [lax.all_gather(v.reshape(-1), "dp", tiled=True) for v in (token_ids, target_ids, mask)]
        return found + [lax.all_gather(norms.astype(BF), "dp", axis=1, tiled=True)]

    def embed(self, table_low, local_ids, rows):
        def one(ids):
            looked = jnp.take(table_low, jnp.maximum(ids, 0), axis=0)
            looked = jnp.where(ids[:, None] >= 0, looked, jnp.zeros((), BF))
            return lax.psum_scatter(looked, ("dp", "mp"), tiled=True)

        return lax.map(one, self.split(local_ids, rows)).reshape(rows, -1)

    def gather_group(self, own):
        return lax.all_gather(own, "mp", tiled=True)

    def sum_group(self, parts):
        return lax.psum_scatter(parts, "mp", tiled=True)

    def head(self, hidden, table_low, targets, weights, vocab_size):
        rows, width = hidden.shape
        shard = table_low.shape[0]

        def one(carried, packed):
            own, ids, weight = packed
            table_grad, loss_part = carried
            hidden_all = lax.all_gather(own, ("dp", "mp"), tiled=True)
            logits = contract_cols(hidden_all, table_low)
            top = lax.pmax(jnp.max(logits, axis=1), ("dp", "mp"))
            onehot = jnp.arange(shard)[None, :] == ids[:, None]
            picked = jnp.sum(logits * jnp.where(onehot, 1.0 - smoothing + even, even), axis=1)
            total = lax.psum(jnp.sum(jnp.exp(logits - top[:, None]), axis=1), ("dp", "mp"))
            total = top + jnp.log(total)
            grads = jnp.exp(logits - total[:, None]) - jnp.where(onehot, 1.0 - smoothing, 0.0)
            grads = ((grads - even) * weight[:, None]).astype(BF)
            partial = dot_nn(grads, table_low).astype(BF)
            grad_hidden = lax.psum_scatter(partial, ("dp", "mp"), tiled=True).astype(F32)
            table_grad = table_grad + contract_rows(grads, hidden_all)
            return (table_grad, loss_part + jnp.sum((total / devices - picked) * weight)), grad_hidden

        even = smoothing / vocab_size
        devices = lax.axis_size("dp") * lax.axis_size("mp")
        first = (jnp.zeros((shard, width), F32), jnp.zeros((), F32))
        own = hidden.reshape(self.parts, rows // self.parts, width)
        (table_grad, loss_part), grad_hidden = lax.scan(
            one, first, (own, self.split(targets, rows), self.split(weights, rows))
        )
        return grad_hidden.reshape(rows, width), table_grad, loss_part

    def scatter(self, grad_start, norms_grad, local_ids, table_grad, span):
        shard = table_grad.shape[0]
        rows, width = grad_start.shape

        def one(carried, packed):
            own, ids = packed
            everything = lax.all_gather(own, ("dp", "mp"), tiled=True).astype(F32)
            safe = jnp.where(ids >= 0, ids, shard)
            return carried + jax.ops.segment_sum(everything, safe, num_segments=shard), None

        own = grad_start.astype(BF).reshape(self.parts, rows // self.parts, width)
        table_grad, unused = lax.scan(one, table_grad, (own, self.split(local_ids, rows)))
        spread = jnp.zeros((lax.axis_size("mp") * rows, width), F32)
        spread = lax.dynamic_update_slice(spread, grad_start, (lax.axis_index("mp") * rows, 0))
        positions_grad = lax.psum(lax.psum_scatter(spread, "dp", tiled=True), "mp")
        norms_part = lax.psum(
            lax.psum_scatter(norms_grad, "dp", scatter_dimension=1, tiled=True), "mp"
        )
        return table_grad, positions_grad, norms_part, jnp.sum(table_grad * table_grad)

    def total(self, scalars):
        return list(lax.psum(tuple(scalars), ("dp", "mp")))


def attend_scores(queries, keys, length):
    scores = jnp.einsum("qhe,khe->hqk", queries, keys, preferred_element_type=F32) * HD ** (-0.5)
    place_at = jnp.arange(queries.shape[0])
    allowed = (place_at[None, :] <= place_at[:, None]) & (place_at[None, :] < length)
    return jnp.where(allowed[None], scores, -1e30)


def attend_forward(queries, keys, values, length):
    scores = attend_scores(queries, keys, length)
    top = jnp.max(scores, axis=-1, keepdims=True)
    log_total = jnp.log(jnp.sum(jnp.exp(scores - top), axis=-1, keepdims=True)) + top
    probs = jnp.exp(scores - log_total).astype(BF)
    attended = jnp.einsum("hqk,khe->qhe", probs, values, preferred_element_type=F32)
    return attended.astype(BF), log_total


def attend_backward(queries, keys, values, length, log_total, grad):
    probs = jnp.exp(attend_scores(queries, keys, length) - log_total)
    grad_values = jnp.einsum("hqk,qhe->khe", probs.astype(BF), grad, preferred_element_type=F32)
    grad_probs = jnp.einsum("qhe,khe->hqk", grad, values, preferred_element_type=F32)
    inner = jnp.sum(grad_probs * probs, axis=-1, keepdims=True)
    grad_scores = (probs * (grad_probs - inner)).astype(BF)
    scale = HD ** (-0.5)
    grad_queries = jnp.einsum("hqk,khe->qhe", grad_scores, keys, preferred_element_type=F32) * scale
    grad_keys = jnp.einsum("hqk,qhe->khe", grad_scores, queries, preferred_element_type=F32) * scale
    return grad_queries.astype(BF), grad_keys.astype(BF), grad_values.astype(BF)


def local(
    moves,
    token_ids,
    target_ids,
    loss_mask,
    lengths,
    step_count,
    *weights,
):
    masters, firsts, seconds = weights[:7], weights[7:14], weights[14:]
    table, positions, attn_in, attn_out, mlp_in, mlp_out, norms = masters
    shard = table.shape[0]
    width = table.shape[1]
    dp, mp = lax.axis_index("dp"), lax.axis_index("mp")
    dp_count, mp_count = lax.axis_size("dp"), lax.axis_size("mp")
    vocab_size = shard * dp_count * mp_count
    seq_len = token_ids.shape[1]
    rows = token_ids.size // mp_count
    table_low = table.astype(BF)
    ids_all, targets_all, mask_all, norms_all = moves.small(token_ids, target_ids, loss_mask, norms)
    gains = norms_all.astype(F32)
    mask_all = mask_all.astype(F32)
    token_total = jnp.sum(mask_all)
    row_weights = mask_all / token_total
    base = (dp * mp_count + mp) * shard

    def local_of(ids):
        inside = (ids >= base) & (ids < base + shard)
        return jnp.where(inside, ids - base, -1)

    local_ids, local_targets = local_of(ids_all), local_of(targets_all)
    attn_pack = jnp.concatenate([attn_in, attn_out[None]], axis=0).astype(BF)
    mlp_pack = jnp.stack([mlp_in, mlp_out]).astype(BF)
    positions_all = lax.all_gather(positions.astype(BF), "dp", axis=0, tiled=True)
    attn_all = lax.all_gather(attn_pack, "dp", axis=1, tiled=True)
    mlp_all = lax.all_gather(mlp_pack, "dp", axis=1, tiled=True)

    embedded = moves.embed(table_low, local_ids, rows)
    first_row = (mp * rows) % seq_len
    own_positions = lax.dynamic_slice(positions_all, (first_row, 0), (rows, width))
    start_rows = embedded.astype(F32) + own_positions.astype(F32)
    normed_one = moves.gather_group(layer_norm(start_rows, gains[0], gains[1]).astype(BF))
    head_shape = (seq_len, attn_all.shape[2] // HD, HD)
    queries, keys, values = (dot_nn(normed_one, attn_all[i]).astype(BF) for i in range(3))
    heads = [v.reshape(head_shape) for v in (queries, keys, values)]
    attended, log_total = attend_forward(*heads, lengths[0])
    attended = attended.reshape(seq_len, -1)
    middle = start_rows + moves.sum_group(contract_cols(attended, attn_all[3]))
    normed_two = moves.gather_group(layer_norm(middle, gains[2], gains[3]).astype(BF))
    pre_gelu = dot_nn(normed_two, mlp_all[0])
    activated = gelu_tanh(pre_gelu).astype(BF)
    last_rows = middle + moves.sum_group(contract_cols(activated, mlp_all[1]))
    hidden = layer_norm(last_rows, gains[4], gains[5]).astype(BF)

    grad_hidden, table_grad, loss_part = moves.head(
        hidden, table_low, local_targets, row_weights, vocab_size
    )
    unused, norm_three_back = jax.vjp(layer_norm, last_rows, gains[4], gains[5])
    grad_last, gain_three, shift_three = norm_three_back(grad_hidden)
    grad_last_low = moves.gather_group(grad_last.astype(BF))
    mlp_out_grad = contract_rows(grad_last_low, activated)
    grad_activated = dot_nn(grad_last_low, mlp_all[1])
    unused, gelu_back = jax.vjp(gelu_tanh, pre_gelu)
    grad_pre = gelu_back(grad_activated)[0].astype(BF)
    mlp_in_grad = contract_rows(normed_two, grad_pre)
    grad_normed_two = moves.sum_group(contract_cols(grad_pre, mlp_all[0]))
    mlp_share = lax.psum_scatter(
        jnp.stack([mlp_in_grad, mlp_out_grad]).astype(BF), "dp", scatter_dimension=1, tiled=True
    ).astype(F32)
    unused, norm_two_back = jax.vjp(layer_norm, middle, gains[2], gains[3])
    grad_from_two, gain_two, shift_two = norm_two_back(grad_normed_two)
    grad_middle = grad_last + grad_from_two
    grad_middle_low = moves.gather_group(grad_middle.astype(BF))
    attn_out_grad = contract_rows(grad_middle_low, attended)
    grad_attended = dot_nn(grad_middle_low, attn_all[3]).astype(BF).reshape(head_shape)
    members = [
        v.reshape(seq_len, -1)
        for v in attend_backward(*heads, lengths[0], log_total, grad_attended)
    ]
    attn_grads = [contract_rows(normed_one, v) for v in members] + [attn_out_grad]
    grad_normed_one = moves.sum_group(
        sum(contract_cols(members[i], attn_all[i]) for i in range(3))
    )
    attn_share = lax.psum_scatter(
        jnp.stack(attn_grads).astype(BF), "dp", scatter_dimension=1, tiled=True
    ).astype(F32)
    unused, norm_one_back = jax.vjp(layer_norm, start_rows, gains[0], gains[1])
    grad_from_one, gain_one, shift_one = norm_one_back(grad_normed_one)
    grad_start = grad_middle + grad_from_one
    norms_grad = jnp.stack([gain_one, shift_one, gain_two, shift_two, gain_three, shift_three])
    table_grad, positions_grad, norms_part, table_square = moves.scatter(
        grad_start, norms_grad, local_ids, table_grad, positions.shape[0]
    )
    shares = (
        table_grad,
        positions_grad,
        attn_share[:3],
        attn_share[3],
        mlp_share[0],
        mlp_share[1],
        norms_part,
    )
    copies = (1.0, mp_count, 1.0, 1.0, 1.0, 1.0, mp_count)
    squares = sum((jnp.sum(v * v) / n for v, n in zip(shares[1:], copies[1:])), table_square)
    total_square, loss = moves.total([squares, loss_part])
    grad_norm = jnp.sqrt(total_square)
    factor = jnp.minimum(1.0, clip_norm / (grad_norm + 1e-06))
    step_float = step_count[0].astype(F32)
    updated = [
        adam_update(
            masters[i],
            firsts[i],
            seconds[i],
            factor * shares[i],
            learn_rates[i],
            decay_rates[i],
            step_float,
        )
        for i in range(7)
    ]
    return (loss, grad_norm) + tuple(updated[i][part] for part in range(3) for i in range(7))


def fits_kernels(mesh):
    if mesh.shape["mp"] != 4 or mesh.shape["dp"] != 8:
        return False
    for (dp, mp), item in zip(
        ((i, j) for i in range(8) for j in range(4)), mesh.devices.reshape(-1)
    ):
        coords = getattr(item, "coords", None)
        if coords is not None and (tuple(coords), item.core_on_chip) != (
            (dp % 2, mp // 2, dp // 2),
            mp % 2,
        ):
            return False
    return True


def solution(mesh):
    table, rows, heads, grid, norms = (
        P(("dp", "mp"), None),
        P("dp", None),
        P(None, "dp", "mp"),
        P("dp", "mp"),
        P(None, "dp"),
    )
    each = (table, rows, heads, grid, grid, grid, norms)
    in_specs = (rows, rows, rows, P("dp"), P()) + each * 3
    out_specs = (P(), P()) + each * 3
    moves = KernelMoves(mesh.shape["dp"] // 2) if fits_kernels(mesh) else PlainMoves()
    return jax.shard_map(
        functools.partial(local, moves),
        mesh=mesh,
        in_specs=in_specs,
        out_specs=out_specs,
        check_vma=False,
    )
```

```python
import functools

import jax
import jax.numpy as jnp
from jax import lax
from jax.experimental import pallas as pl
from jax.experimental.pallas import tpu as pltpu
from jax.sharding import PartitionSpec as P

HD = 64
VOCAB = 50688
MESH = pl.DeviceIdType.MESH
ANY = pl.ANY
VMEM = pltpu.VMEM
BF = jnp.bfloat16
F32 = jnp.float32

smoothing = 0.1
clip_norm = 0.01
beta_one = 0.9
beta_two = 0.999
adam_eps = 1e-08
learn_rates = (0.06, 0.06, 0.03, 0.03, 0.03, 0.004, 0.3)
decay_rates = (0.1, 0.0, 0.1, 0.1, 0.1, 0.1, 0.0)


def layer_norm(values, gain_row, shift_row):
    centered = values - jnp.mean(values, axis=-1, keepdims=True)
    spread = jnp.mean(centered * centered, axis=-1, keepdims=True)
    return centered * lax.rsqrt(spread + 1e-05) * gain_row + shift_row


def gelu_tanh(values):
    return jax.nn.gelu(values, approximate=True)


def adam_update(weight, first_moment, second, grad_item, rate, decay, step_float):
    first_new = beta_one * first_moment + (1.0 - beta_one) * grad_item
    second_new = beta_two * second + (1.0 - beta_two) * grad_item * grad_item
    first_hat = first_new / (1.0 - beta_one**step_float)
    second_hat = second_new / (1.0 - beta_two**step_float)
    weight_new = weight - rate * (first_hat / (jnp.sqrt(second_hat) + adam_eps) + decay * weight)
    return (weight_new, first_new, second_new)


def contract_rows(left, right):
    return lax.dot_general(
        left, right, (((0,), (0,)), ((), ())), preferred_element_type=F32
    )


def contract_cols(left, right):
    return lax.dot_general(
        left, right, (((1,), (1,)), ((), ())), preferred_element_type=F32
    )


def dot_nn(left, right):
    return lax.dot_general(
        left, right, (((1,), (0,)), ((), ())), preferred_element_type=F32
    )


def place():
    dp = lax.axis_index("dp")
    mp = lax.axis_index("mp")
    return dp // 2, dp % 2, mp // 2, mp % 2


def device(z, x, y, c):
    return (z * 2 + x, y * 2 + c)


def flip(bit, by):
    return bit + by - 2 * bit * by


def greet(peers):
    barrier = pltpu.get_barrier_semaphore()
    for peer in peers:
        pl.semaphore_signal(barrier, inc=1, device_id=peer, device_id_type=MESH)
    pl.semaphore_wait(barrier, len(peers))


def remote(src, dst, send_sem, recv_sem, peer):
    return pltpu.make_async_remote_copy(
        src_ref=src,
        dst_ref=dst,
        send_sem=send_sem,
        recv_sem=recv_sem,
        device_id=peer,
        device_id_type=MESH,
    )


def to_column(row):
    wide = jnp.broadcast_to(row, (128, row.shape[1]))
    return jnp.transpose(wide)[:, :1]


def to_row(column):
    wide = jnp.broadcast_to(column, (column.shape[0], 128))
    return jnp.transpose(wide)[:1, :]


ARRIVALS = (
    "000o 010p 100d 001q 200d 110p 011q 101q 201q 300d 210p 111q 310d 301q 211q 311q",
    "100o 000u 200d 010u 300d 110p 201q 310d 001q 301q 210p 111q 011q 101q 211q 311q",
)
DEPTH = 4
EVENTS = 16


def sent_on(z, source, kind):
    up = ["u"] if z < DEPTH - 1 else []
    down = ["d"] if z > 0 else []
    if source in (1, 2):
        return {"o": up + down + ["p", "q"], "u": up + ["p", "q"], "d": down + ["p", "q"]}.get(
            kind, ["q"] if kind == "p" else []
        )
    return {
        "o": ["p"] + up + down + ["q"],
        "p": up + down + ["q"],
        "u": up + ["q"],
        "d": down + ["q"],
    }.get(kind, [])


@functools.lru_cache
def route_tables():
    mirror = {"u": "d", "d": "u"}
    events = {}
    for z in range(DEPTH):
        rows = []
        for item in ARRIVALS[min(z, DEPTH - 1 - z)].split():
            source, first, second, kind = int(item[0]), int(item[1]), int(item[2]), item[3]
            if z >= 2:
                source, kind = DEPTH - 1 - source, mirror.get(kind, kind)
            rows.append((source, first, second, kind))
        events[z] = rows
    order = ("p", "q", "u", "d")
    slots, firsts, flags = {}, {}, {}
    for z in range(DEPTH):
        count = 0
        turned = ("p", "q", "u", "d") if z < 2 else ("p", "q", "d", "u")
        for n, (source, first, second, kind) in enumerate(events[z]):
            sends = sent_on(z, source, kind)
            firsts[z, n] = count
            flags[z, n] = sum(1 << i for i, k in enumerate(turned) if k in sends)
            for k in turned:
                if k in sends:
                    slots[z, source, first, second, k] = count
                    count += 1
    tables = []
    most = 1 + max(slots.values())
    for z in range(2):
        rows = []
        for n, (source, first, second, kind) in enumerate(events[z]):
            if kind == "o":
                slot, origin = 0, 0
            else:
                at = z - 1 if kind == "u" else z + 1 if kind == "d" else z
                up_first = 1 - first if kind == "p" else first
                up_second = 1 - second if kind == "q" else second
                slot = slots[at, source, up_first, up_second, kind]
                origin = order.index(kind)
            rows.append((source, 2 * first + second, flags[z, n], slot, firsts[z, n], origin))
        tables.append(rows)
    return tables, most


RADIX = 1024


class Route:
    def __init__(self):
        self.z, self.x, self.y, self.c = place()
        tables, self.slots = route_tables()
        kind = flip(self.z % 2, self.z // 2)
        self.mirrored = self.z // 2
        self.packed = []
        for digits in (
            lambda row: row[0] + 4 * row[1] + 16 * row[2] + 256 * row[5],
            lambda row: row[3] + 32 * row[4],
        ):
            low, high = (
                [digits(rows[n]) + RADIX * digits(rows[n + 1]) for n in range(0, EVENTS, 2)]
                for rows in tables
            )
            self.packed.append([a + kind * (b - a) for a, b in zip(low, high)])
        sign = 1 - 2 * self.mirrored
        z, x, y, c = self.z, self.x, self.y, self.c
        self.c_peer = device(z, x, y, 1 - c)
        self.peers = (
            device(z, flip(x, 1 - c), flip(y, c), c),
            device(z, flip(x, c), flip(y, 1 - c), c),
            device(z + sign, x, y, c),
            device(z - sign * kind, x, y, c),
        )

    def greet(self):
        z, x, y, c = self.z, self.x, self.y, self.c
        along = [device((z + k) % DEPTH, x, y, c) for k in range(1, DEPTH)]
        greet(along + [self.peers[0], self.peers[1], self.c_peer])

    def digits(self, which, n):
        pair = n // 2
        bits = (pair % 2, pair // 2 % 2, pair // 4)
        total = 0
        for number, value in enumerate(self.packed[which]):
            chosen = value
            for i, bit in enumerate(bits):
                chosen = chosen * (bit if number >> i & 1 else 1 - bit)
            total = total + chosen
        return total // (1 + (RADIX - 1) * (n % 2)) % RADIX

    def flags(self, n):
        return self.digits(0, n) // 16 % 16

    def origin(self, n):
        return self.digits(0, n) // 256

    def parent_slot(self, n):
        return self.digits(1, n) % 32

    def first_slot(self, n):
        return self.digits(1, n) // 32

    def family(self, n, core):
        digits = self.digits(0, n)
        source = digits % 4
        source = source + self.mirrored * (DEPTH - 1 - 2 * source)
        first, second = digits // 8 % 2, digits // 4 % 2
        by_x = first * (1 - core) + second * core
        by_y = second * (1 - core) + first * core
        return (source * 2 + flip(self.x, by_x)) * 2 + flip(self.y, by_y)

    def sends(self, n, act):
        flags = self.flags(n)
        for i in range(4):

            @pl.when((flags // (1 << i)) % 2 == 1)
            def _():
                act(i)


def gather_scratch():
    return [
        pltpu.SemaphoreType.DMA((1,)),
        pltpu.SemaphoreType.DMA((4 * EVENTS,)),
        pltpu.SemaphoreType.DMA((EVENTS,)),
        pltpu.SemaphoreType.DMA((EVENTS,)),
        pltpu.SemaphoreType.DMA((EVENTS,)),
    ]


def gather_blocks(own_ref, land, scratch, consume):
    lsem, ss, rs, cs, cr = scratch
    route = Route()
    c = route.c
    route.greet()
    own = route.family(0, c) * 2 + c
    local = pltpu.make_async_copy(own_ref, land.at[own], lsem.at[0])
    local.start()
    local.wait()

    def copy(family, i):
        block = land.at[family * 2 + c]
        return remote(block, block, ss.at[i * EVENTS + family], rs.at[family], route.peers[i])

    def c_copy(family, core):
        block = land.at[family * 2 + core]
        return remote(block, block, cs.at[family], cr.at[family], route.c_peer)

    def event(n, carry):
        @pl.when(n < EVENTS)
        def _():
            family = route.family(n, c)

            @pl.when(n >= 1)
            def _():
                copy(family, 0).wait_recv()

            route.sends(n, lambda i: copy(family, i).start())
            c_copy(family, c).start()

        def one(i, inner):
            at = n - i

            @pl.when((at >= 0) & (at < EVENTS))
            def _():
                core = flip(c, i)
                family = route.family(at, core)

                @pl.when(i == 1)
                def _():
                    c_copy(family, core).wait_recv()

                consume(family * 2 + core, 2 * n - 1 + i + (EVENTS - n) // EVENTS - n // EVENTS)

            return inner

        lax.fori_loop(0, 2, one, 0)
        return carry

    lax.fori_loop(0, EVENTS + 1, event, 0)

    def drain(n, carry):
        family = route.family(n, c)
        route.sends(n, lambda i: copy(family, i).wait_send())
        c_copy(family, c).wait_send()
        return carry

    lax.fori_loop(0, EVENTS, drain, 0)


def reduce_scratch(rows, width):
    slots = route_tables()[1]
    return [
        VMEM((2, rows, width), F32),
        VMEM((EVENTS, rows, width), BF),
        VMEM((EVENTS, rows, width), BF),
        VMEM((EVENTS, rows, width), BF),
        VMEM((slots, rows, width), BF),
        pltpu.SemaphoreType.DMA((EVENTS,)),
        pltpu.SemaphoreType.DMA((slots,)),
        pltpu.SemaphoreType.DMA((EVENTS,)),
        pltpu.SemaphoreType.DMA((EVENTS,)),
    ]


def reduce_blocks(out_ref, scratch, produce, start=None):
    own, oth, cbuf, sbuf, rbuf, ss, rs, cs, cr = scratch
    route = Route()
    c = route.c

    def target(k):
        core = flip(c, 1 - k % 2)
        return route.family(EVENTS - 1 - k // 2, core) * 2 + core

    route.greet()
    if start is not None:
        start(target)

    def c_copy(n):
        return remote(oth.at[n], cbuf.at[n], cs.at[n], cr.at[n], route.c_peer)

    def copy(n, slot, i):
        return remote(sbuf.at[n], rbuf.at[slot], ss.at[n], rs.at[slot], route.peers[i])

    def finish(n):
        half = n % 2
        c_copy(n).wait_recv()
        own[half] += cbuf[n].astype(F32)
        flags, base = route.flags(n), route.first_slot(n)

        def arrived(i):
            slot = base
            for lower in range(i):
                slot = slot + (flags // (1 << lower)) % 2
            copy(n, slot, 0).wait_recv()
            own[half] += rbuf[slot].astype(F32)

        route.sends(n, arrived)

        @pl.when(n > 0)
        def _():
            sbuf[n] = own[half].astype(BF)
            for i, back in enumerate((0, 1, 3, 2)):

                @pl.when(route.origin(n) == i)
                def _():
                    copy(n, route.parent_slot(n), back).start()

    def step(m, carry):
        n = EVENTS - 1 - m

        def one(i, inner):
            @pl.when(m < EVENTS)
            def _():
                value = produce(2 * m + i, target(2 * m + i))

                @pl.when(i == 0)
                def _():
                    oth[n] = value.astype(BF)
                    c_copy(n).start()

                @pl.when(i == 1)
                def _():
                    own[n % 2] = value

            @pl.when((i == 0) & (m >= 1))
            def _():
                finish(n + 1)

            return inner

        lax.fori_loop(0, 2, one, 0)
        return carry

    lax.fori_loop(0, EVENTS + 1, step, 0)
    out_ref[...] = own[0].astype(out_ref.dtype)

    def drain(n, carry):
        c_copy(n).wait_send()

        @pl.when(n > 0)
        def _():
            copy(n, 0, 0).wait_send()

        return carry

    lax.fori_loop(0, EVENTS, drain, 0)


def comm_params(number, limit_mib=60):
    return pltpu.CompilerParams(
        collective_id=number, has_side_effects=True, vmem_limit_bytes=limit_mib << 20
    )


def vspec():
    return pl.BlockSpec(memory_space=VMEM)


def aspec():
    return pl.BlockSpec(memory_space=ANY)


def embed_kernel(depth, table_ref, ids_ref, out_ref, *scratch):
    def produce(n, block):
        wanted = to_column(ids_ref[block])
        rows = wanted.shape[0]
        vocab = lax.broadcasted_iota(jnp.int32, (rows, table_ref.shape[0]), 1).astype(F32)
        onehot = (vocab == wanted).astype(F32).astype(BF)
        return dot_nn(onehot, table_ref[...])

    reduce_blocks(out_ref, scratch, produce)


def embed_call(depth, table_low, local_ids):
    blocks, unused, rows = local_ids.shape
    width = table_low.shape[1]
    return pl.pallas_call(
        functools.partial(embed_kernel, depth),
        out_shape=jax.ShapeDtypeStruct((rows, width), BF),
        in_specs=[vspec(), vspec()],
        out_specs=vspec(),
        scratch_shapes=reduce_scratch(rows, width),
        compiler_params=comm_params(1),
        name="embed_exchange",
    )(table_low, local_ids)


def combine_logs(first, second):
    top = jnp.maximum(first, second)
    return top + jnp.log(jnp.exp(first - top) + jnp.exp(second - top))


def logits_kernel(
    depth, vocab_size, hidden_ref, table_ref, targets_ref, all_ref, expo_ref, top_ref, total_ref, picked_ref,
    land, stage, snap, got, out_sem, all_sem, xs, xr, *sems
):
    z, x, y, c = place()
    blocks = land.shape[0]
    even = smoothing / vocab_size

    def out_copy(slot, block):
        return pltpu.make_async_copy(stage.at[slot], expo_ref.at[block], out_sem.at[slot])

    def keep(block):
        return pltpu.make_async_copy(land.at[block], all_ref.at[block], all_sem.at[block])

    def consume(block, number):
        slot = number % 2
        keep(block).start()
        logits = contract_cols(land[block], table_ref[...])
        top = jnp.max(logits, axis=1, keepdims=True)
        expo = jnp.exp(logits - top)
        total = jnp.sum(expo, axis=1, keepdims=True)
        wanted = to_column(targets_ref[block])
        vocab = lax.broadcasted_iota(jnp.int32, logits.shape, 1).astype(F32)
        mixed = logits * jnp.where(vocab == wanted, 1.0 - smoothing + even, even)
        picked = jnp.sum(mixed, axis=1, keepdims=True)
        top_row = to_row(top)
        top_ref[block] = top_row
        picked_ref[block] = to_row(picked)
        total_ref[block] = top_row + jnp.log(to_row(total))

        @pl.when(number >= 2)
        def _():
            out_copy(slot, block).wait()

        stage[slot] = expo.astype(BF)
        out_copy(slot, block).start()

    gather_blocks(hidden_ref, land, sems, consume)
    peers = [device(z, x, y, 1 - c), device(z, x, 1 - y, c), device(z, 1 - x, y, c)]
    for number, peer in enumerate(peers):
        snap[number] = total_ref[...]
        copy = remote(snap.at[number], got.at[number], xs.at[number], xr.at[number], peer)
        copy.start()
        copy.wait()
        total_ref[...] = combine_logs(snap[number], got[number])
    snap[3] = total_ref[...]
    copies = [
        remote(
            snap.at[3], got.at[2 + k], xs.at[2 + k], xr.at[2 + k], device((z + k) % depth, x, y, c)
        )
        for k in range(1, depth)
    ]
    for copy in copies:
        copy.start()
    for k, copy in enumerate(copies):
        copy.wait()
        total_ref[...] = combine_logs(total_ref[...], got[3 + k])
    for slot in range(2):
        out_copy(slot, 0).wait()

    def kept(block, carry):
        keep(block).wait()
        return carry

    lax.fori_loop(0, blocks, kept, 0)


def logits_call(depth, vocab_size, hidden, table_low, targets):
    blocks, unused, rows = targets.shape
    shard, width = table_low.shape
    row_shape = jax.ShapeDtypeStruct((blocks, 1, rows), F32)
    return pl.pallas_call(
        functools.partial(logits_kernel, depth, vocab_size),
        out_shape=(
            jax.ShapeDtypeStruct((blocks, rows, width), BF),
            jax.ShapeDtypeStruct((blocks, rows, shard), BF),
            row_shape,
            row_shape,
            row_shape,
        ),
        in_specs=[vspec(), vspec(), vspec()],
        out_specs=(aspec(), aspec(), vspec(), vspec(), vspec()),
        scratch_shapes=[
            VMEM((blocks, rows, width), BF),
            VMEM((2, rows, shard), BF),
            VMEM((4, blocks, 1, rows), F32),
            VMEM((2 + depth, blocks, 1, rows), F32),
            pltpu.SemaphoreType.DMA((2,)),
            pltpu.SemaphoreType.DMA((blocks,)),
            pltpu.SemaphoreType.DMA((2 + depth,)),
            pltpu.SemaphoreType.DMA((2 + depth,)),
        ]
        + gather_scratch(),
        compiler_params=comm_params(2),
        name="logits_exchange",
    )(hidden, table_low, targets)


def grads_kernel(
    depth, vocab_size, table_ref, targets_ref, weights_ref, top_ref, total_ref, expo_ref, out_ref, grad_ref,
    inbox, outbox, in_sem, out_sem, *scratch
):
    steps = 2 * EVENTS

    def fetch(slot, block):
        return pltpu.make_async_copy(expo_ref.at[block], inbox.at[slot], in_sem.at[slot])

    def store(slot, block):
        return pltpu.make_async_copy(outbox.at[slot], grad_ref.at[block], out_sem.at[slot])

    targets = []

    def start(target):
        targets.append(target)
        fetch(0, target(0)).start()

    def produce(n, block):
        slot = n % 2
        fetch(slot, block).wait()

        @pl.when(n + 1 < steps)
        def _():
            fetch(1 - slot, targets[0](n + 1)).start()

        weight = weights_ref[block]
        scale = to_column(jnp.exp(top_ref[block] - total_ref[block]) * weight)
        wanted = to_column(targets_ref[block])
        weight = to_column(weight)
        vocab = lax.broadcasted_iota(jnp.int32, inbox.shape[1:], 1).astype(F32)
        low = -(smoothing / vocab_size) * weight
        hit = low - (1.0 - smoothing) * weight
        grad = inbox[slot].astype(F32) * scale + jnp.where(vocab == wanted, hit, low)
        grad = grad.astype(BF)

        @pl.when(n >= 2)
        def _():
            store(slot, block).wait()

        outbox[slot] = grad
        store(slot, block).start()
        return dot_nn(grad, table_ref[...])

    reduce_blocks(out_ref, scratch, produce, start)
    for slot in range(2):
        store(slot, 0).wait()


def grads_call(depth, vocab_size, table_low, targets, weights, top, total, expo):
    blocks, rows, shard = expo.shape
    width = table_low.shape[1]
    return pl.pallas_call(
        functools.partial(grads_kernel, depth, vocab_size),
        out_shape=(
            jax.ShapeDtypeStruct((rows, width), F32),
            jax.ShapeDtypeStruct((blocks, rows, shard), BF),
        ),
        in_specs=[vspec(), vspec(), vspec(), vspec(), vspec(), aspec()],
        out_specs=(vspec(), aspec()),
        scratch_shapes=[
            VMEM((2, rows, shard), BF),
            VMEM((2, rows, shard), BF),
            pltpu.SemaphoreType.DMA((2,)),
            pltpu.SemaphoreType.DMA((2,)),
        ]
        + reduce_scratch(rows, width),
        compiler_params=comm_params(3),
        name="grads_exchange",
    )(table_low, targets, weights, top, total, expo)


def scatter_kernel(
    depth, rows, sent_ref, ids_ref, grads_ref, hidden_ref, out_ref, pos_ref, rest_ref, square_ref,
    left, right, left_sem, right_sem, land, *scratch
):
    out_ref[...] = jnp.zeros(out_ref.shape, F32)
    shard = out_ref.shape[0]

    def fetch(slot, block):
        top = pl.ds(0, rows)
        return (
            pltpu.make_async_copy(grads_ref.at[block], left.at[slot, top, :], left_sem.at[slot]),
            pltpu.make_async_copy(hidden_ref.at[block], right.at[slot, top, :], right_sem.at[slot]),
        )

    for copy in fetch(0, 0):
        copy.start()

    def consume(block, number):
        slot = number % 2
        for copy in fetch(slot, number):
            copy.wait()

        @pl.when(number + 1 < land.shape[0])
        def _():
            for copy in fetch(1 - slot, number + 1):
                copy.start()

        vocab = lax.broadcasted_iota(jnp.int32, (rows, shard), 1).astype(F32)
        onehot = (vocab == to_column(ids_ref[block])).astype(F32).astype(BF)
        left[slot, rows:, :] = onehot
        right[slot, rows:, :] = land[block, :rows, :]
        out_ref[...] += contract_rows(left[slot], right[slot])

    gather_blocks(sent_ref, land, scratch, consume)
    dp = lax.axis_index("dp")
    slots = 2 * depth
    span = pos_ref.shape[0]
    per = rows // span
    total = jnp.zeros(pos_ref.shape, F32)
    rest = jnp.zeros(rest_ref.shape, F32)
    first = pl.multiple_of((dp % per) * span, span)
    for slot in range(slots):
        total = total + land[slot * 4 + dp // per, pl.ds(first, span), :].astype(F32)
    pos_ref[...] = total
    for block in range(land.shape[0]):
        rest = rest + land[block, rows:, :].astype(F32)
    rest_ref[...] = rest
    square_ref[...] = jnp.zeros(square_ref.shape, F32) + jnp.sum(out_ref[...] * out_ref[...])


def scatter_call(depth, sent, ids, grads, hidden_all, span):
    blocks, unused, rows = ids.shape
    extended, width = sent.shape
    shard = grads.shape[2]
    return pl.pallas_call(
        functools.partial(scatter_kernel, depth, rows),
        out_shape=(
            jax.ShapeDtypeStruct((shard, width), F32),
            jax.ShapeDtypeStruct((span, width), F32),
            jax.ShapeDtypeStruct((extended - rows, width), F32),
            jax.ShapeDtypeStruct((8, 128), F32),
        ),
        in_specs=[vspec(), vspec(), aspec(), aspec()],
        out_specs=(vspec(),) * 4,
        scratch_shapes=[
            VMEM((2, 2 * rows, shard), BF),
            VMEM((2, 2 * rows, width), BF),
            pltpu.SemaphoreType.DMA((2,)),
            pltpu.SemaphoreType.DMA((2,)),
            VMEM((blocks, extended, width), BF),
        ]
        + gather_scratch(),
        compiler_params=comm_params(4),
        name="rows_exchange",
    )(sent, ids, grads, hidden_all)


class Group:
    def __init__(self, send_sem, recv_sem, sums=()):
        self.z, self.x, self.y, self.c = place()
        self.y_peer = device(self.z, self.x, 1 - self.y, self.c)
        self.c_peer = device(self.z, self.x, self.y, 1 - self.c)
        self.sems = send_sem, recv_sem
        self.used = 0
        self.sums = sums
        self.me = self.y * 2 + self.c

    def copy(self, src, dst, peer):
        number = self.used
        self.used += 1
        return remote(src, dst, self.sems[0].at[number], self.sems[1].at[number], peer)

    def pair(self, across, first, consume):
        row = flip(self.y, across)

        def one(m, carry):
            i = flip(m, first)
            consume(row * 2 + flip(self.c, i), i)
            return carry

        lax.fori_loop(0, 2, one, 0)

    def gather(self, land, consume, between=None):
        own, there = land.at[self.me], land.at[(1 - self.y) * 2 + self.c]
        to_y, to_c = self.copy(own, own, self.y_peer), self.copy(own, own, self.c_peer)
        on = self.copy(there, there, self.c_peer)
        to_y.start()
        to_c.start()

        def near(block, i):
            @pl.when(i == 1)
            def _():
                to_c.wait_recv()

            consume(block, i, 0)

        def far(block, i):
            @pl.when(i == 1)
            def _():
                on.wait_recv()

            consume(block, i, 1)

        self.pair(0, 0, near)
        to_y.wait_recv()
        on.start()
        self.pair(1, 0, far)
        for copy in (to_y, to_c, on):
            copy.wait_send()


class GroupSum:
    def __init__(self, group, number):
        self.group = group
        keep, mine, theirs, mixed, arrived = group.sums
        self.keep = [keep.at[0], keep.at[1]]
        self.mine = [mine.at[number, 0], mine.at[number, 1]]
        self.theirs = [theirs.at[number, 0], theirs.at[number, 1]]
        self.mixed, self.arrived = mixed.at[number], arrived.at[number]
        self.to_core = [group.copy(self.mine[i], self.theirs[i], group.c_peer) for i in range(2)]
        self.to_across = group.copy(self.mixed, self.arrived, group.y_peer)

    def add(self, part, i, side):
        @pl.when(i == 0)
        def _():
            self.keep[side][...] = part

        @pl.when(i == 1)
        def _():
            self.mine[side][...] = part.astype(BF)
            self.to_core[side].start()

    def pass_on(self):
        self.to_core[1].wait_recv()
        self.mixed[...] = (self.keep[1][...] + self.theirs[1][...].astype(F32)).astype(BF)
        self.to_across.start()

    def finish(self):
        self.to_core[0].wait_recv()
        total = self.keep[0][...] + self.theirs[0][...].astype(F32)
        self.to_across.wait_recv()
        total = total + self.arrived[...].astype(F32)
        for copy in self.to_core + [self.to_across]:
            copy.wait_send()
        return total


def group_scratch(rows, width):
    return [
        VMEM((2, rows, width), F32),
        VMEM((2, 2, rows, width), BF),
        VMEM((2, 2, rows, width), BF),
        VMEM((2, rows, width), BF),
        VMEM((2, rows, width), BF),
        pltpu.SemaphoreType.DMA((12,)),
        pltpu.SemaphoreType.DMA((12,)),
    ]


def flat(values):
    return values.reshape(-1, values.shape[-1])


def head_mask(head, columns, value):
    lane = lax.broadcasted_iota(jnp.int32, (1, columns), 1)
    return jnp.where(lane // HD == head, value, 0.0).astype(BF)


def score_bias(block, length_row, seq_len):
    shape = (seq_len, length_row.shape[1])
    key = lax.broadcasted_iota(jnp.int32, shape, 0)
    query = lax.broadcasted_iota(jnp.int32, shape, 1) + block * length_row.shape[1]
    allowed = (key <= query) & (key.astype(F32) < length_row)
    return jnp.where(allowed, 0.0, -1e30)


def columns_of(values, heads):
    return jnp.transpose(values.astype(F32)).astype(BF).reshape(heads, HD, -1)


def forward_kernel(
    start_ref, gains_ref, length_ref, weights_hbm,
    normed_one_hbm, members_hbm, attended_hbm, logs_ref, middle_ref, normed_two_hbm, pre_hbm, act_hbm,
    last_ref, hidden_ref,
    weights, normed_one, members, value_cols, attended, att_cols, bias, normed_two, pre, act,
    load_sem, store_sem, *scratch
):
    group = Group(scratch[5], scratch[6], scratch[:5])
    loads = [pltpu.make_async_copy(weights_hbm.at[i], weights.at[i], load_sem.at[i]) for i in range(3)]
    for i in (2, 0, 1):
        loads[i].start()
    normed_one[group.me] = layer_norm(start_ref[...], gains_ref[0:1], gains_ref[1:2]).astype(BF)
    greet([group.y_peer, group.c_peer])
    blocks, rows, unused = normed_one.shape
    cols = members.shape[3]
    heads = cols // HD
    stores = []

    def store(src, dst):
        stores.append(pltpu.make_async_copy(src, dst, store_sem.at[len(stores)]))
        stores[-1].start()

    def project(block, i, side):
        out = dot_nn(normed_one[block], weights[2, :, : 3 * cols])
        for m in range(3):
            members[m, block] = out[:, m * cols : (m + 1) * cols].astype(BF)

    loads[2].wait()
    group.gather(normed_one, project)
    store(normed_one, normed_one_hbm)
    store(members, members_hbm)
    value_cols[...] = columns_of(flat(members[2]), heads)
    sums = GroupSum(group, 0)

    def attend(block, i, side):
        bias[...] = score_bias(block, length_ref[...], blocks * rows)

        def head(h, carry):
            queries = members[0, block] * head_mask(h, cols, HD ** (-0.5))
            scores = contract_cols(flat(members[1]), queries) + bias[...]
            top = jnp.max(scores, axis=0, keepdims=True)
            expo = jnp.exp(scores - top)
            total = jnp.sum(expo, axis=0, keepdims=True)
            probs = (expo * (1.0 / total)).astype(BF)
            att_cols[h] = dot_nn(value_cols[h], probs)
            logs_ref[h, block] = top + jnp.log(total)
            return carry

        lax.fori_loop(0, heads, head, 0)
        rows_out = jnp.transpose(flat(att_cols[...])).astype(BF)
        attended[block] = rows_out
        sums.add(contract_cols(rows_out, weights[2, :, 3 * cols :]), i, side)

    group.pair(1, 1, lambda block, i: attend(block, i, 1))
    sums.pass_on()
    group.pair(0, 1, lambda block, i: attend(block, i, 0))
    store(attended, attended_hbm)
    middle = start_ref[...] + sums.finish()
    middle_ref[...] = middle
    normed_two[group.me] = layer_norm(middle, gains_ref[2:3], gains_ref[3:4]).astype(BF)
    again = GroupSum(group, 1)

    def feed(block, i, side):
        units = dot_nn(normed_two[block], weights[0])
        pre[block] = units
        active = gelu_tanh(units).astype(BF)
        act[block] = active
        again.add(contract_cols(active, weights[1]), i, side)

    loads[0].wait()
    loads[1].wait()
    group.gather(normed_two, feed)
    again.pass_on()
    store(normed_two, normed_two_hbm)
    store(pre, pre_hbm)
    store(act, act_hbm)
    last = middle_ref[...] + again.finish()
    last_ref[...] = last
    hidden_ref[...] = layer_norm(last, gains_ref[4:5], gains_ref[5:6]).astype(BF)
    for copy in stores:
        copy.wait()


def forward_call(start_rows, gains, length, weights):
    rows, width = start_rows.shape
    hidden_units = weights.shape[2]
    cols = hidden_units // 4
    heads = cols // HD
    gathered = (4, rows, width)
    units = (4, rows, hidden_units)

    def shape(dims, kind):
        return jax.ShapeDtypeStruct(dims, kind)

    return pl.pallas_call(
        forward_kernel,
        out_shape=(
            shape(gathered, BF),
            shape((3, 4, rows, cols), BF),
            shape((4, rows, cols), BF),
            shape((heads, 4, 1, rows), F32),
            shape((rows, width), F32),
            shape(gathered, BF),
            shape(units, F32),
            shape(units, BF),
            shape((rows, width), F32),
            shape((rows, width), BF),
        ),
        in_specs=[vspec(), vspec(), vspec(), aspec()],
        out_specs=(
            aspec(), aspec(), aspec(), vspec(), vspec(), aspec(), aspec(), aspec(), vspec(), vspec(),
        ),
        scratch_shapes=[
            VMEM((3, width, hidden_units), BF),
            VMEM(gathered, BF),
            VMEM((3, 4, rows, cols), BF),
            VMEM((heads, HD, 4 * rows), BF),
            VMEM((4, rows, cols), BF),
            VMEM((heads, HD, rows), F32),
            VMEM((4 * rows, rows), F32),
            VMEM(gathered, BF),
            VMEM(units, F32),
            VMEM(units, BF),
            pltpu.SemaphoreType.DMA((3,)),
            pltpu.SemaphoreType.DMA((6,)),
        ]
        + group_scratch(rows, width),
        compiler_params=comm_params(7),
        name="layer_forward",
    )(start_rows, gains, length, weights)


def norm_back(values, gain_row, cotangent):
    centered = values - jnp.mean(values, axis=-1, keepdims=True)
    scale = lax.rsqrt(jnp.mean(centered * centered, axis=-1, keepdims=True) + 1e-05)
    normed = centered * scale
    weighted = cotangent * gain_row
    first = jnp.mean(weighted, axis=-1, keepdims=True)
    second = jnp.mean(weighted * normed, axis=-1, keepdims=True)
    grad = (weighted - first - normed * second) * scale
    gain = jnp.sum(cotangent * normed, axis=0, keepdims=True)
    return grad, gain, jnp.sum(cotangent, axis=0, keepdims=True)


def gelu_slope(values):
    root, cube = 0.7978845608028654, 0.044715
    square = values * values
    bent = jnp.tanh(root * (values + cube * values * square))
    return 0.5 * (1.0 + bent) + 0.5 * values * (1.0 - bent * bent) * root * (1.0 + 3.0 * cube * square)


def backward_kernel(
    grad_ref, start_ref, middle_ref, last_ref, gains_ref, length_ref, logs_ref,
    weights_hbm, normed_one_hbm, members_hbm, attended_hbm, normed_two_hbm, pre_hbm, act_hbm,
    out_ref, norms_ref, weight_grads_hbm,
    weights, normed_one, members, attended, normed_two, pre, act,
    grad_last, grad_low, grad_pre, key_cols, query_cols, bias, key_grad, value_grad, grad_mid, grad_att, member_grads,
    weight_grads, load_sem, store_sem, *scratch
):
    group = Group(scratch[5], scratch[6], scratch[:5])
    sources = (
        (weights_hbm.at[1], weights.at[1]),
        (pre_hbm, pre),
        (weights_hbm.at[0], weights.at[0]),
        (act_hbm, act),
        (normed_two_hbm, normed_two),
        (weights_hbm.at[2], weights.at[2]),
        (members_hbm, members),
        (normed_one_hbm, normed_one),
        (attended_hbm, attended),
    )
    loads = [
        pltpu.make_async_copy(src, dst, load_sem.at[n]) for n, (src, dst) in enumerate(sources)
    ]
    for copy in loads:
        copy.start()
    blocks, rows, width = grad_low.shape
    cols = attended.shape[2]
    heads = cols // HD
    grad, gain, shift = norm_back(last_ref[...], gains_ref[4:5], grad_ref[...])
    grad_last[...] = grad
    norms_ref[4:5] = gain
    norms_ref[5:6] = shift
    grad_low[group.me] = grad.astype(BF)
    greet([group.y_peer, group.c_peer])
    sums = GroupSum(group, 0)

    def feed(block, i, side):
        active = dot_nn(grad_low[block], weights[1])
        low = (active * gelu_slope(pre[block])).astype(BF)
        grad_pre[block] = low
        sums.add(contract_cols(low, weights[0]), i, side)

    for copy in loads[:3]:
        copy.wait()
    group.gather(grad_low, feed)
    sums.pass_on()
    for copy in loads[3:]:
        copy.wait()

    def chunk(ref, j):
        return flat(ref[:, :, pl.ds(pl.multiple_of(j * rows, rows), rows)])

    def place_of(j):
        return pl.ds(pl.multiple_of(j * rows, rows), rows)

    def mlp_grads(j, carry):
        weight_grads[0, place_of(j), :] = contract_rows(chunk(normed_two, j), flat(grad_pre[...])).astype(BF)
        weight_grads[1, place_of(j), :] = contract_rows(chunk(grad_low, j), flat(act[...])).astype(BF)
        return carry

    lax.fori_loop(0, width // rows, mlp_grads, 0)
    grad, gain, shift = norm_back(middle_ref[...], gains_ref[2:3], sums.finish())
    norms_ref[2:3] = gain
    norms_ref[3:4] = shift
    grad = grad + grad_last[...]
    grad_last[...] = grad
    grad_mid[group.me] = grad.astype(BF)
    key_cols[...] = columns_of(flat(members[1]), heads)
    key_grad[...] = jnp.zeros(key_grad.shape, F32)
    value_grad[...] = jnp.zeros(value_grad.shape, F32)

    def attend(block, i, side):
        grad_att[block] = dot_nn(grad_mid[block], weights[2, :, 3 * cols :]).astype(BF)
        bias[...] = score_bias(block, length_ref[...], blocks * rows)

        def head(h, carry):
            queries = members[0, block] * head_mask(h, cols, HD ** (-0.5))
            grads = grad_att[block] * head_mask(h, cols, 1.0)
            scores = contract_cols(flat(members[1]), queries) + bias[...]
            probs = jnp.exp(scores - logs_ref[h, block])
            grad_probs = contract_cols(flat(members[2]), grads)
            inner = jnp.sum(grad_probs * probs, axis=0, keepdims=True)
            grad_scores = (probs * (grad_probs - inner)).astype(BF)
            key_grad[...] += dot_nn(grad_scores, queries)
            value_grad[...] += dot_nn(probs.astype(BF), grads)
            query_cols[h] = dot_nn(key_cols[h], grad_scores)
            return carry

        lax.fori_loop(0, heads, head, 0)
        turned = jnp.transpose(flat(query_cols[...])) * HD ** (-0.5)
        member_grads[block, :, :cols] = turned.astype(BF)

    group.gather(grad_mid, attend)
    split = (blocks, rows, cols)
    member_grads[:, :, cols : 2 * cols] = key_grad[...].astype(BF).reshape(split)
    member_grads[:, :, 2 * cols :] = value_grad[...].astype(BF).reshape(split)
    again = GroupSum(group, 1)

    def back(block, i, side):
        again.add(contract_cols(member_grads[block], weights[2, :, : 3 * cols]), i, side)

    group.pair(1, 1, lambda block, i: back(block, i, 1))
    again.pass_on()
    group.pair(0, 1, lambda block, i: back(block, i, 0))

    def attn_grads(j, carry):
        weight_grads[2, place_of(j), : 3 * cols] = contract_rows(
            chunk(normed_one, j), flat(member_grads[...])
        ).astype(BF)
        weight_grads[2, place_of(j), 3 * cols :] = contract_rows(
            chunk(grad_mid, j), flat(attended[...])
        ).astype(BF)
        return carry

    lax.fori_loop(0, width // rows, attn_grads, 0)
    store = pltpu.make_async_copy(weight_grads, weight_grads_hbm, store_sem.at[0])
    store.start()
    grad, gain, shift = norm_back(start_ref[...], gains_ref[0:1], again.finish())
    norms_ref[0:1] = gain
    norms_ref[1:2] = shift
    out_ref[...] = grad_last[...] + grad
    store.wait()


def backward_call(grad_hidden, start_rows, middle, last_rows, gains, length, logs, weights, kept):
    rows, width = start_rows.shape
    hidden_units = weights.shape[2]
    cols = hidden_units // 4
    heads = cols // HD
    gathered = (4, rows, width)
    units = (4, rows, hidden_units)
    stack = (3, width, hidden_units)
    return pl.pallas_call(
        backward_kernel,
        out_shape=(
            jax.ShapeDtypeStruct((rows, width), F32),
            jax.ShapeDtypeStruct((6, width), F32),
            jax.ShapeDtypeStruct(stack, BF),
        ),
        in_specs=[vspec()] * 7 + [aspec()] * 7,
        out_specs=(vspec(), vspec(), aspec()),
        scratch_shapes=[
            VMEM(stack, BF),
            VMEM(gathered, BF),
            VMEM((3, 4, rows, cols), BF),
            VMEM((4, rows, cols), BF),
            VMEM(gathered, BF),
            VMEM(units, F32),
            VMEM(units, BF),
            VMEM((rows, width), F32),
            VMEM(gathered, BF),
            VMEM(units, BF),
            VMEM((heads, HD, 4 * rows), BF),
            VMEM((heads, HD, rows), F32),
            VMEM((4 * rows, rows), F32),
            VMEM((4 * rows, cols), F32),
            VMEM((4 * rows, cols), F32),
            VMEM(gathered, BF),
            VMEM((4, rows, cols), BF),
            VMEM((4, rows, 3 * cols), BF),
            VMEM(stack, BF),
            pltpu.SemaphoreType.DMA((9,)),
            pltpu.SemaphoreType.DMA((1,)),
        ]
        + group_scratch(rows, width),
        compiler_params=comm_params(8),
        name="layer_backward",
    )(grad_hidden, start_rows, middle, last_rows, gains, length, logs, weights, *kept)


def small_gather_kernel(depth, ints_ref, norms_ref, ints_out, norms_out, ss, rs, ns, nr):
    z, x, y, c = place()
    dp = lax.axis_index("dp")
    mp = lax.axis_index("mp")
    count = 2 * depth
    peers = [((dp + k) % count, mp) for k in range(1, count)]
    greet(peers)
    ints_out[dp] = ints_ref[...]
    norms_out[dp] = norms_ref[...]
    copies = []
    for k, peer in enumerate(peers):
        copies.append(remote(ints_ref, ints_out.at[dp], ss.at[k], rs.at[k], peer))
        copies.append(remote(norms_ref, norms_out.at[dp], ns.at[k], nr.at[k], peer))
    for copy in copies:
        copy.start()
    for copy in copies:
        copy.wait()


def small_gather(depth, ints, norms):
    count = 2 * depth
    return pl.pallas_call(
        functools.partial(small_gather_kernel, depth),
        out_shape=(
            jax.ShapeDtypeStruct((count, *ints.shape), ints.dtype),
            jax.ShapeDtypeStruct((count, *norms.shape), norms.dtype),
        ),
        in_specs=[vspec(), vspec()],
        out_specs=(vspec(), vspec()),
        scratch_shapes=[pltpu.SemaphoreType.DMA((count - 1,))] * 4,
        compiler_params=comm_params(5, 8),
        name="small_gather",
    )(ints, norms)


def scalar_sum_kernel(depth, own_ref, out_ref, snap, got, ss, rs):
    z, x, y, c = place()
    peers = [device(z, x, y, 1 - c), device(z, x, 1 - y, c), device(z, 1 - x, y, c)]
    z_peers = [device((z + k) % depth, x, y, c) for k in range(1, depth)]
    greet(peers + z_peers)
    snap[0] = own_ref[...]
    for number, peer in enumerate(peers):
        copy = remote(snap.at[number], got.at[depth + number], ss.at[number], rs.at[number], peer)
        copy.start()
        copy.wait()
        snap[number + 1] = snap[number] + got[depth + number]
    copies = [
        remote(snap.at[3], got.at[z], ss.at[2 + k], rs.at[2 + k], z_peers[k - 1])
        for k in range(1, depth)
    ]
    for copy in copies:
        copy.start()
    got[z] = snap[3]
    for copy in copies:
        copy.wait()
    total = got[0]
    for k in range(1, depth):
        total = total + got[k]
    out_ref[...] = total


def scalar_sum(depth, values):
    return pl.pallas_call(
        functools.partial(scalar_sum_kernel, depth),
        out_shape=jax.ShapeDtypeStruct(values.shape, F32),
        in_specs=[vspec()],
        out_specs=vspec(),
        scratch_shapes=[
            VMEM((4, *values.shape), F32),
            VMEM((depth + 3, *values.shape), F32),
            pltpu.SemaphoreType.DMA((depth + 2,)),
            pltpu.SemaphoreType.DMA((depth + 2,)),
        ],
        compiler_params=comm_params(6, 8),
        name="scalar_sum",
    )(values)


class KernelMoves:
    def __init__(self, depth):
        self.depth = depth

    def small(self, token_ids, target_ids, mask, norms):
        packed = jnp.concatenate([v.reshape(-1, 128) for v in (token_ids, target_ids, mask)], axis=0)
        each = packed.shape[0] // 3
        low = jnp.pad(norms.astype(BF), ((0, 16 - norms.shape[0]), (0, 0)))
        ints, norms_all = small_gather(self.depth, packed, low)
        norms_all = jnp.transpose(norms_all, (1, 0, 2)).reshape(16, -1)[: norms.shape[0]]
        return [ints[:, i * each : (i + 1) * each].reshape(-1) for i in range(3)] + [norms_all]

    def embed(self, table_low, local_ids, rows):
        return embed_call(self.depth, table_low, local_ids.astype(F32).reshape(-1, 1, rows))

    def weights(self, positions, attn_in, attn_out, mlp_in, mlp_out):
        attn = jnp.concatenate([attn_in[0], attn_in[1], attn_in[2], attn_out], axis=1)
        pack = jnp.stack([mlp_in, mlp_out, attn, positions]).astype(BF)
        gathered = lax.all_gather(pack, "dp", axis=1, tiled=True)
        return gathered[3], gathered

    def forward(self, start_rows, gains, length, weights):
        row = jnp.full((1, start_rows.shape[0]), length.astype(F32))
        normed_one, members, attended, logs, middle, normed_two, pre, act, last_rows, hidden = forward_call(
            start_rows, gains, row, weights
        )
        kept = (normed_one, members, attended, normed_two, pre, act)
        return hidden, (start_rows, middle, last_rows, gains, row, logs, weights, kept)

    def backward(self, grad_hidden, saved):
        grad_start, norms_grad, grads = backward_call(grad_hidden, *saved)
        share = lax.psum_scatter(grads, "dp", scatter_dimension=1, tiled=True).astype(F32)
        cols = share.shape[2] // 4
        attn = jnp.stack([share[2, :, i * cols : (i + 1) * cols] for i in range(4)])
        return grad_start, norms_grad, attn, share[:2]

    def head(self, hidden, table_low, targets, weights, vocab_size):
        rows = hidden.shape[0]
        targets = targets.astype(F32).reshape(-1, 1, rows)
        weights = weights.reshape(-1, 1, rows)
        hidden_all, expo, top, total, picked = logits_call(
            self.depth, vocab_size, hidden, table_low, targets
        )
        grad_hidden, grads = grads_call(
            self.depth, vocab_size, table_low, targets, weights, top, total, expo
        )
        weights = weights.reshape(-1)
        first = (lax.axis_index("dp") * lax.axis_size("mp") + lax.axis_index("mp")) * rows
        own_logs = lax.dynamic_slice(total.reshape(-1), (first,), (rows,))
        log_sum = jnp.sum(own_logs * lax.dynamic_slice(weights, (first,), (rows,)))
        loss_part = log_sum - jnp.sum(picked.reshape(-1) * weights)
        return grad_hidden, (grads, hidden_all), loss_part

    def scatter(self, grad_start, norms_grad, local_ids, table_grad, span):
        rows = grad_start.shape[0]
        count = norms_grad.shape[0]
        rest = jnp.pad(norms_grad, ((0, 16 - count), (0, 0)))
        sent = jnp.concatenate([grad_start, rest], axis=0).astype(BF)
        ids = local_ids.astype(F32).reshape(-1, 1, rows)
        grads, hidden_all = table_grad
        table_grad, positions_grad, rest, square = scatter_call(
            self.depth, sent, ids, grads, hidden_all, span
        )
        dp = lax.axis_index("dp")
        part = rest.shape[1] // lax.axis_size("dp")
        norms_part = lax.dynamic_slice(rest, (0, dp * part), (16, part))[:count]
        return table_grad, positions_grad, norms_part, square[0, 0]

    def total(self, scalars):
        row = jnp.concatenate([jnp.full((1, 128), value, F32) for value in scalars], axis=0)
        row = jnp.pad(row, ((0, 8 - len(scalars)), (0, 0)))
        summed = scalar_sum(self.depth, row)
        return [summed[i, 0] for i in range(len(scalars))]


class PlainMoves:
    parts = 4

    def split(self, values, rows):
        piece = rows // self.parts
        return jnp.swapaxes(values.reshape(-1, self.parts, piece), 0, 1).reshape(self.parts, -1)

    def small(self, token_ids, target_ids, mask, norms):
        found = [lax.all_gather(v.reshape(-1), "dp", tiled=True) for v in (token_ids, target_ids, mask)]
        return found + [lax.all_gather(norms.astype(BF), "dp", axis=1, tiled=True)]

    def embed(self, table_low, local_ids, rows):
        def one(ids):
            looked = jnp.take(table_low, jnp.maximum(ids, 0), axis=0)
            looked = jnp.where(ids[:, None] >= 0, looked, jnp.zeros((), BF))
            return lax.psum_scatter(looked, ("dp", "mp"), tiled=True)

        return lax.map(one, self.split(local_ids, rows)).reshape(rows, -1)

    def gather_group(self, own):
        return lax.all_gather(own, "mp", tiled=True)

    def sum_group(self, parts):
        return lax.psum_scatter(parts, "mp", tiled=True)

    def weights(self, positions, attn_in, attn_out, mlp_in, mlp_out):
        attn_pack = jnp.concatenate([attn_in, attn_out[None]], axis=0).astype(BF)
        mlp_pack = jnp.stack([mlp_in, mlp_out]).astype(BF)
        positions_all = lax.all_gather(positions.astype(BF), "dp", axis=0, tiled=True)
        attn_all = lax.all_gather(attn_pack, "dp", axis=1, tiled=True)
        mlp_all = lax.all_gather(mlp_pack, "dp", axis=1, tiled=True)
        return positions_all, (attn_all, mlp_all)

    def forward(self, start_rows, gains, length, weights):
        attn_all, mlp_all = weights
        normed_one = self.gather_group(layer_norm(start_rows, gains[0], gains[1]).astype(BF))
        seq_len = normed_one.shape[0]
        head_shape = (seq_len, attn_all.shape[2] // HD, HD)
        queries, keys, values = (dot_nn(normed_one, attn_all[i]).astype(BF) for i in range(3))
        heads = [v.reshape(head_shape) for v in (queries, keys, values)]
        attended, log_total = attend_forward(*heads, length)
        attended = attended.reshape(seq_len, -1)
        middle = start_rows + self.sum_group(contract_cols(attended, attn_all[3]))
        normed_two = self.gather_group(layer_norm(middle, gains[2], gains[3]).astype(BF))
        pre_gelu = dot_nn(normed_two, mlp_all[0])
        activated = gelu_tanh(pre_gelu).astype(BF)
        last_rows = middle + self.sum_group(contract_cols(activated, mlp_all[1]))
        hidden = layer_norm(last_rows, gains[4], gains[5]).astype(BF)
        return hidden, (
            start_rows, middle, last_rows, gains, length, weights, normed_one, heads, attended, log_total,
            normed_two, pre_gelu, activated,
        )

    def backward(self, grad_hidden, saved):
        (
            start_rows, middle, last_rows, gains, length, weights, normed_one, heads, attended, log_total,
            normed_two, pre_gelu, activated,
        ) = saved
        attn_all, mlp_all = weights
        grad_last, gain_three, shift_three = norm_back(last_rows, gains[4], grad_hidden)
        grad_last_low = self.gather_group(grad_last.astype(BF))
        mlp_out_grad = contract_rows(grad_last_low, activated)
        grad_activated = dot_nn(grad_last_low, mlp_all[1])
        grad_pre = (grad_activated * gelu_slope(pre_gelu)).astype(BF)
        mlp_in_grad = contract_rows(normed_two, grad_pre)
        grad_normed_two = self.sum_group(contract_cols(grad_pre, mlp_all[0]))
        mlp_share = lax.psum_scatter(
            jnp.stack([mlp_in_grad, mlp_out_grad]).astype(BF), "dp", scatter_dimension=1, tiled=True
        ).astype(F32)
        grad_from_two, gain_two, shift_two = norm_back(middle, gains[2], grad_normed_two)
        grad_middle = grad_last + grad_from_two
        grad_middle_low = self.gather_group(grad_middle.astype(BF))
        attn_out_grad = contract_rows(grad_middle_low, attended)
        grad_attended = dot_nn(grad_middle_low, attn_all[3]).astype(BF).reshape(heads[0].shape)
        members = [
            v.reshape(attended.shape)
            for v in attend_backward(*heads, length, log_total, grad_attended)
        ]
        attn_grads = [contract_rows(normed_one, v) for v in members] + [attn_out_grad]
        grad_normed_one = self.sum_group(
            sum(contract_cols(members[i], attn_all[i]) for i in range(3))
        )
        attn_share = lax.psum_scatter(
            jnp.stack(attn_grads).astype(BF), "dp", scatter_dimension=1, tiled=True
        ).astype(F32)
        grad_from_one, gain_one, shift_one = norm_back(start_rows, gains[0], grad_normed_one)
        rows_of = (gain_one, shift_one, gain_two, shift_two, gain_three, shift_three)
        return grad_middle + grad_from_one, jnp.concatenate(rows_of), attn_share, mlp_share

    def head(self, hidden, table_low, targets, weights, vocab_size):
        rows, width = hidden.shape
        shard = table_low.shape[0]

        def one(carried, packed):
            own, ids, weight = packed
            table_grad, loss_part = carried
            hidden_all = lax.all_gather(own, ("dp", "mp"), tiled=True)
            logits = contract_cols(hidden_all, table_low)
            top = lax.pmax(jnp.max(logits, axis=1), ("dp", "mp"))
            onehot = jnp.arange(shard)[None, :] == ids[:, None]
            picked = jnp.sum(logits * jnp.where(onehot, 1.0 - smoothing + even, even), axis=1)
            total = lax.psum(jnp.sum(jnp.exp(logits - top[:, None]), axis=1), ("dp", "mp"))
            total = top + jnp.log(total)
            grads = jnp.exp(logits - total[:, None]) - jnp.where(onehot, 1.0 - smoothing, 0.0)
            grads = ((grads - even) * weight[:, None]).astype(BF)
            partial = dot_nn(grads, table_low).astype(BF)
            grad_hidden = lax.psum_scatter(partial, ("dp", "mp"), tiled=True).astype(F32)
            table_grad = table_grad + contract_rows(grads, hidden_all)
            return (table_grad, loss_part + jnp.sum((total / devices - picked) * weight)), grad_hidden

        even = smoothing / vocab_size
        devices = lax.axis_size("dp") * lax.axis_size("mp")
        first = (jnp.zeros((shard, width), F32), jnp.zeros((), F32))
        own = hidden.reshape(self.parts, rows // self.parts, width)
        (table_grad, loss_part), grad_hidden = lax.scan(
            one, first, (own, self.split(targets, rows), self.split(weights, rows))
        )
        return grad_hidden.reshape(rows, width), table_grad, loss_part

    def scatter(self, grad_start, norms_grad, local_ids, table_grad, span):
        shard = table_grad.shape[0]
        rows, width = grad_start.shape

        def one(carried, packed):
            own, ids = packed
            everything = lax.all_gather(own, ("dp", "mp"), tiled=True).astype(F32)
            safe = jnp.where(ids >= 0, ids, shard)
            return carried + jax.ops.segment_sum(everything, safe, num_segments=shard), None

        own = grad_start.astype(BF).reshape(self.parts, rows // self.parts, width)
        table_grad, unused = lax.scan(one, table_grad, (own, self.split(local_ids, rows)))
        spread = jnp.zeros((lax.axis_size("mp") * rows, width), F32)
        spread = lax.dynamic_update_slice(spread, grad_start, (lax.axis_index("mp") * rows, 0))
        positions_grad = lax.psum(lax.psum_scatter(spread, "dp", tiled=True), "mp")
        norms_part = lax.psum(
            lax.psum_scatter(norms_grad, "dp", scatter_dimension=1, tiled=True), "mp"
        )
        return table_grad, positions_grad, norms_part, jnp.sum(table_grad * table_grad)

    def total(self, scalars):
        return list(lax.psum(tuple(scalars), ("dp", "mp")))


def attend_scores(queries, keys, length):
    scores = jnp.einsum("qhe,khe->hqk", queries, keys, preferred_element_type=F32) * HD ** (-0.5)
    place_at = jnp.arange(queries.shape[0])
    allowed = (place_at[None, :] <= place_at[:, None]) & (place_at[None, :] < length)
    return jnp.where(allowed[None], scores, -1e30)


def attend_forward(queries, keys, values, length):
    scores = attend_scores(queries, keys, length)
    top = jnp.max(scores, axis=-1, keepdims=True)
    log_total = jnp.log(jnp.sum(jnp.exp(scores - top), axis=-1, keepdims=True)) + top
    probs = jnp.exp(scores - log_total).astype(BF)
    attended = jnp.einsum("hqk,khe->qhe", probs, values, preferred_element_type=F32)
    return attended.astype(BF), log_total


def attend_backward(queries, keys, values, length, log_total, grad):
    probs = jnp.exp(attend_scores(queries, keys, length) - log_total)
    grad_values = jnp.einsum("hqk,qhe->khe", probs.astype(BF), grad, preferred_element_type=F32)
    grad_probs = jnp.einsum("qhe,khe->hqk", grad, values, preferred_element_type=F32)
    inner = jnp.sum(grad_probs * probs, axis=-1, keepdims=True)
    grad_scores = (probs * (grad_probs - inner)).astype(BF)
    scale = HD ** (-0.5)
    grad_queries = jnp.einsum("hqk,khe->qhe", grad_scores, keys, preferred_element_type=F32) * scale
    grad_keys = jnp.einsum("hqk,qhe->khe", grad_scores, queries, preferred_element_type=F32) * scale
    return grad_queries.astype(BF), grad_keys.astype(BF), grad_values.astype(BF)


def local(
    moves,
    token_ids,
    target_ids,
    loss_mask,
    lengths,
    step_count,
    *weights,
):
    masters, firsts, seconds = weights[:7], weights[7:14], weights[14:]
    table, positions, attn_in, attn_out, mlp_in, mlp_out, norms = masters
    shard = table.shape[0]
    width = table.shape[1]
    dp, mp = lax.axis_index("dp"), lax.axis_index("mp")
    dp_count, mp_count = lax.axis_size("dp"), lax.axis_size("mp")
    vocab_size = shard * dp_count * mp_count
    seq_len = token_ids.shape[1]
    rows = token_ids.size // mp_count
    table_low = table.astype(BF)
    ids_all, targets_all, mask_all, norms_all = moves.small(token_ids, target_ids, loss_mask, norms)
    gains = norms_all.astype(F32)
    mask_all = mask_all.astype(F32)
    token_total = jnp.sum(mask_all)
    row_weights = mask_all / token_total
    base = (dp * mp_count + mp) * shard

    def local_of(ids):
        inside = (ids >= base) & (ids < base + shard)
        return jnp.where(inside, ids - base, -1)

    local_ids, local_targets = local_of(ids_all), local_of(targets_all)
    positions_all, layer_weights = moves.weights(positions, attn_in, attn_out, mlp_in, mlp_out)

    embedded = moves.embed(table_low, local_ids, rows)
    first_row = (mp * rows) % seq_len
    own_positions = lax.dynamic_slice(positions_all, (first_row, 0), (rows, width))
    start_rows = embedded.astype(F32) + own_positions.astype(F32)
    hidden, saved = moves.forward(start_rows, gains, lengths[0], layer_weights)

    grad_hidden, table_grad, loss_part = moves.head(
        hidden, table_low, local_targets, row_weights, vocab_size
    )
    grad_start, norms_grad, attn_share, mlp_share = moves.backward(grad_hidden, saved)
    table_grad, positions_grad, norms_part, table_square = moves.scatter(
        grad_start, norms_grad, local_ids, table_grad, positions.shape[0]
    )
    shares = (
        table_grad,
        positions_grad,
        attn_share[:3],
        attn_share[3],
        mlp_share[0],
        mlp_share[1],
        norms_part,
    )
    copies = (1.0, mp_count, 1.0, 1.0, 1.0, 1.0, mp_count)
    squares = sum((jnp.sum(v * v) / n for v, n in zip(shares[1:], copies[1:])), table_square)
    total_square, loss = moves.total([squares, loss_part])
    grad_norm = jnp.sqrt(total_square)
    factor = jnp.minimum(1.0, clip_norm / (grad_norm + 1e-06))
    step_float = step_count[0].astype(F32)
    updated = [
        adam_update(
            masters[i],
            firsts[i],
            seconds[i],
            factor * shares[i],
            learn_rates[i],
            decay_rates[i],
            step_float,
        )
        for i in range(7)
    ]
    return (loss, grad_norm) + tuple(updated[i][part] for part in range(3) for i in range(7))


def fits_kernels(mesh):
    if mesh.shape["mp"] != 4 or mesh.shape["dp"] != 8:
        return False
    for (dp, mp), item in zip(
        ((i, j) for i in range(8) for j in range(4)), mesh.devices.reshape(-1)
    ):
        coords = getattr(item, "coords", None)
        if coords is not None and (tuple(coords), item.core_on_chip) != (
            (dp % 2, mp // 2, dp // 2),
            mp % 2,
        ):
            return False
    return True


def solution(mesh):
    table, rows, heads, grid, norms = (
        P(("dp", "mp"), None),
        P("dp", None),
        P(None, "dp", "mp"),
        P("dp", "mp"),
        P(None, "dp"),
    )
    each = (table, rows, heads, grid, grid, grid, norms)
    in_specs = (rows, rows, rows, P("dp"), P()) + each * 3
    out_specs = (P(), P()) + each * 3
    moves = KernelMoves(mesh.shape["dp"] // 2) if fits_kernels(mesh) else PlainMoves()
    return jax.shard_map(
        functools.partial(local, moves),
        mesh=mesh,
        in_specs=in_specs,
        out_specs=out_specs,
        check_vma=False,
    )
```

```python
import functools

import jax
import jax.numpy as jnp
from jax import lax
from jax.experimental import pallas as pl
from jax.experimental.pallas import tpu as pltpu
from jax.sharding import PartitionSpec as P

HD = 64
VOCAB = 50688
MESH = pl.DeviceIdType.MESH
ANY = pl.ANY
VMEM = pltpu.VMEM
BF = jnp.bfloat16
F32 = jnp.float32

smoothing = 0.1
clip_norm = 0.01
beta_one = 0.9
beta_two = 0.999
adam_eps = 1e-08
learn_rates = (0.06, 0.06, 0.03, 0.03, 0.03, 0.004, 0.3)
decay_rates = (0.1, 0.0, 0.1, 0.1, 0.1, 0.1, 0.0)


def layer_norm(values, gain_row, shift_row):
    centered = values - jnp.mean(values, axis=-1, keepdims=True)
    spread = jnp.mean(centered * centered, axis=-1, keepdims=True)
    return centered * lax.rsqrt(spread + 1e-05) * gain_row + shift_row


def gelu_tanh(values):
    return jax.nn.gelu(values, approximate=True)


def adam_update(weight, first_moment, second, grad_item, rate, decay, step_float):
    first_new = beta_one * first_moment + (1.0 - beta_one) * grad_item
    second_new = beta_two * second + (1.0 - beta_two) * grad_item * grad_item
    first_hat = first_new / (1.0 - beta_one**step_float)
    second_hat = second_new / (1.0 - beta_two**step_float)
    weight_new = weight - rate * (first_hat / (jnp.sqrt(second_hat) + adam_eps) + decay * weight)
    return (weight_new, first_new, second_new)


def contract_rows(left, right):
    return lax.dot_general(
        left, right, (((0,), (0,)), ((), ())), preferred_element_type=F32
    )


def contract_cols(left, right):
    return lax.dot_general(
        left, right, (((1,), (1,)), ((), ())), preferred_element_type=F32
    )


def dot_nn(left, right):
    return lax.dot_general(
        left, right, (((1,), (0,)), ((), ())), preferred_element_type=F32
    )


def place():
    dp = lax.axis_index("dp")
    mp = lax.axis_index("mp")
    return dp // 2, dp % 2, mp // 2, mp % 2


def device(z, x, y, c):
    return (z * 2 + x, y * 2 + c)


def flip(bit, by):
    return bit + by - 2 * bit * by


def greet(peers):
    barrier = pltpu.get_barrier_semaphore()
    for peer in peers:
        pl.semaphore_signal(barrier, inc=1, device_id=peer, device_id_type=MESH)
    pl.semaphore_wait(barrier, len(peers))


def remote(src, dst, send_sem, recv_sem, peer):
    return pltpu.make_async_remote_copy(
        src_ref=src,
        dst_ref=dst,
        send_sem=send_sem,
        recv_sem=recv_sem,
        device_id=peer,
        device_id_type=MESH,
    )


def to_column(row):
    wide = jnp.broadcast_to(row, (128, row.shape[1]))
    return jnp.transpose(wide)[:, :1]


def to_row(column):
    wide = jnp.broadcast_to(column, (column.shape[0], 128))
    return jnp.transpose(wide)[:1, :]


ARRIVALS = (
    "000o 010p 100d 001q 200d 110p 011q 101q 201q 300d 210p 111q 310d 301q 211q 311q",
    "100o 000u 200d 010u 300d 110p 201q 310d 001q 301q 210p 111q 011q 101q 211q 311q",
)
DEPTH = 4
EVENTS = 16


def sent_on(z, source, kind):
    up = ["u"] if z < DEPTH - 1 else []
    down = ["d"] if z > 0 else []
    if source in (1, 2):
        return {"o": up + down + ["p", "q"], "u": up + ["p", "q"], "d": down + ["p", "q"]}.get(
            kind, ["q"] if kind == "p" else []
        )
    return {
        "o": ["p"] + up + down + ["q"],
        "p": up + down + ["q"],
        "u": up + ["q"],
        "d": down + ["q"],
    }.get(kind, [])


@functools.lru_cache
def route_tables():
    mirror = {"u": "d", "d": "u"}
    events = {}
    for z in range(DEPTH):
        rows = []
        for item in ARRIVALS[min(z, DEPTH - 1 - z)].split():
            source, first, second, kind = int(item[0]), int(item[1]), int(item[2]), item[3]
            if z >= 2:
                source, kind = DEPTH - 1 - source, mirror.get(kind, kind)
            rows.append((source, first, second, kind))
        events[z] = rows
    order = ("p", "q", "u", "d")
    slots, firsts, flags = {}, {}, {}
    for z in range(DEPTH):
        count = 0
        turned = ("p", "q", "u", "d") if z < 2 else ("p", "q", "d", "u")
        for n, (source, first, second, kind) in enumerate(events[z]):
            sends = sent_on(z, source, kind)
            firsts[z, n] = count
            flags[z, n] = sum(1 << i for i, k in enumerate(turned) if k in sends)
            for k in turned:
                if k in sends:
                    slots[z, source, first, second, k] = count
                    count += 1
    tables = []
    most = 1 + max(slots.values())
    for z in range(2):
        rows = []
        for n, (source, first, second, kind) in enumerate(events[z]):
            if kind == "o":
                slot, origin = 0, 0
            else:
                at = z - 1 if kind == "u" else z + 1 if kind == "d" else z
                up_first = 1 - first if kind == "p" else first
                up_second = 1 - second if kind == "q" else second
                slot = slots[at, source, up_first, up_second, kind]
                origin = order.index(kind)
            rows.append((source, 2 * first + second, flags[z, n], slot, firsts[z, n], origin))
        tables.append(rows)
    return tables, most


RADIX = 1024


class Route:
    def __init__(self):
        self.z, self.x, self.y, self.c = place()
        tables, self.slots = route_tables()
        kind = flip(self.z % 2, self.z // 2)
        self.mirrored = self.z // 2
        self.packed = []
        for digits in (
            lambda row: row[0] + 4 * row[1] + 16 * row[2] + 256 * row[5],
            lambda row: row[3] + 32 * row[4],
        ):
            low, high = (
                [digits(rows[n]) + RADIX * digits(rows[n + 1]) for n in range(0, EVENTS, 2)]
                for rows in tables
            )
            self.packed.append([a + kind * (b - a) for a, b in zip(low, high)])
        sign = 1 - 2 * self.mirrored
        z, x, y, c = self.z, self.x, self.y, self.c
        self.c_peer = device(z, x, y, 1 - c)
        self.peers = (
            device(z, flip(x, 1 - c), flip(y, c), c),
            device(z, flip(x, c), flip(y, 1 - c), c),
            device(z + sign, x, y, c),
            device(z - sign * kind, x, y, c),
        )

    def greet(self, others=()):
        z, x, y, c = self.z, self.x, self.y, self.c
        along = [device((z + k) % DEPTH, x, y, c) for k in range(1, DEPTH)]
        greet(along + [self.peers[0], self.peers[1], self.c_peer] + list(others))

    def digits(self, which, n):
        pair = n // 2
        bits = (pair % 2, pair // 2 % 2, pair // 4)
        total = 0
        for number, value in enumerate(self.packed[which]):
            chosen = value
            for i, bit in enumerate(bits):
                chosen = chosen * (bit if number >> i & 1 else 1 - bit)
            total = total + chosen
        return total // (1 + (RADIX - 1) * (n % 2)) % RADIX

    def flags(self, n):
        return self.digits(0, n) // 16 % 16

    def origin(self, n):
        return self.digits(0, n) // 256

    def parent_slot(self, n):
        return self.digits(1, n) % 32

    def first_slot(self, n):
        return self.digits(1, n) // 32

    def family(self, n, core):
        digits = self.digits(0, n)
        source = digits % 4
        source = source + self.mirrored * (DEPTH - 1 - 2 * source)
        first, second = digits // 8 % 2, digits // 4 % 2
        by_x = first * (1 - core) + second * core
        by_y = second * (1 - core) + first * core
        return (source * 2 + flip(self.x, by_x)) * 2 + flip(self.y, by_y)

    def sends(self, n, act):
        flags = self.flags(n)
        for i in range(4):

            @pl.when((flags // (1 << i)) % 2 == 1)
            def _():
                act(i)


def gather_scratch():
    return [
        pltpu.SemaphoreType.DMA((1,)),
        pltpu.SemaphoreType.DMA((4 * EVENTS,)),
        pltpu.SemaphoreType.DMA((EVENTS,)),
        pltpu.SemaphoreType.DMA((EVENTS,)),
        pltpu.SemaphoreType.DMA((EVENTS,)),
    ]


def gather_blocks(own_ref, land, scratch, consume):
    lsem, ss, rs, cs, cr = scratch
    route = Route()
    c = route.c
    route.greet()
    own = route.family(0, c) * 2 + c
    local = pltpu.make_async_copy(own_ref, land.at[own], lsem.at[0])
    local.start()
    local.wait()

    def copy(family, i):
        block = land.at[family * 2 + c]
        return remote(block, block, ss.at[i * EVENTS + family], rs.at[family], route.peers[i])

    def c_copy(family, core):
        block = land.at[family * 2 + core]
        return remote(block, block, cs.at[family], cr.at[family], route.c_peer)

    def event(n, carry):
        @pl.when(n < EVENTS)
        def _():
            family = route.family(n, c)

            @pl.when(n >= 1)
            def _():
                copy(family, 0).wait_recv()

            route.sends(n, lambda i: copy(family, i).start())
            c_copy(family, c).start()

        def one(i, inner):
            at = n - i

            @pl.when((at >= 0) & (at < EVENTS))
            def _():
                core = flip(c, i)
                family = route.family(at, core)

                @pl.when(i == 1)
                def _():
                    c_copy(family, core).wait_recv()

                consume(family * 2 + core, 2 * n - 1 + i + (EVENTS - n) // EVENTS - n // EVENTS)

            return inner

        lax.fori_loop(0, 2, one, 0)
        return carry

    lax.fori_loop(0, EVENTS + 1, event, 0)

    def drain(n, carry):
        family = route.family(n, c)
        route.sends(n, lambda i: copy(family, i).wait_send())
        c_copy(family, c).wait_send()
        return carry

    lax.fori_loop(0, EVENTS, drain, 0)


def reduce_scratch(rows, width):
    slots = route_tables()[1]
    return [
        VMEM((2, rows, width), F32),
        VMEM((EVENTS, rows, width), BF),
        VMEM((EVENTS, rows, width), BF),
        VMEM((EVENTS, rows, width), BF),
        VMEM((slots, rows, width), BF),
        pltpu.SemaphoreType.DMA((EVENTS,)),
        pltpu.SemaphoreType.DMA((slots,)),
        pltpu.SemaphoreType.DMA((EVENTS,)),
        pltpu.SemaphoreType.DMA((EVENTS,)),
    ]


def reduce_blocks(out_ref, scratch, produce, start=None, others=()):
    own, oth, cbuf, sbuf, rbuf, ss, rs, cs, cr = scratch
    route = Route()
    c = route.c

    def target(k):
        core = flip(c, 1 - k % 2)
        return route.family(EVENTS - 1 - k // 2, core) * 2 + core

    route.greet(others)
    if start is not None:
        start(target)

    def c_copy(n):
        return remote(oth.at[n], cbuf.at[n], cs.at[n], cr.at[n], route.c_peer)

    def copy(n, slot, i):
        return remote(sbuf.at[n], rbuf.at[slot], ss.at[n], rs.at[slot], route.peers[i])

    def finish(n):
        half = n % 2
        c_copy(n).wait_recv()
        own[half] += cbuf[n].astype(F32)
        flags, base = route.flags(n), route.first_slot(n)

        def arrived(i):
            slot = base
            for lower in range(i):
                slot = slot + (flags // (1 << lower)) % 2
            copy(n, slot, 0).wait_recv()
            own[half] += rbuf[slot].astype(F32)

        route.sends(n, arrived)

        @pl.when(n > 0)
        def _():
            sbuf[n] = own[half].astype(BF)
            for i, back in enumerate((0, 1, 3, 2)):

                @pl.when(route.origin(n) == i)
                def _():
                    copy(n, route.parent_slot(n), back).start()

    def step(m, carry):
        n = EVENTS - 1 - m

        def one(i, inner):
            @pl.when(m < EVENTS)
            def _():
                value = produce(2 * m + i, target(2 * m + i))

                @pl.when(i == 0)
                def _():
                    oth[n] = value.astype(BF)
                    c_copy(n).start()

                @pl.when(i == 1)
                def _():
                    own[n % 2] = value

            @pl.when((i == 0) & (m >= 1))
            def _():
                finish(n + 1)

            return inner

        lax.fori_loop(0, 2, one, 0)
        return carry

    lax.fori_loop(0, EVENTS + 1, step, 0)
    out_ref[...] = own[0].astype(out_ref.dtype)

    def drain(n, carry):
        c_copy(n).wait_send()

        @pl.when(n > 0)
        def _():
            copy(n, 0, 0).wait_send()

        return carry

    lax.fori_loop(0, EVENTS, drain, 0)


def comm_params(number, limit_mib=60):
    return pltpu.CompilerParams(
        collective_id=number, has_side_effects=True, vmem_limit_bytes=limit_mib << 20
    )


def vspec():
    return pl.BlockSpec(memory_space=VMEM)


def aspec():
    return pl.BlockSpec(memory_space=ANY)


def embed_kernel(depth, table_ref, ids_ref, positions_ref, out_ref, spots, spot_send, spot_recv, *scratch):
    z, x, y, c = place()
    holds = z == y * 2 + c
    others = [device((z + k // 2) % depth, flip(x, k % 2), y, c) for k in range(1, 2 * depth)]
    copies = [
        remote(positions_ref, spots.at[x], spot_send.at[k], spot_recv.at[x], peer)
        for k, peer in enumerate(others)
    ]

    def start(target):
        @pl.when(holds)
        def _():
            for copy in copies:
                copy.start()
            spots[x] = positions_ref[...]

    def produce(n, block):
        wanted = to_column(ids_ref[block])
        rows = wanted.shape[0]
        vocab = lax.broadcasted_iota(jnp.int32, (rows, table_ref.shape[0]), 1).astype(F32)
        onehot = (vocab == wanted).astype(F32).astype(BF)
        return dot_nn(onehot, table_ref[...])

    reduce_blocks(out_ref, scratch, produce, start, others)

    @pl.when(holds)
    def _():
        for copy in copies:
            copy.wait_send()

    for half in range(2):

        @pl.when(1 - holds.astype(jnp.int32) * (1 - flip(x, half)) == 1)
        def _():
            remote(positions_ref, spots.at[half], spot_send.at[0], spot_recv.at[half], others[0]).wait_recv()

    out_ref[...] += flat(spots[...]).astype(F32)


def embed_call(depth, table_low, local_ids, positions):
    blocks, unused, rows = local_ids.shape
    width = table_low.shape[1]
    return pl.pallas_call(
        functools.partial(embed_kernel, depth),
        out_shape=jax.ShapeDtypeStruct((rows, width), F32),
        in_specs=[vspec(), vspec(), vspec()],
        out_specs=vspec(),
        scratch_shapes=[
            VMEM((2, *positions.shape), BF),
            pltpu.SemaphoreType.DMA((2 * depth - 1,)),
            pltpu.SemaphoreType.DMA((2,)),
        ]
        + reduce_scratch(rows, width),
        compiler_params=comm_params(1),
        name="embed_exchange",
    )(table_low, local_ids, positions)


def combine_logs(first, second):
    top = jnp.maximum(first, second)
    return top + jnp.log(jnp.exp(first - top) + jnp.exp(second - top))


def logits_kernel(
    depth, vocab_size, hidden_ref, table_ref, targets_ref, all_ref, expo_ref, top_ref, total_ref, picked_ref,
    land, stage, snap, got, out_sem, all_sem, xs, xr, *sems
):
    z, x, y, c = place()
    blocks = land.shape[0]
    even = smoothing / vocab_size

    def out_copy(slot, block):
        return pltpu.make_async_copy(stage.at[slot], expo_ref.at[block], out_sem.at[slot])

    def keep(block):
        return pltpu.make_async_copy(land.at[block], all_ref.at[block], all_sem.at[block])

    def consume(block, number):
        slot = number % 2
        keep(block).start()
        logits = contract_cols(land[block], table_ref[...])
        top = jnp.max(logits, axis=1, keepdims=True)
        expo = jnp.exp(logits - top)
        total = jnp.sum(expo, axis=1, keepdims=True)
        wanted = to_column(targets_ref[block])
        vocab = lax.broadcasted_iota(jnp.int32, logits.shape, 1).astype(F32)
        mixed = logits * jnp.where(vocab == wanted, 1.0 - smoothing + even, even)
        picked = jnp.sum(mixed, axis=1, keepdims=True)
        top_row = to_row(top)
        top_ref[block] = top_row
        picked_ref[block] = to_row(picked)
        total_ref[block] = top_row + jnp.log(to_row(total))

        @pl.when(number >= 2)
        def _():
            out_copy(slot, block).wait()

        stage[slot] = expo.astype(BF)
        out_copy(slot, block).start()

    gather_blocks(hidden_ref, land, sems, consume)
    peers = [device(z, x, y, 1 - c), device(z, x, 1 - y, c), device(z, 1 - x, y, c)]
    for number, peer in enumerate(peers):
        snap[number] = total_ref[...]
        copy = remote(snap.at[number], got.at[number], xs.at[number], xr.at[number], peer)
        copy.start()
        copy.wait()
        total_ref[...] = combine_logs(snap[number], got[number])
    snap[3] = total_ref[...]
    copies = [
        remote(
            snap.at[3], got.at[2 + k], xs.at[2 + k], xr.at[2 + k], device((z + k) % depth, x, y, c)
        )
        for k in range(1, depth)
    ]
    for copy in copies:
        copy.start()
    for k, copy in enumerate(copies):
        copy.wait()
        total_ref[...] = combine_logs(total_ref[...], got[3 + k])
    for slot in range(2):
        out_copy(slot, 0).wait()

    def kept(block, carry):
        keep(block).wait()
        return carry

    lax.fori_loop(0, blocks, kept, 0)


def logits_call(depth, vocab_size, hidden, table_low, targets):
    blocks, unused, rows = targets.shape
    shard, width = table_low.shape
    row_shape = jax.ShapeDtypeStruct((blocks, 1, rows), F32)
    return pl.pallas_call(
        functools.partial(logits_kernel, depth, vocab_size),
        out_shape=(
            jax.ShapeDtypeStruct((blocks, rows, width), BF),
            jax.ShapeDtypeStruct((blocks, rows, shard), BF),
            row_shape,
            row_shape,
            row_shape,
        ),
        in_specs=[vspec(), vspec(), vspec()],
        out_specs=(aspec(), aspec(), vspec(), vspec(), vspec()),
        scratch_shapes=[
            VMEM((blocks, rows, width), BF),
            VMEM((2, rows, shard), BF),
            VMEM((4, blocks, 1, rows), F32),
            VMEM((2 + depth, blocks, 1, rows), F32),
            pltpu.SemaphoreType.DMA((2,)),
            pltpu.SemaphoreType.DMA((blocks,)),
            pltpu.SemaphoreType.DMA((2 + depth,)),
            pltpu.SemaphoreType.DMA((2 + depth,)),
        ]
        + gather_scratch(),
        compiler_params=comm_params(2),
        name="logits_exchange",
    )(hidden, table_low, targets)


def grads_kernel(
    depth, vocab_size, table_ref, targets_ref, weights_ref, top_ref, total_ref, expo_ref, out_ref, grad_ref,
    inbox, outbox, in_sem, out_sem, *scratch
):
    steps = 2 * EVENTS

    def fetch(slot, block):
        return pltpu.make_async_copy(expo_ref.at[block], inbox.at[slot], in_sem.at[slot])

    def store(slot, block):
        return pltpu.make_async_copy(outbox.at[slot], grad_ref.at[block], out_sem.at[slot])

    targets = []

    def start(target):
        targets.append(target)
        fetch(0, target(0)).start()

    def produce(n, block):
        slot = n % 2
        fetch(slot, block).wait()

        @pl.when(n + 1 < steps)
        def _():
            fetch(1 - slot, targets[0](n + 1)).start()

        weight = weights_ref[block]
        scale = to_column(jnp.exp(top_ref[block] - total_ref[block]) * weight)
        wanted = to_column(targets_ref[block])
        weight = to_column(weight)
        vocab = lax.broadcasted_iota(jnp.int32, inbox.shape[1:], 1).astype(F32)
        low = -(smoothing / vocab_size) * weight
        hit = low - (1.0 - smoothing) * weight
        grad = inbox[slot].astype(F32) * scale + jnp.where(vocab == wanted, hit, low)
        grad = grad.astype(BF)

        @pl.when(n >= 2)
        def _():
            store(slot, block).wait()

        outbox[slot] = grad
        store(slot, block).start()
        return dot_nn(grad, table_ref[...])

    reduce_blocks(out_ref, scratch, produce, start)
    for slot in range(2):
        store(slot, 0).wait()


def grads_call(depth, vocab_size, table_low, targets, weights, top, total, expo):
    blocks, rows, shard = expo.shape
    width = table_low.shape[1]
    return pl.pallas_call(
        functools.partial(grads_kernel, depth, vocab_size),
        out_shape=(
            jax.ShapeDtypeStruct((rows, width), F32),
            jax.ShapeDtypeStruct((blocks, rows, shard), BF),
        ),
        in_specs=[vspec(), vspec(), vspec(), vspec(), vspec(), aspec()],
        out_specs=(vspec(), aspec()),
        scratch_shapes=[
            VMEM((2, rows, shard), BF),
            VMEM((2, rows, shard), BF),
            pltpu.SemaphoreType.DMA((2,)),
            pltpu.SemaphoreType.DMA((2,)),
        ]
        + reduce_scratch(rows, width),
        compiler_params=comm_params(3),
        name="grads_exchange",
    )(table_low, targets, weights, top, total, expo)


def scatter_kernel(
    depth, rows, sent_ref, ids_ref, grads_ref, hidden_ref, out_ref, pos_ref, rest_ref, square_ref,
    left, right, left_sem, right_sem, land, *scratch
):
    out_ref[...] = jnp.zeros(out_ref.shape, F32)
    shard = out_ref.shape[0]

    def fetch(slot, block):
        top = pl.ds(0, rows)
        return (
            pltpu.make_async_copy(grads_ref.at[block], left.at[slot, top, :], left_sem.at[slot]),
            pltpu.make_async_copy(hidden_ref.at[block], right.at[slot, top, :], right_sem.at[slot]),
        )

    for copy in fetch(0, 0):
        copy.start()

    def consume(block, number):
        slot = number % 2
        for copy in fetch(slot, number):
            copy.wait()

        @pl.when(number + 1 < land.shape[0])
        def _():
            for copy in fetch(1 - slot, number + 1):
                copy.start()

        vocab = lax.broadcasted_iota(jnp.int32, (rows, shard), 1).astype(F32)
        onehot = (vocab == to_column(ids_ref[block])).astype(F32).astype(BF)
        left[slot, rows:, :] = onehot
        right[slot, rows:, :] = land[block, :rows, :]
        out_ref[...] += contract_rows(left[slot], right[slot])

    gather_blocks(sent_ref, land, scratch, consume)
    dp = lax.axis_index("dp")
    slots = 2 * depth
    span = pos_ref.shape[0]
    per = rows // span
    total = jnp.zeros(pos_ref.shape, F32)
    rest = jnp.zeros(rest_ref.shape, F32)
    first = pl.multiple_of((dp % per) * span, span)
    for slot in range(slots):
        total = total + land[slot * 4 + dp // per, pl.ds(first, span), :].astype(F32)
    pos_ref[...] = total
    for block in range(land.shape[0]):
        rest = rest + land[block, rows:, :].astype(F32)
    rest_ref[...] = rest
    square_ref[...] = jnp.zeros(square_ref.shape, F32) + jnp.sum(out_ref[...] * out_ref[...])


def scatter_call(depth, sent, ids, grads, hidden_all, span):
    blocks, unused, rows = ids.shape
    extended, width = sent.shape
    shard = grads.shape[2]
    return pl.pallas_call(
        functools.partial(scatter_kernel, depth, rows),
        out_shape=(
            jax.ShapeDtypeStruct((shard, width), F32),
            jax.ShapeDtypeStruct((span, width), F32),
            jax.ShapeDtypeStruct((extended - rows, width), F32),
            jax.ShapeDtypeStruct((8, 128), F32),
        ),
        in_specs=[vspec(), vspec(), aspec(), aspec()],
        out_specs=(vspec(),) * 4,
        scratch_shapes=[
            VMEM((2, 2 * rows, shard), BF),
            VMEM((2, 2 * rows, width), BF),
            pltpu.SemaphoreType.DMA((2,)),
            pltpu.SemaphoreType.DMA((2,)),
            VMEM((blocks, extended, width), BF),
        ]
        + gather_scratch(),
        compiler_params=comm_params(4),
        name="rows_exchange",
    )(sent, ids, grads, hidden_all)


class Group:
    def __init__(self, send_sem, recv_sem, sums=()):
        self.z, self.x, self.y, self.c = place()
        self.y_peer = device(self.z, self.x, 1 - self.y, self.c)
        self.c_peer = device(self.z, self.x, self.y, 1 - self.c)
        self.sems = send_sem, recv_sem
        self.used = 0
        self.sums = sums
        self.me = self.y * 2 + self.c

    def copy(self, src, dst, peer):
        number = self.used
        self.used += 1
        return remote(src, dst, self.sems[0].at[number], self.sems[1].at[number], peer)

    def pair(self, across, first, consume):
        row = flip(self.y, across)

        def one(m, carry):
            i = flip(m, first)
            consume(row * 2 + flip(self.c, i), i)
            return carry

        lax.fori_loop(0, 2, one, 0)

    def gather(self, land, consume, between=None):
        own, there = land.at[self.me], land.at[(1 - self.y) * 2 + self.c]
        to_y, to_c = self.copy(own, own, self.y_peer), self.copy(own, own, self.c_peer)
        on = self.copy(there, there, self.c_peer)
        to_y.start()
        to_c.start()

        def near(block, i):
            @pl.when(i == 1)
            def _():
                to_c.wait_recv()

            consume(block, i, 0)

        def far(block, i):
            @pl.when(i == 1)
            def _():
                on.wait_recv()

            consume(block, i, 1)

        if between is not None:
            between()
        self.pair(0, 0, near)
        to_y.wait_recv()
        on.start()
        self.pair(1, 0, far)
        for copy in (to_y, to_c, on):
            copy.wait_send()


class LineGather:
    def __init__(self, depth, own_ref, land, z_send, z_recv, x_send, x_recv):
        self.z, self.x, y, c = place()
        self.depth, self.own, self.land = depth, own_ref, land
        self.sems = z_send, z_recv, x_send, x_recv
        self.ways = (device(self.z + 1, self.x, y, c), device(self.z - 1, self.x, y, c))
        self.x_peer = device(self.z, 1 - self.x, y, c)

    def peers(self):
        z, x = self.z, self.x
        along = [device((z + k) % self.depth, x, self.x_peer[1] // 2, self.x_peer[1] % 2) for k in range(1, self.depth)]
        return along + [self.x_peer]

    def block(self, stream, source):
        rows = self.own.shape[1]
        first = pl.multiple_of((source * 2 + self.x) * rows, rows)
        return self.land.at[stream, pl.ds(first, rows), :]

    def along(self, stream, source, way, own=False):
        block = self.block(stream, source)
        number = stream * self.depth + source
        src = self.own.at[stream] if own else block
        z_send, z_recv = self.sems[:2]
        return remote(src, block, z_send.at[number * 2 + way], z_recv.at[number], self.ways[way])

    def across(self, stream, source, own=False):
        block = self.block(stream, source)
        number = stream * self.depth + source
        src = self.own.at[stream] if own else block
        return remote(src, block, self.sems[2].at[number], self.sems[3].at[number], self.x_peer)

    def moves_on(self, way):
        return self.z < self.depth - 1 if way == 0 else self.z > 0

    def start(self):
        for stream in range(2):
            for way in range(2):

                @pl.when(self.moves_on(way))
                def _():
                    self.along(stream, self.z, way, True).start()

            self.across(stream, self.z, True).start()
            rows = self.own.shape[1]
            first = pl.multiple_of((self.z * 2 + self.x) * rows, rows)
            self.land[stream, pl.ds(first, rows), :] = self.own[stream]

    def serve(self, stream, distance):
        for way in range(2):
            source = self.z - distance if way == 0 else self.z + distance

            @pl.when(source >= 0 if way == 0 else source < self.depth)
            def _():
                self.along(stream, source, way).wait_recv()

                @pl.when(self.moves_on(way))
                def _():
                    self.along(stream, source, way).start()

                self.across(stream, source).start()

    def finish(self, stream):
        for source in range(self.depth):
            self.across(stream, source).wait_recv()

    def drain(self):
        for stream in range(2):
            for source in range(self.depth):
                self.across(stream, source).wait_send()

                @pl.when((source <= self.z) & self.moves_on(0))
                def _():
                    self.along(stream, source, 0).wait_send()

                @pl.when((source >= self.z) & self.moves_on(1))
                def _():
                    self.along(stream, source, 1).wait_send()


class GroupSum:
    def __init__(self, group, number):
        self.group = group
        keep, mine, theirs, mixed, arrived = group.sums
        self.keep = [keep.at[0], keep.at[1]]
        self.mine = [mine.at[number, 0], mine.at[number, 1]]
        self.theirs = [theirs.at[number, 0], theirs.at[number, 1]]
        self.mixed, self.arrived = mixed.at[number], arrived.at[number]
        self.to_core = [group.copy(self.mine[i], self.theirs[i], group.c_peer) for i in range(2)]
        self.to_across = group.copy(self.mixed, self.arrived, group.y_peer)

    def add(self, part, i, side):
        @pl.when(i == 0)
        def _():
            self.keep[side][...] = part

        @pl.when(i == 1)
        def _():
            self.mine[side][...] = part.astype(BF)
            self.to_core[side].start()

    def pass_on(self):
        self.to_core[1].wait_recv()
        self.mixed[...] = (self.keep[1][...] + self.theirs[1][...].astype(F32)).astype(BF)
        self.to_across.start()

    def finish(self):
        self.to_core[0].wait_recv()
        total = self.keep[0][...] + self.theirs[0][...].astype(F32)
        self.to_across.wait_recv()
        total = total + self.arrived[...].astype(F32)
        for copy in self.to_core + [self.to_across]:
            copy.wait_send()
        return total


def group_scratch(rows, width):
    return [
        VMEM((2, rows, width), F32),
        VMEM((2, 2, rows, width), BF),
        VMEM((2, 2, rows, width), BF),
        VMEM((2, rows, width), BF),
        VMEM((2, rows, width), BF),
        pltpu.SemaphoreType.DMA((12,)),
        pltpu.SemaphoreType.DMA((12,)),
    ]


def flat(values):
    return values.reshape(-1, values.shape[-1])


def head_mask(head, columns, value):
    lane = lax.broadcasted_iota(jnp.int32, (1, columns), 1)
    return jnp.where(lane // HD == head, value, 0.0).astype(BF)


def score_bias(block, length_row, seq_len):
    shape = (seq_len, length_row.shape[1])
    key = lax.broadcasted_iota(jnp.int32, shape, 0)
    query = lax.broadcasted_iota(jnp.int32, shape, 1) + block * length_row.shape[1]
    allowed = (key <= query) & (key.astype(F32) < length_row)
    return jnp.where(allowed, 0.0, -1e30)


def columns_of(values, heads):
    return jnp.transpose(values.astype(F32)).astype(BF).reshape(heads, HD, -1)


def forward_kernel(
    depth, start_ref, gains_ref, length_ref, own_mlp_ref, attn_hbm,
    mlp_hbm, normed_one_hbm, members_hbm, attended_hbm, logs_ref, middle_ref, normed_two_hbm, pre_hbm, act_hbm,
    last_ref, hidden_ref,
    weights, attn, normed_one, members, value_cols, attended, att_cols, bias, normed_two, pre, act,
    load_sem, store_sem, z_send, z_recv, x_send, x_recv, *scratch
):
    group = Group(scratch[5], scratch[6], scratch[:5])
    line = LineGather(depth, own_mlp_ref, weights, z_send, z_recv, x_send, x_recv)
    load = pltpu.make_async_copy(attn_hbm, attn, load_sem.at[0])
    load.start()
    greet([group.y_peer, group.c_peer] + line.peers())
    line.start()
    normed_one[group.me] = layer_norm(start_ref[...], gains_ref[0:1], gains_ref[1:2]).astype(BF)
    blocks, rows, unused = normed_one.shape
    cols = members.shape[3]
    heads = cols // HD
    stores = []

    def store(src, dst):
        stores.append(pltpu.make_async_copy(src, dst, store_sem.at[len(stores)]))
        stores[-1].start()

    def project(block, i, side):
        out = dot_nn(normed_one[block], attn[:, : 3 * cols])
        for m in range(3):
            members[m, block] = out[:, m * cols : (m + 1) * cols].astype(BF)

    load.wait()
    group.gather(normed_one, project, lambda: line.serve(0, 1))
    line.serve(1, 1)
    store(normed_one, normed_one_hbm)
    store(members, members_hbm)
    value_cols[...] = columns_of(flat(members[2]), heads)
    sums = GroupSum(group, 0)

    def attend(block, i, side):
        bias[...] = score_bias(block, length_ref[...], blocks * rows)

        def head(h, carry):
            queries = members[0, block] * head_mask(h, cols, HD ** (-0.5))
            scores = contract_cols(flat(members[1]), queries) + bias[...]
            top = jnp.max(scores, axis=0, keepdims=True)
            expo = jnp.exp(scores - top)
            total = jnp.sum(expo, axis=0, keepdims=True)
            probs = (expo * (1.0 / total)).astype(BF)
            att_cols[h] = dot_nn(value_cols[h], probs)
            logs_ref[h, block] = top + jnp.log(total)
            return carry

        lax.fori_loop(0, heads, head, 0)
        rows_out = jnp.transpose(flat(att_cols[...])).astype(BF)
        attended[block] = rows_out
        sums.add(contract_cols(rows_out, attn[:, 3 * cols :]), i, side)

    group.pair(1, 1, lambda block, i: attend(block, i, 1))
    sums.pass_on()
    for stream in range(2):
        line.serve(stream, 2)
    group.pair(0, 1, lambda block, i: attend(block, i, 0))
    for stream in range(2):
        line.serve(stream, 3)
    store(attended, attended_hbm)
    middle = start_ref[...] + sums.finish()
    middle_ref[...] = middle
    normed_two[group.me] = layer_norm(middle, gains_ref[2:3], gains_ref[3:4]).astype(BF)
    again = GroupSum(group, 1)

    def feed(block, i, side):
        units = dot_nn(normed_two[block], weights[0])
        pre[block] = units
        active = gelu_tanh(units).astype(BF)
        act[block] = active
        again.add(contract_cols(active, weights[1]), i, side)

    def weights_here():
        for stream in range(2):
            line.finish(stream)
        store(weights, mlp_hbm)

    group.gather(normed_two, feed, weights_here)
    again.pass_on()
    store(normed_two, normed_two_hbm)
    store(pre, pre_hbm)
    store(act, act_hbm)
    last = middle_ref[...] + again.finish()
    last_ref[...] = last
    hidden_ref[...] = layer_norm(last, gains_ref[4:5], gains_ref[5:6]).astype(BF)
    line.drain()
    for copy in stores:
        copy.wait()


def forward_call(depth, start_rows, gains, length, attn, own_mlp):
    rows, width = start_rows.shape
    hidden_units = own_mlp.shape[2]
    line_sems = [pltpu.SemaphoreType.DMA((n * depth,)) for n in (4, 2, 2, 2)]
    cols = hidden_units // 4
    heads = cols // HD
    gathered = (4, rows, width)
    units = (4, rows, hidden_units)

    def shape(dims, kind):
        return jax.ShapeDtypeStruct(dims, kind)

    return pl.pallas_call(
        functools.partial(forward_kernel, depth),
        out_shape=(
            shape((2, width, hidden_units), BF),
            shape(gathered, BF),
            shape((3, 4, rows, cols), BF),
            shape((4, rows, cols), BF),
            shape((heads, 4, 1, rows), F32),
            shape((rows, width), F32),
            shape(gathered, BF),
            shape(units, F32),
            shape(units, BF),
            shape((rows, width), F32),
            shape((rows, width), BF),
        ),
        in_specs=[vspec(), vspec(), vspec(), vspec(), aspec()],
        out_specs=(
            aspec(), aspec(), aspec(), aspec(), vspec(), vspec(), aspec(), aspec(), aspec(), vspec(), vspec(),
        ),
        scratch_shapes=[
            VMEM((2, width, hidden_units), BF),
            VMEM((width, hidden_units), BF),
            VMEM(gathered, BF),
            VMEM((3, 4, rows, cols), BF),
            VMEM((heads, HD, 4 * rows), BF),
            VMEM((4, rows, cols), BF),
            VMEM((heads, HD, rows), F32),
            VMEM((4 * rows, rows), F32),
            VMEM(gathered, BF),
            VMEM(units, F32),
            VMEM(units, BF),
            pltpu.SemaphoreType.DMA((1,)),
            pltpu.SemaphoreType.DMA((7,)),
        ]
        + line_sems
        + group_scratch(rows, width),
        compiler_params=comm_params(7),
        name="layer_forward",
    )(start_rows, gains, length, own_mlp, attn)


def norm_back(values, gain_row, cotangent):
    centered = values - jnp.mean(values, axis=-1, keepdims=True)
    scale = lax.rsqrt(jnp.mean(centered * centered, axis=-1, keepdims=True) + 1e-05)
    normed = centered * scale
    weighted = cotangent * gain_row
    first = jnp.mean(weighted, axis=-1, keepdims=True)
    second = jnp.mean(weighted * normed, axis=-1, keepdims=True)
    grad = (weighted - first - normed * second) * scale
    gain = jnp.sum(cotangent * normed, axis=0, keepdims=True)
    return grad, gain, jnp.sum(cotangent, axis=0, keepdims=True)


def gelu_slope(values):
    root, cube = 0.7978845608028654, 0.044715
    square = values * values
    bent = jnp.tanh(root * (values + cube * values * square))
    return 0.5 * (1.0 + bent) + 0.5 * values * (1.0 - bent * bent) * root * (1.0 + 3.0 * cube * square)


def backward_kernel(
    grad_ref, start_ref, middle_ref, last_ref, gains_ref, length_ref, logs_ref,
    weights_hbm, attn_hbm, normed_one_hbm, members_hbm, attended_hbm, normed_two_hbm, pre_hbm, act_hbm,
    out_ref, norms_ref, weight_grads_hbm,
    weights, normed_one, members, attended, normed_two, pre, act,
    grad_last, grad_low, grad_pre, key_cols, query_cols, bias, key_grad, value_grad, grad_mid, grad_att, member_grads,
    weight_grads, load_sem, store_sem, *scratch
):
    group = Group(scratch[5], scratch[6], scratch[:5])
    sources = (
        (weights_hbm.at[1], weights.at[1]),
        (pre_hbm, pre),
        (weights_hbm.at[0], weights.at[0]),
        (act_hbm, act),
        (normed_two_hbm, normed_two),
        (attn_hbm, weights.at[2]),
        (members_hbm, members),
        (normed_one_hbm, normed_one),
        (attended_hbm, attended),
    )
    loads = [
        pltpu.make_async_copy(src, dst, load_sem.at[n]) for n, (src, dst) in enumerate(sources)
    ]
    for copy in loads:
        copy.start()
    blocks, rows, width = grad_low.shape
    cols = attended.shape[2]
    heads = cols // HD
    grad, gain, shift = norm_back(last_ref[...], gains_ref[4:5], grad_ref[...])
    grad_last[...] = grad
    norms_ref[4:5] = gain
    norms_ref[5:6] = shift
    grad_low[group.me] = grad.astype(BF)
    greet([group.y_peer, group.c_peer])
    sums = GroupSum(group, 0)

    def feed(block, i, side):
        active = dot_nn(grad_low[block], weights[1])
        low = (active * gelu_slope(pre[block])).astype(BF)
        grad_pre[block] = low
        sums.add(contract_cols(low, weights[0]), i, side)

    for copy in loads[:3]:
        copy.wait()
    group.gather(grad_low, feed)
    sums.pass_on()
    for copy in loads[3:]:
        copy.wait()

    def chunk(ref, j):
        return flat(ref[:, :, pl.ds(pl.multiple_of(j * rows, rows), rows)])

    def place_of(j):
        return pl.ds(pl.multiple_of(j * rows, rows), rows)

    def mlp_grads(j, carry):
        weight_grads[0, place_of(j), :] = contract_rows(chunk(normed_two, j), flat(grad_pre[...])).astype(BF)
        weight_grads[1, place_of(j), :] = contract_rows(chunk(grad_low, j), flat(act[...])).astype(BF)
        return carry

    lax.fori_loop(0, width // rows, mlp_grads, 0)
    grad, gain, shift = norm_back(middle_ref[...], gains_ref[2:3], sums.finish())
    norms_ref[2:3] = gain
    norms_ref[3:4] = shift
    grad = grad + grad_last[...]
    grad_last[...] = grad
    grad_mid[group.me] = grad.astype(BF)
    key_cols[...] = columns_of(flat(members[1]), heads)
    key_grad[...] = jnp.zeros(key_grad.shape, F32)
    value_grad[...] = jnp.zeros(value_grad.shape, F32)

    def attend(block, i, side):
        grad_att[block] = dot_nn(grad_mid[block], weights[2, :, 3 * cols :]).astype(BF)
        bias[...] = score_bias(block, length_ref[...], blocks * rows)

        def head(h, carry):
            queries = members[0, block] * head_mask(h, cols, HD ** (-0.5))
            grads = grad_att[block] * head_mask(h, cols, 1.0)
            scores = contract_cols(flat(members[1]), queries) + bias[...]
            probs = jnp.exp(scores - logs_ref[h, block])
            grad_probs = contract_cols(flat(members[2]), grads)
            inner = jnp.sum(grad_probs * probs, axis=0, keepdims=True)
            grad_scores = (probs * (grad_probs - inner)).astype(BF)
            key_grad[...] += dot_nn(grad_scores, queries)
            value_grad[...] += dot_nn(probs.astype(BF), grads)
            query_cols[h] = dot_nn(key_cols[h], grad_scores)
            return carry

        lax.fori_loop(0, heads, head, 0)
        turned = jnp.transpose(flat(query_cols[...])) * HD ** (-0.5)
        member_grads[block, :, :cols] = turned.astype(BF)

    group.gather(grad_mid, attend)
    split = (blocks, rows, cols)
    member_grads[:, :, cols : 2 * cols] = key_grad[...].astype(BF).reshape(split)
    member_grads[:, :, 2 * cols :] = value_grad[...].astype(BF).reshape(split)
    again = GroupSum(group, 1)

    def back(block, i, side):
        again.add(contract_cols(member_grads[block], weights[2, :, : 3 * cols]), i, side)

    group.pair(1, 1, lambda block, i: back(block, i, 1))
    again.pass_on()
    group.pair(0, 1, lambda block, i: back(block, i, 0))

    def attn_grads(j, carry):
        weight_grads[2, place_of(j), : 3 * cols] = contract_rows(
            chunk(normed_one, j), flat(member_grads[...])
        ).astype(BF)
        weight_grads[2, place_of(j), 3 * cols :] = contract_rows(
            chunk(grad_mid, j), flat(attended[...])
        ).astype(BF)
        return carry

    lax.fori_loop(0, width // rows, attn_grads, 0)
    store = pltpu.make_async_copy(weight_grads, weight_grads_hbm, store_sem.at[0])
    store.start()
    grad, gain, shift = norm_back(start_ref[...], gains_ref[0:1], again.finish())
    norms_ref[0:1] = gain
    norms_ref[1:2] = shift
    out_ref[...] = grad_last[...] + grad
    store.wait()


def backward_call(grad_hidden, start_rows, middle, last_rows, gains, length, logs, mlp, attn, kept):
    rows, width = start_rows.shape
    hidden_units = mlp.shape[2]
    cols = hidden_units // 4
    heads = cols // HD
    gathered = (4, rows, width)
    units = (4, rows, hidden_units)
    stack = (3, width, hidden_units)
    return pl.pallas_call(
        backward_kernel,
        out_shape=(
            jax.ShapeDtypeStruct((rows, width), F32),
            jax.ShapeDtypeStruct((6, width), F32),
            jax.ShapeDtypeStruct(stack, BF),
        ),
        in_specs=[vspec()] * 7 + [aspec()] * 8,
        out_specs=(vspec(), vspec(), aspec()),
        scratch_shapes=[
            VMEM(stack, BF),
            VMEM(gathered, BF),
            VMEM((3, 4, rows, cols), BF),
            VMEM((4, rows, cols), BF),
            VMEM(gathered, BF),
            VMEM(units, F32),
            VMEM(units, BF),
            VMEM((rows, width), F32),
            VMEM(gathered, BF),
            VMEM(units, BF),
            VMEM((heads, HD, 4 * rows), BF),
            VMEM((heads, HD, rows), F32),
            VMEM((4 * rows, rows), F32),
            VMEM((4 * rows, cols), F32),
            VMEM((4 * rows, cols), F32),
            VMEM(gathered, BF),
            VMEM((4, rows, cols), BF),
            VMEM((4, rows, 3 * cols), BF),
            VMEM(stack, BF),
            pltpu.SemaphoreType.DMA((9,)),
            pltpu.SemaphoreType.DMA((1,)),
        ]
        + group_scratch(rows, width),
        compiler_params=comm_params(8),
        name="layer_backward",
    )(grad_hidden, start_rows, middle, last_rows, gains, length, logs, mlp, attn, *kept)


def small_gather_kernel(depth, ints_ref, norms_ref, ints_out, norms_out, ss, rs, ns, nr):
    z, x, y, c = place()
    dp = lax.axis_index("dp")
    mp = lax.axis_index("mp")
    count = 2 * depth
    peers = [((dp + k) % count, mp) for k in range(1, count)]
    greet(peers)
    ints_out[dp] = ints_ref[...]
    norms_out[dp] = norms_ref[...]
    copies = []
    for k, peer in enumerate(peers):
        copies.append(remote(ints_ref, ints_out.at[dp], ss.at[k], rs.at[k], peer))
        copies.append(remote(norms_ref, norms_out.at[dp], ns.at[k], nr.at[k], peer))
    for copy in copies:
        copy.start()
    for copy in copies:
        copy.wait()


def small_gather(depth, ints, norms):
    count = 2 * depth
    return pl.pallas_call(
        functools.partial(small_gather_kernel, depth),
        out_shape=(
            jax.ShapeDtypeStruct((count, *ints.shape), ints.dtype),
            jax.ShapeDtypeStruct((count, *norms.shape), norms.dtype),
        ),
        in_specs=[vspec(), vspec()],
        out_specs=(vspec(), vspec()),
        scratch_shapes=[pltpu.SemaphoreType.DMA((count - 1,))] * 4,
        compiler_params=comm_params(5, 8),
        name="small_gather",
    )(ints, norms)


def scalar_sum_kernel(depth, own_ref, out_ref, snap, got, ss, rs):
    z, x, y, c = place()
    peers = [device(z, x, y, 1 - c), device(z, x, 1 - y, c), device(z, 1 - x, y, c)]
    z_peers = [device((z + k) % depth, x, y, c) for k in range(1, depth)]
    greet(peers + z_peers)
    snap[0] = own_ref[...]
    for number, peer in enumerate(peers):
        copy = remote(snap.at[number], got.at[depth + number], ss.at[number], rs.at[number], peer)
        copy.start()
        copy.wait()
        snap[number + 1] = snap[number] + got[depth + number]
    copies = [
        remote(snap.at[3], got.at[z], ss.at[2 + k], rs.at[2 + k], z_peers[k - 1])
        for k in range(1, depth)
    ]
    for copy in copies:
        copy.start()
    got[z] = snap[3]
    for copy in copies:
        copy.wait()
    total = got[0]
    for k in range(1, depth):
        total = total + got[k]
    out_ref[...] = total


def scalar_sum(depth, values):
    return pl.pallas_call(
        functools.partial(scalar_sum_kernel, depth),
        out_shape=jax.ShapeDtypeStruct(values.shape, F32),
        in_specs=[vspec()],
        out_specs=vspec(),
        scratch_shapes=[
            VMEM((4, *values.shape), F32),
            VMEM((depth + 3, *values.shape), F32),
            pltpu.SemaphoreType.DMA((depth + 2,)),
            pltpu.SemaphoreType.DMA((depth + 2,)),
        ],
        compiler_params=comm_params(6, 8),
        name="scalar_sum",
    )(values)


class KernelMoves:
    def __init__(self, depth):
        self.depth = depth

    def small(self, token_ids, target_ids, mask, norms):
        packed = jnp.concatenate([v.reshape(-1, 128) for v in (token_ids, target_ids, mask)], axis=0)
        each = packed.shape[0] // 3
        low = jnp.pad(norms.astype(BF), ((0, 16 - norms.shape[0]), (0, 0)))
        ints, norms_all = small_gather(self.depth, packed, low)
        norms_all = jnp.transpose(norms_all, (1, 0, 2)).reshape(16, -1)[: norms.shape[0]]
        return [ints[:, i * each : (i + 1) * each].reshape(-1) for i in range(3)] + [norms_all]

    def embed(self, table_low, local_ids, rows, positions, first_row):
        ids = local_ids.astype(F32).reshape(-1, 1, rows)
        return embed_call(self.depth, table_low, ids, positions.astype(BF))

    def weights(self, attn_in, attn_out, mlp_in, mlp_out):
        attn = jnp.concatenate([attn_in[0], attn_in[1], attn_in[2], attn_out], axis=1)
        gathered = lax.all_gather(attn.astype(BF), "dp", axis=0, tiled=True)
        return gathered, jnp.stack([mlp_in, mlp_out]).astype(BF)

    def forward(self, start_rows, gains, length, weights):
        row = jnp.full((1, start_rows.shape[0]), length.astype(F32))
        attn, own_mlp = weights
        mlp, normed_one, members, attended, logs, middle, normed_two, pre, act, last_rows, hidden = (
            forward_call(self.depth, start_rows, gains, row, attn, own_mlp)
        )
        kept = (normed_one, members, attended, normed_two, pre, act)
        return hidden, (start_rows, middle, last_rows, gains, row, logs, mlp, attn, kept)

    def backward(self, grad_hidden, saved):
        grad_start, norms_grad, grads = backward_call(grad_hidden, *saved)
        share = lax.psum_scatter(grads, "dp", scatter_dimension=1, tiled=True).astype(F32)
        cols = share.shape[2] // 4
        attn = jnp.stack([share[2, :, i * cols : (i + 1) * cols] for i in range(4)])
        return grad_start, norms_grad, attn, share[:2]

    def head(self, hidden, table_low, targets, weights, vocab_size):
        rows = hidden.shape[0]
        targets = targets.astype(F32).reshape(-1, 1, rows)
        weights = weights.reshape(-1, 1, rows)
        hidden_all, expo, top, total, picked = logits_call(
            self.depth, vocab_size, hidden, table_low, targets
        )
        grad_hidden, grads = grads_call(
            self.depth, vocab_size, table_low, targets, weights, top, total, expo
        )
        weights = weights.reshape(-1)
        first = (lax.axis_index("dp") * lax.axis_size("mp") + lax.axis_index("mp")) * rows
        own_logs = lax.dynamic_slice(total.reshape(-1), (first,), (rows,))
        log_sum = jnp.sum(own_logs * lax.dynamic_slice(weights, (first,), (rows,)))
        loss_part = log_sum - jnp.sum(picked.reshape(-1) * weights)
        return grad_hidden, (grads, hidden_all), loss_part

    def scatter(self, grad_start, norms_grad, local_ids, table_grad, span):
        rows = grad_start.shape[0]
        count = norms_grad.shape[0]
        rest = jnp.pad(norms_grad, ((0, 16 - count), (0, 0)))
        sent = jnp.concatenate([grad_start, rest], axis=0).astype(BF)
        ids = local_ids.astype(F32).reshape(-1, 1, rows)
        grads, hidden_all = table_grad
        table_grad, positions_grad, rest, square = scatter_call(
            self.depth, sent, ids, grads, hidden_all, span
        )
        dp = lax.axis_index("dp")
        part = rest.shape[1] // lax.axis_size("dp")
        norms_part = lax.dynamic_slice(rest, (0, dp * part), (16, part))[:count]
        return table_grad, positions_grad, norms_part, square[0, 0]

    def total(self, scalars):
        row = jnp.concatenate([jnp.full((1, 128), value, F32) for value in scalars], axis=0)
        row = jnp.pad(row, ((0, 8 - len(scalars)), (0, 0)))
        summed = scalar_sum(self.depth, row)
        return [summed[i, 0] for i in range(len(scalars))]


class PlainMoves:
    parts = 4

    def split(self, values, rows):
        piece = rows // self.parts
        return jnp.swapaxes(values.reshape(-1, self.parts, piece), 0, 1).reshape(self.parts, -1)

    def small(self, token_ids, target_ids, mask, norms):
        found = [lax.all_gather(v.reshape(-1), "dp", tiled=True) for v in (token_ids, target_ids, mask)]
        return found + [lax.all_gather(norms.astype(BF), "dp", axis=1, tiled=True)]

    def embed(self, table_low, local_ids, rows, positions, first_row):
        positions_all = lax.all_gather(positions.astype(BF), "dp", axis=0, tiled=True)
        own_positions = lax.dynamic_slice(positions_all, (first_row, 0), (rows, positions.shape[1]))

        def one(ids):
            looked = jnp.take(table_low, jnp.maximum(ids, 0), axis=0)
            looked = jnp.where(ids[:, None] >= 0, looked, jnp.zeros((), BF))
            return lax.psum_scatter(looked, ("dp", "mp"), tiled=True)

        embedded = lax.map(one, self.split(local_ids, rows)).reshape(rows, -1)
        return embedded.astype(F32) + own_positions.astype(F32)

    def gather_group(self, own):
        return lax.all_gather(own, "mp", tiled=True)

    def sum_group(self, parts):
        return lax.psum_scatter(parts, "mp", tiled=True)

    def weights(self, attn_in, attn_out, mlp_in, mlp_out):
        attn_pack = jnp.concatenate([attn_in, attn_out[None]], axis=0).astype(BF)
        mlp_pack = jnp.stack([mlp_in, mlp_out]).astype(BF)
        attn_all = lax.all_gather(attn_pack, "dp", axis=1, tiled=True)
        mlp_all = lax.all_gather(mlp_pack, "dp", axis=1, tiled=True)
        return attn_all, mlp_all

    def forward(self, start_rows, gains, length, weights):
        attn_all, mlp_all = weights
        normed_one = self.gather_group(layer_norm(start_rows, gains[0], gains[1]).astype(BF))
        seq_len = normed_one.shape[0]
        head_shape = (seq_len, attn_all.shape[2] // HD, HD)
        queries, keys, values = (dot_nn(normed_one, attn_all[i]).astype(BF) for i in range(3))
        heads = [v.reshape(head_shape) for v in (queries, keys, values)]
        attended, log_total = attend_forward(*heads, length)
        attended = attended.reshape(seq_len, -1)
        middle = start_rows + self.sum_group(contract_cols(attended, attn_all[3]))
        normed_two = self.gather_group(layer_norm(middle, gains[2], gains[3]).astype(BF))
        pre_gelu = dot_nn(normed_two, mlp_all[0])
        activated = gelu_tanh(pre_gelu).astype(BF)
        last_rows = middle + self.sum_group(contract_cols(activated, mlp_all[1]))
        hidden = layer_norm(last_rows, gains[4], gains[5]).astype(BF)
        return hidden, (
            start_rows, middle, last_rows, gains, length, weights, normed_one, heads, attended, log_total,
            normed_two, pre_gelu, activated,
        )

    def backward(self, grad_hidden, saved):
        (
            start_rows, middle, last_rows, gains, length, weights, normed_one, heads, attended, log_total,
            normed_two, pre_gelu, activated,
        ) = saved
        attn_all, mlp_all = weights
        grad_last, gain_three, shift_three = norm_back(last_rows, gains[4], grad_hidden)
        grad_last_low = self.gather_group(grad_last.astype(BF))
        mlp_out_grad = contract_rows(grad_last_low, activated)
        grad_activated = dot_nn(grad_last_low, mlp_all[1])
        grad_pre = (grad_activated * gelu_slope(pre_gelu)).astype(BF)
        mlp_in_grad = contract_rows(normed_two, grad_pre)
        grad_normed_two = self.sum_group(contract_cols(grad_pre, mlp_all[0]))
        mlp_share = lax.psum_scatter(
            jnp.stack([mlp_in_grad, mlp_out_grad]).astype(BF), "dp", scatter_dimension=1, tiled=True
        ).astype(F32)
        grad_from_two, gain_two, shift_two = norm_back(middle, gains[2], grad_normed_two)
        grad_middle = grad_last + grad_from_two
        grad_middle_low = self.gather_group(grad_middle.astype(BF))
        attn_out_grad = contract_rows(grad_middle_low, attended)
        grad_attended = dot_nn(grad_middle_low, attn_all[3]).astype(BF).reshape(heads[0].shape)
        members = [
            v.reshape(attended.shape)
            for v in attend_backward(*heads, length, log_total, grad_attended)
        ]
        attn_grads = [contract_rows(normed_one, v) for v in members] + [attn_out_grad]
        grad_normed_one = self.sum_group(
            sum(contract_cols(members[i], attn_all[i]) for i in range(3))
        )
        attn_share = lax.psum_scatter(
            jnp.stack(attn_grads).astype(BF), "dp", scatter_dimension=1, tiled=True
        ).astype(F32)
        grad_from_one, gain_one, shift_one = norm_back(start_rows, gains[0], grad_normed_one)
        rows_of = (gain_one, shift_one, gain_two, shift_two, gain_three, shift_three)
        return grad_middle + grad_from_one, jnp.concatenate(rows_of), attn_share, mlp_share

    def head(self, hidden, table_low, targets, weights, vocab_size):
        rows, width = hidden.shape
        shard = table_low.shape[0]

        def one(carried, packed):
            own, ids, weight = packed
            table_grad, loss_part = carried
            hidden_all = lax.all_gather(own, ("dp", "mp"), tiled=True)
            logits = contract_cols(hidden_all, table_low)
            top = lax.pmax(jnp.max(logits, axis=1), ("dp", "mp"))
            onehot = jnp.arange(shard)[None, :] == ids[:, None]
            picked = jnp.sum(logits * jnp.where(onehot, 1.0 - smoothing + even, even), axis=1)
            total = lax.psum(jnp.sum(jnp.exp(logits - top[:, None]), axis=1), ("dp", "mp"))
            total = top + jnp.log(total)
            grads = jnp.exp(logits - total[:, None]) - jnp.where(onehot, 1.0 - smoothing, 0.0)
            grads = ((grads - even) * weight[:, None]).astype(BF)
            partial = dot_nn(grads, table_low).astype(BF)
            grad_hidden = lax.psum_scatter(partial, ("dp", "mp"), tiled=True).astype(F32)
            table_grad = table_grad + contract_rows(grads, hidden_all)
            return (table_grad, loss_part + jnp.sum((total / devices - picked) * weight)), grad_hidden

        even = smoothing / vocab_size
        devices = lax.axis_size("dp") * lax.axis_size("mp")
        first = (jnp.zeros((shard, width), F32), jnp.zeros((), F32))
        own = hidden.reshape(self.parts, rows // self.parts, width)
        (table_grad, loss_part), grad_hidden = lax.scan(
            one, first, (own, self.split(targets, rows), self.split(weights, rows))
        )
        return grad_hidden.reshape(rows, width), table_grad, loss_part

    def scatter(self, grad_start, norms_grad, local_ids, table_grad, span):
        shard = table_grad.shape[0]
        rows, width = grad_start.shape

        def one(carried, packed):
            own, ids = packed
            everything = lax.all_gather(own, ("dp", "mp"), tiled=True).astype(F32)
            safe = jnp.where(ids >= 0, ids, shard)
            return carried + jax.ops.segment_sum(everything, safe, num_segments=shard), None

        own = grad_start.astype(BF).reshape(self.parts, rows // self.parts, width)
        table_grad, unused = lax.scan(one, table_grad, (own, self.split(local_ids, rows)))
        spread = jnp.zeros((lax.axis_size("mp") * rows, width), F32)
        spread = lax.dynamic_update_slice(spread, grad_start, (lax.axis_index("mp") * rows, 0))
        positions_grad = lax.psum(lax.psum_scatter(spread, "dp", tiled=True), "mp")
        norms_part = lax.psum(
            lax.psum_scatter(norms_grad, "dp", scatter_dimension=1, tiled=True), "mp"
        )
        return table_grad, positions_grad, norms_part, jnp.sum(table_grad * table_grad)

    def total(self, scalars):
        return list(lax.psum(tuple(scalars), ("dp", "mp")))


def attend_scores(queries, keys, length):
    scores = jnp.einsum("qhe,khe->hqk", queries, keys, preferred_element_type=F32) * HD ** (-0.5)
    place_at = jnp.arange(queries.shape[0])
    allowed = (place_at[None, :] <= place_at[:, None]) & (place_at[None, :] < length)
    return jnp.where(allowed[None], scores, -1e30)


def attend_forward(queries, keys, values, length):
    scores = attend_scores(queries, keys, length)
    top = jnp.max(scores, axis=-1, keepdims=True)
    log_total = jnp.log(jnp.sum(jnp.exp(scores - top), axis=-1, keepdims=True)) + top
    probs = jnp.exp(scores - log_total).astype(BF)
    attended = jnp.einsum("hqk,khe->qhe", probs, values, preferred_element_type=F32)
    return attended.astype(BF), log_total


def attend_backward(queries, keys, values, length, log_total, grad):
    probs = jnp.exp(attend_scores(queries, keys, length) - log_total)
    grad_values = jnp.einsum("hqk,qhe->khe", probs.astype(BF), grad, preferred_element_type=F32)
    grad_probs = jnp.einsum("qhe,khe->hqk", grad, values, preferred_element_type=F32)
    inner = jnp.sum(grad_probs * probs, axis=-1, keepdims=True)
    grad_scores = (probs * (grad_probs - inner)).astype(BF)
    scale = HD ** (-0.5)
    grad_queries = jnp.einsum("hqk,khe->qhe", grad_scores, keys, preferred_element_type=F32) * scale
    grad_keys = jnp.einsum("hqk,qhe->khe", grad_scores, queries, preferred_element_type=F32) * scale
    return grad_queries.astype(BF), grad_keys.astype(BF), grad_values.astype(BF)


def local(
    moves,
    token_ids,
    target_ids,
    loss_mask,
    lengths,
    step_count,
    *weights,
):
    masters, firsts, seconds = weights[:7], weights[7:14], weights[14:]
    table, positions, attn_in, attn_out, mlp_in, mlp_out, norms = masters
    shard = table.shape[0]
    width = table.shape[1]
    dp, mp = lax.axis_index("dp"), lax.axis_index("mp")
    dp_count, mp_count = lax.axis_size("dp"), lax.axis_size("mp")
    vocab_size = shard * dp_count * mp_count
    seq_len = token_ids.shape[1]
    rows = token_ids.size // mp_count
    table_low = table.astype(BF)
    ids_all, targets_all, mask_all, norms_all = moves.small(token_ids, target_ids, loss_mask, norms)
    gains = norms_all.astype(F32)
    mask_all = mask_all.astype(F32)
    token_total = jnp.sum(mask_all)
    row_weights = mask_all / token_total
    base = (dp * mp_count + mp) * shard

    def local_of(ids):
        inside = (ids >= base) & (ids < base + shard)
        return jnp.where(inside, ids - base, -1)

    local_ids, local_targets = local_of(ids_all), local_of(targets_all)
    layer_weights = moves.weights(attn_in, attn_out, mlp_in, mlp_out)

    first_row = (mp * rows) % seq_len
    start_rows = moves.embed(table_low, local_ids, rows, positions, first_row)
    hidden, saved = moves.forward(start_rows, gains, lengths[0], layer_weights)

    grad_hidden, table_grad, loss_part = moves.head(
        hidden, table_low, local_targets, row_weights, vocab_size
    )
    grad_start, norms_grad, attn_share, mlp_share = moves.backward(grad_hidden, saved)
    table_grad, positions_grad, norms_part, table_square = moves.scatter(
        grad_start, norms_grad, local_ids, table_grad, positions.shape[0]
    )
    shares = (
        table_grad,
        positions_grad,
        attn_share[:3],
        attn_share[3],
        mlp_share[0],
        mlp_share[1],
        norms_part,
    )
    copies = (1.0, mp_count, 1.0, 1.0, 1.0, 1.0, mp_count)
    squares = sum((jnp.sum(v * v) / n for v, n in zip(shares[1:], copies[1:])), table_square)
    total_square, loss = moves.total([squares, loss_part])
    grad_norm = jnp.sqrt(total_square)
    factor = jnp.minimum(1.0, clip_norm / (grad_norm + 1e-06))
    step_float = step_count[0].astype(F32)
    updated = [
        adam_update(
            masters[i],
            firsts[i],
            seconds[i],
            factor * shares[i],
            learn_rates[i],
            decay_rates[i],
            step_float,
        )
        for i in range(7)
    ]
    return (loss, grad_norm) + tuple(updated[i][part] for part in range(3) for i in range(7))


def fits_kernels(mesh):
    if mesh.shape["mp"] != 4 or mesh.shape["dp"] != 8:
        return False
    for (dp, mp), item in zip(
        ((i, j) for i in range(8) for j in range(4)), mesh.devices.reshape(-1)
    ):
        coords = getattr(item, "coords", None)
        if coords is not None and (tuple(coords), item.core_on_chip) != (
            (dp % 2, mp // 2, dp // 2),
            mp % 2,
        ):
            return False
    return True


def solution(mesh):
    table, rows, heads, grid, norms = (
        P(("dp", "mp"), None),
        P("dp", None),
        P(None, "dp", "mp"),
        P("dp", "mp"),
        P(None, "dp"),
    )
    each = (table, rows, heads, grid, grid, grid, norms)
    in_specs = (rows, rows, rows, P("dp"), P()) + each * 3
    out_specs = (P(), P()) + each * 3
    moves = KernelMoves(mesh.shape["dp"] // 2) if fits_kernels(mesh) else PlainMoves()
    return jax.shard_map(
        functools.partial(local, moves),
        mesh=mesh,
        in_specs=in_specs,
        out_specs=out_specs,
        check_vma=False,
    )
```

```python
import functools

import jax
import jax.numpy as jnp
from jax import lax
from jax.experimental import pallas as pl
from jax.experimental.pallas import tpu as pltpu
from jax.sharding import PartitionSpec as P

HD = 64
VOCAB = 50688
MESH = pl.DeviceIdType.MESH
ANY = pl.ANY
VMEM = pltpu.VMEM
BF = jnp.bfloat16
F32 = jnp.float32

smoothing = 0.1
clip_norm = 0.01
beta_one = 0.9
beta_two = 0.999
adam_eps = 1e-08
learn_rates = (0.06, 0.06, 0.03, 0.03, 0.03, 0.004, 0.3)
decay_rates = (0.1, 0.0, 0.1, 0.1, 0.1, 0.1, 0.0)


def layer_norm(values, gain_row, shift_row):
    centered = values - jnp.mean(values, axis=-1, keepdims=True)
    spread = jnp.mean(centered * centered, axis=-1, keepdims=True)
    return centered * lax.rsqrt(spread + 1e-05) * gain_row + shift_row


def gelu_tanh(values):
    return jax.nn.gelu(values, approximate=True)


def adam_update(weight, first_moment, second, grad_item, rate, decay, step_float):
    first_new = beta_one * first_moment + (1.0 - beta_one) * grad_item
    second_new = beta_two * second + (1.0 - beta_two) * grad_item * grad_item
    first_hat = first_new / (1.0 - beta_one**step_float)
    second_hat = second_new / (1.0 - beta_two**step_float)
    weight_new = weight - rate * (first_hat / (jnp.sqrt(second_hat) + adam_eps) + decay * weight)
    return (weight_new, first_new, second_new)


def contract_rows(left, right):
    return lax.dot_general(
        left, right, (((0,), (0,)), ((), ())), preferred_element_type=F32
    )


def contract_cols(left, right):
    return lax.dot_general(
        left, right, (((1,), (1,)), ((), ())), preferred_element_type=F32
    )


def dot_nn(left, right):
    return lax.dot_general(
        left, right, (((1,), (0,)), ((), ())), preferred_element_type=F32
    )


def place():
    dp = lax.axis_index("dp")
    mp = lax.axis_index("mp")
    return dp // 2, dp % 2, mp // 2, mp % 2


def device(z, x, y, c):
    return (z * 2 + x, y * 2 + c)


def flip(bit, by):
    return bit + by - 2 * bit * by


def greet(peers):
    barrier = pltpu.get_barrier_semaphore()
    for peer in peers:
        pl.semaphore_signal(barrier, inc=1, device_id=peer, device_id_type=MESH)
    pl.semaphore_wait(barrier, len(peers))


def remote(src, dst, send_sem, recv_sem, peer):
    return pltpu.make_async_remote_copy(
        src_ref=src,
        dst_ref=dst,
        send_sem=send_sem,
        recv_sem=recv_sem,
        device_id=peer,
        device_id_type=MESH,
    )


def to_column(row):
    wide = jnp.broadcast_to(row, (128, row.shape[1]))
    return jnp.transpose(wide)[:, :1]


def to_row(column):
    wide = jnp.broadcast_to(column, (column.shape[0], 128))
    return jnp.transpose(wide)[:1, :]


ARRIVALS = (
    "000o 010p 100d 001q 200d 110p 011q 101q 201q 300d 210p 111q 310d 301q 211q 311q",
    "100o 000u 200d 010u 300d 110p 201q 310d 001q 301q 210p 111q 011q 101q 211q 311q",
)
DEPTH = 4
EVENTS = 16


def sent_on(z, source, kind):
    up = ["u"] if z < DEPTH - 1 else []
    down = ["d"] if z > 0 else []
    if source in (1, 2):
        return {"o": up + down + ["p", "q"], "u": up + ["p", "q"], "d": down + ["p", "q"]}.get(
            kind, ["q"] if kind == "p" else []
        )
    return {
        "o": ["p"] + up + down + ["q"],
        "p": up + down + ["q"],
        "u": up + ["q"],
        "d": down + ["q"],
    }.get(kind, [])


@functools.lru_cache
def route_tables():
    mirror = {"u": "d", "d": "u"}
    events = {}
    for z in range(DEPTH):
        rows = []
        for item in ARRIVALS[min(z, DEPTH - 1 - z)].split():
            source, first, second, kind = int(item[0]), int(item[1]), int(item[2]), item[3]
            if z >= 2:
                source, kind = DEPTH - 1 - source, mirror.get(kind, kind)
            rows.append((source, first, second, kind))
        events[z] = rows
    order = ("p", "q", "u", "d")
    slots, firsts, flags = {}, {}, {}
    for z in range(DEPTH):
        count = 0
        turned = ("p", "q", "u", "d") if z < 2 else ("p", "q", "d", "u")
        for n, (source, first, second, kind) in enumerate(events[z]):
            sends = sent_on(z, source, kind)
            firsts[z, n] = count
            flags[z, n] = sum(1 << i for i, k in enumerate(turned) if k in sends)
            for k in turned:
                if k in sends:
                    slots[z, source, first, second, k] = count
                    count += 1
    tables = []
    most = 1 + max(slots.values())
    for z in range(2):
        rows = []
        for n, (source, first, second, kind) in enumerate(events[z]):
            if kind == "o":
                slot, origin = 0, 0
            else:
                at = z - 1 if kind == "u" else z + 1 if kind == "d" else z
                up_first = 1 - first if kind == "p" else first
                up_second = 1 - second if kind == "q" else second
                slot = slots[at, source, up_first, up_second, kind]
                origin = order.index(kind)
            rows.append((source, 2 * first + second, flags[z, n], slot, firsts[z, n], origin))
        tables.append(rows)
    return tables, most


RADIX = 1024


class Route:
    def __init__(self):
        self.z, self.x, self.y, self.c = place()
        tables, self.slots = route_tables()
        kind = flip(self.z % 2, self.z // 2)
        self.mirrored = self.z // 2
        self.packed = []
        for digits in (
            lambda row: row[0] + 4 * row[1] + 16 * row[2] + 256 * row[5],
            lambda row: row[3] + 32 * row[4],
        ):
            low, high = (
                [digits(rows[n]) + RADIX * digits(rows[n + 1]) for n in range(0, EVENTS, 2)]
                for rows in tables
            )
            self.packed.append([a + kind * (b - a) for a, b in zip(low, high)])
        sign = 1 - 2 * self.mirrored
        z, x, y, c = self.z, self.x, self.y, self.c
        self.c_peer = device(z, x, y, 1 - c)
        self.peers = (
            device(z, flip(x, 1 - c), flip(y, c), c),
            device(z, flip(x, c), flip(y, 1 - c), c),
            device(z + sign, x, y, c),
            device(z - sign * kind, x, y, c),
        )

    def greet(self, others=()):
        z, x, y, c = self.z, self.x, self.y, self.c
        along = [device((z + k) % DEPTH, x, y, c) for k in range(1, DEPTH)]
        greet(along + [self.peers[0], self.peers[1], self.c_peer] + list(others))

    def digits(self, which, n):
        pair = n // 2
        bits = (pair % 2, pair // 2 % 2, pair // 4)
        total = 0
        for number, value in enumerate(self.packed[which]):
            chosen = value
            for i, bit in enumerate(bits):
                chosen = chosen * (bit if number >> i & 1 else 1 - bit)
            total = total + chosen
        return total // (1 + (RADIX - 1) * (n % 2)) % RADIX

    def flags(self, n):
        return self.digits(0, n) // 16 % 16

    def origin(self, n):
        return self.digits(0, n) // 256

    def parent_slot(self, n):
        return self.digits(1, n) % 32

    def first_slot(self, n):
        return self.digits(1, n) // 32

    def family(self, n, core):
        digits = self.digits(0, n)
        source = digits % 4
        source = source + self.mirrored * (DEPTH - 1 - 2 * source)
        first, second = digits // 8 % 2, digits // 4 % 2
        by_x = first * (1 - core) + second * core
        by_y = second * (1 - core) + first * core
        return (source * 2 + flip(self.x, by_x)) * 2 + flip(self.y, by_y)

    def sends(self, n, act):
        flags = self.flags(n)
        for i in range(4):

            @pl.when((flags // (1 << i)) % 2 == 1)
            def _():
                act(i)


def gather_scratch():
    return [
        pltpu.SemaphoreType.DMA((1,)),
        pltpu.SemaphoreType.DMA((4 * EVENTS,)),
        pltpu.SemaphoreType.DMA((EVENTS,)),
        pltpu.SemaphoreType.DMA((EVENTS,)),
        pltpu.SemaphoreType.DMA((EVENTS,)),
    ]


def gather_blocks(own_ref, land, scratch, consume):
    lsem, ss, rs, cs, cr = scratch
    route = Route()
    c = route.c
    route.greet()
    own = route.family(0, c) * 2 + c
    local = pltpu.make_async_copy(own_ref, land.at[own], lsem.at[0])
    local.start()
    local.wait()

    def copy(family, i):
        block = land.at[family * 2 + c]
        return remote(block, block, ss.at[i * EVENTS + family], rs.at[family], route.peers[i])

    def c_copy(family, core):
        block = land.at[family * 2 + core]
        return remote(block, block, cs.at[family], cr.at[family], route.c_peer)

    def event(n, carry):
        @pl.when(n < EVENTS)
        def _():
            family = route.family(n, c)

            @pl.when(n >= 1)
            def _():
                copy(family, 0).wait_recv()

            route.sends(n, lambda i: copy(family, i).start())
            c_copy(family, c).start()

        def one(i, inner):
            at = n - i

            @pl.when((at >= 0) & (at < EVENTS))
            def _():
                core = flip(c, i)
                family = route.family(at, core)

                @pl.when(i == 1)
                def _():
                    c_copy(family, core).wait_recv()

                consume(family * 2 + core, 2 * n - 1 + i + (EVENTS - n) // EVENTS - n // EVENTS)

            return inner

        lax.fori_loop(0, 2, one, 0)
        return carry

    lax.fori_loop(0, EVENTS + 1, event, 0)

    def drain(n, carry):
        family = route.family(n, c)
        route.sends(n, lambda i: copy(family, i).wait_send())
        c_copy(family, c).wait_send()
        return carry

    lax.fori_loop(0, EVENTS, drain, 0)


def reduce_scratch(rows, width):
    slots = route_tables()[1]
    return [
        VMEM((2, rows, width), F32),
        VMEM((EVENTS, rows, width), BF),
        VMEM((EVENTS, rows, width), BF),
        VMEM((EVENTS, rows, width), BF),
        VMEM((slots, rows, width), BF),
        pltpu.SemaphoreType.DMA((EVENTS,)),
        pltpu.SemaphoreType.DMA((slots,)),
        pltpu.SemaphoreType.DMA((EVENTS,)),
        pltpu.SemaphoreType.DMA((EVENTS,)),
    ]


def reduce_blocks(out_ref, scratch, produce, start=None, others=()):
    own, oth, cbuf, sbuf, rbuf, ss, rs, cs, cr = scratch
    route = Route()
    c = route.c

    def target(k):
        core = flip(c, 1 - k % 2)
        return route.family(EVENTS - 1 - k // 2, core) * 2 + core

    route.greet(others)
    if start is not None:
        start(target)

    def c_copy(n):
        return remote(oth.at[n], cbuf.at[n], cs.at[n], cr.at[n], route.c_peer)

    def copy(n, slot, i):
        return remote(sbuf.at[n], rbuf.at[slot], ss.at[n], rs.at[slot], route.peers[i])

    def finish(n):
        half = n % 2
        c_copy(n).wait_recv()
        own[half] += cbuf[n].astype(F32)
        flags, base = route.flags(n), route.first_slot(n)

        def arrived(i):
            slot = base
            for lower in range(i):
                slot = slot + (flags // (1 << lower)) % 2
            copy(n, slot, 0).wait_recv()
            own[half] += rbuf[slot].astype(F32)

        route.sends(n, arrived)

        @pl.when(n > 0)
        def _():
            sbuf[n] = own[half].astype(BF)
            for i, back in enumerate((0, 1, 3, 2)):

                @pl.when(route.origin(n) == i)
                def _():
                    copy(n, route.parent_slot(n), back).start()

    def step(m, carry):
        n = EVENTS - 1 - m

        def one(i, inner):
            @pl.when(m < EVENTS)
            def _():
                value = produce(2 * m + i, target(2 * m + i))

                @pl.when(i == 0)
                def _():
                    oth[n] = value.astype(BF)
                    c_copy(n).start()

                @pl.when(i == 1)
                def _():
                    own[n % 2] = value

            @pl.when((i == 0) & (m >= 1))
            def _():
                finish(n + 1)

            return inner

        lax.fori_loop(0, 2, one, 0)
        return carry

    lax.fori_loop(0, EVENTS + 1, step, 0)
    out_ref[...] = own[0].astype(out_ref.dtype)

    def drain(n, carry):
        c_copy(n).wait_send()

        @pl.when(n > 0)
        def _():
            copy(n, 0, 0).wait_send()

        return carry

    lax.fori_loop(0, EVENTS, drain, 0)


def comm_params(number, limit_mib=60):
    return pltpu.CompilerParams(
        collective_id=number, has_side_effects=True, vmem_limit_bytes=limit_mib << 20
    )


def vspec():
    return pl.BlockSpec(memory_space=VMEM)


def aspec():
    return pl.BlockSpec(memory_space=ANY)


def embed_kernel(depth, table_ref, ids_ref, positions_ref, out_ref, spots, spot_send, spot_recv, *scratch):
    z, x, y, c = place()
    holds = z == y * 2 + c
    others = [device((z + k // 2) % depth, flip(x, k % 2), y, c) for k in range(1, 2 * depth)]
    copies = [
        remote(positions_ref, spots.at[x], spot_send.at[k], spot_recv.at[x], peer)
        for k, peer in enumerate(others)
    ]

    def start(target):
        @pl.when(holds)
        def _():
            for copy in copies:
                copy.start()
            spots[x] = positions_ref[...]

    def produce(n, block):
        wanted = to_column(ids_ref[block])
        rows = wanted.shape[0]
        vocab = lax.broadcasted_iota(jnp.int32, (rows, table_ref.shape[0]), 1).astype(F32)
        onehot = (vocab == wanted).astype(F32).astype(BF)
        return dot_nn(onehot, table_ref[...])

    reduce_blocks(out_ref, scratch, produce, start, others)

    @pl.when(holds)
    def _():
        for copy in copies:
            copy.wait_send()

    for half in range(2):

        @pl.when(1 - holds.astype(jnp.int32) * (1 - flip(x, half)) == 1)
        def _():
            remote(positions_ref, spots.at[half], spot_send.at[0], spot_recv.at[half], others[0]).wait_recv()

    out_ref[...] += flat(spots[...]).astype(F32)


def embed_call(depth, table_low, local_ids, positions):
    blocks, unused, rows = local_ids.shape
    width = table_low.shape[1]
    return pl.pallas_call(
        functools.partial(embed_kernel, depth),
        out_shape=jax.ShapeDtypeStruct((rows, width), F32),
        in_specs=[vspec(), vspec(), vspec()],
        out_specs=vspec(),
        scratch_shapes=[
            VMEM((2, *positions.shape), BF),
            pltpu.SemaphoreType.DMA((2 * depth - 1,)),
            pltpu.SemaphoreType.DMA((2,)),
        ]
        + reduce_scratch(rows, width),
        compiler_params=comm_params(1),
        name="embed_exchange",
    )(table_low, local_ids, positions)


def combine_logs(first, second):
    top = jnp.maximum(first, second)
    return top + jnp.log(jnp.exp(first - top) + jnp.exp(second - top))


def logits_kernel(
    depth, vocab_size, hidden_ref, table_ref, targets_ref, all_ref, expo_ref, top_ref, total_ref, picked_ref,
    land, stage, snap, got, out_sem, all_sem, xs, xr, *sems
):
    z, x, y, c = place()
    blocks = land.shape[0]
    even = smoothing / vocab_size

    def out_copy(slot, block):
        return pltpu.make_async_copy(stage.at[slot], expo_ref.at[block], out_sem.at[slot])

    def keep(block):
        return pltpu.make_async_copy(land.at[block], all_ref.at[block], all_sem.at[block])

    def consume(block, number):
        slot = number % 2
        keep(block).start()
        logits = contract_cols(land[block], table_ref[...])
        top = jnp.max(logits, axis=1, keepdims=True)
        expo = jnp.exp(logits - top)
        total = jnp.sum(expo, axis=1, keepdims=True)
        wanted = to_column(targets_ref[block])
        vocab = lax.broadcasted_iota(jnp.int32, logits.shape, 1).astype(F32)
        mixed = logits * jnp.where(vocab == wanted, 1.0 - smoothing + even, even)
        picked = jnp.sum(mixed, axis=1, keepdims=True)
        top_row = to_row(top)
        top_ref[block] = top_row
        picked_ref[block] = to_row(picked)
        total_ref[block] = top_row + jnp.log(to_row(total))

        @pl.when(number >= 2)
        def _():
            out_copy(slot, block).wait()

        stage[slot] = expo.astype(BF)
        out_copy(slot, block).start()

    gather_blocks(hidden_ref, land, sems, consume)
    peers = [device(z, x, y, 1 - c), device(z, x, 1 - y, c), device(z, 1 - x, y, c)]
    for number, peer in enumerate(peers):
        snap[number] = total_ref[...]
        copy = remote(snap.at[number], got.at[number], xs.at[number], xr.at[number], peer)
        copy.start()
        copy.wait()
        total_ref[...] = combine_logs(snap[number], got[number])
    snap[3] = total_ref[...]
    copies = [
        remote(
            snap.at[3], got.at[2 + k], xs.at[2 + k], xr.at[2 + k], device((z + k) % depth, x, y, c)
        )
        for k in range(1, depth)
    ]
    for copy in copies:
        copy.start()
    for k, copy in enumerate(copies):
        copy.wait()
        total_ref[...] = combine_logs(total_ref[...], got[3 + k])
    for slot in range(2):
        out_copy(slot, 0).wait()

    def kept(block, carry):
        keep(block).wait()
        return carry

    lax.fori_loop(0, blocks, kept, 0)


def logits_call(depth, vocab_size, hidden, table_low, targets):
    blocks, unused, rows = targets.shape
    shard, width = table_low.shape
    row_shape = jax.ShapeDtypeStruct((blocks, 1, rows), F32)
    return pl.pallas_call(
        functools.partial(logits_kernel, depth, vocab_size),
        out_shape=(
            jax.ShapeDtypeStruct((blocks, rows, width), BF),
            jax.ShapeDtypeStruct((blocks, rows, shard), BF),
            row_shape,
            row_shape,
            row_shape,
        ),
        in_specs=[vspec(), vspec(), vspec()],
        out_specs=(aspec(), aspec(), vspec(), vspec(), vspec()),
        scratch_shapes=[
            VMEM((blocks, rows, width), BF),
            VMEM((2, rows, shard), BF),
            VMEM((4, blocks, 1, rows), F32),
            VMEM((2 + depth, blocks, 1, rows), F32),
            pltpu.SemaphoreType.DMA((2,)),
            pltpu.SemaphoreType.DMA((blocks,)),
            pltpu.SemaphoreType.DMA((2 + depth,)),
            pltpu.SemaphoreType.DMA((2 + depth,)),
        ]
        + gather_scratch(),
        compiler_params=comm_params(2),
        name="logits_exchange",
    )(hidden, table_low, targets)


def grads_kernel(
    depth, vocab_size, table_ref, targets_ref, weights_ref, top_ref, total_ref, expo_ref, out_ref, grad_ref,
    inbox, outbox, in_sem, out_sem, *scratch
):
    steps = 2 * EVENTS

    def fetch(slot, block):
        return pltpu.make_async_copy(expo_ref.at[block], inbox.at[slot], in_sem.at[slot])

    def store(slot, block):
        return pltpu.make_async_copy(outbox.at[slot], grad_ref.at[block], out_sem.at[slot])

    targets = []

    def start(target):
        targets.append(target)
        fetch(0, target(0)).start()

    def produce(n, block):
        slot = n % 2
        fetch(slot, block).wait()

        @pl.when(n + 1 < steps)
        def _():
            fetch(1 - slot, targets[0](n + 1)).start()

        weight = weights_ref[block]
        scale = to_column(jnp.exp(top_ref[block] - total_ref[block]) * weight)
        wanted = to_column(targets_ref[block])
        weight = to_column(weight)
        vocab = lax.broadcasted_iota(jnp.int32, inbox.shape[1:], 1).astype(F32)
        low = -(smoothing / vocab_size) * weight
        hit = low - (1.0 - smoothing) * weight
        grad = inbox[slot].astype(F32) * scale + jnp.where(vocab == wanted, hit, low)
        grad = grad.astype(BF)

        @pl.when(n >= 2)
        def _():
            store(slot, block).wait()

        outbox[slot] = grad
        store(slot, block).start()
        return dot_nn(grad, table_ref[...])

    reduce_blocks(out_ref, scratch, produce, start)
    for slot in range(2):
        store(slot, 0).wait()


def grads_call(depth, vocab_size, table_low, targets, weights, top, total, expo):
    blocks, rows, shard = expo.shape
    width = table_low.shape[1]
    return pl.pallas_call(
        functools.partial(grads_kernel, depth, vocab_size),
        out_shape=(
            jax.ShapeDtypeStruct((rows, width), F32),
            jax.ShapeDtypeStruct((blocks, rows, shard), BF),
        ),
        in_specs=[vspec(), vspec(), vspec(), vspec(), vspec(), aspec()],
        out_specs=(vspec(), aspec()),
        scratch_shapes=[
            VMEM((2, rows, shard), BF),
            VMEM((2, rows, shard), BF),
            pltpu.SemaphoreType.DMA((2,)),
            pltpu.SemaphoreType.DMA((2,)),
        ]
        + reduce_scratch(rows, width),
        compiler_params=comm_params(3),
        name="grads_exchange",
    )(table_low, targets, weights, top, total, expo)


def scatter_kernel(
    depth, rows, sent_ref, ids_ref, grads_ref, hidden_ref, out_ref, pos_ref, rest_ref, square_ref,
    left, right, left_sem, right_sem, land, *scratch
):
    out_ref[...] = jnp.zeros(out_ref.shape, F32)
    shard = out_ref.shape[0]

    def fetch(slot, block):
        top = pl.ds(0, rows)
        return (
            pltpu.make_async_copy(grads_ref.at[block], left.at[slot, top, :], left_sem.at[slot]),
            pltpu.make_async_copy(hidden_ref.at[block], right.at[slot, top, :], right_sem.at[slot]),
        )

    for copy in fetch(0, 0):
        copy.start()

    def consume(block, number):
        slot = number % 2
        for copy in fetch(slot, number):
            copy.wait()

        @pl.when(number + 1 < land.shape[0])
        def _():
            for copy in fetch(1 - slot, number + 1):
                copy.start()

        vocab = lax.broadcasted_iota(jnp.int32, (rows, shard), 1).astype(F32)
        onehot = (vocab == to_column(ids_ref[block])).astype(F32).astype(BF)
        left[slot, rows:, :] = onehot
        right[slot, rows:, :] = land[block, :rows, :]
        out_ref[...] += contract_rows(left[slot], right[slot])

    gather_blocks(sent_ref, land, scratch, consume)
    dp = lax.axis_index("dp")
    slots = 2 * depth
    span = pos_ref.shape[0]
    per = rows // span
    total = jnp.zeros(pos_ref.shape, F32)
    rest = jnp.zeros(rest_ref.shape, F32)
    first = pl.multiple_of((dp % per) * span, span)
    for slot in range(slots):
        total = total + land[slot * 4 + dp // per, pl.ds(first, span), :].astype(F32)
    pos_ref[...] = total
    for block in range(land.shape[0]):
        rest = rest + land[block, rows:, :].astype(F32)
    rest_ref[...] = rest
    square_ref[...] = jnp.zeros(square_ref.shape, F32) + jnp.sum(out_ref[...] * out_ref[...])


def scatter_call(depth, sent, ids, grads, hidden_all, span):
    blocks, unused, rows = ids.shape
    extended, width = sent.shape
    shard = grads.shape[2]
    return pl.pallas_call(
        functools.partial(scatter_kernel, depth, rows),
        out_shape=(
            jax.ShapeDtypeStruct((shard, width), F32),
            jax.ShapeDtypeStruct((span, width), F32),
            jax.ShapeDtypeStruct((extended - rows, width), F32),
            jax.ShapeDtypeStruct((8, 128), F32),
        ),
        in_specs=[vspec(), vspec(), aspec(), aspec()],
        out_specs=(vspec(),) * 4,
        scratch_shapes=[
            VMEM((2, 2 * rows, shard), BF),
            VMEM((2, 2 * rows, width), BF),
            pltpu.SemaphoreType.DMA((2,)),
            pltpu.SemaphoreType.DMA((2,)),
            VMEM((blocks, extended, width), BF),
        ]
        + gather_scratch(),
        compiler_params=comm_params(4),
        name="rows_exchange",
    )(sent, ids, grads, hidden_all)


class Group:
    def __init__(self, send_sem, recv_sem, sums=()):
        self.z, self.x, self.y, self.c = place()
        self.y_peer = device(self.z, self.x, 1 - self.y, self.c)
        self.c_peer = device(self.z, self.x, self.y, 1 - self.c)
        self.sems = send_sem, recv_sem
        self.used = 0
        self.sums = sums
        self.me = self.y * 2 + self.c

    def copy(self, src, dst, peer):
        number = self.used
        self.used += 1
        return remote(src, dst, self.sems[0].at[number], self.sems[1].at[number], peer)

    def pair(self, across, first, consume):
        row = flip(self.y, across)

        def one(m, carry):
            i = flip(m, first)
            consume(row * 2 + flip(self.c, i), i)
            return carry

        lax.fori_loop(0, 2, one, 0)

    def gather(self, land, consume, between=None):
        own, there = land.at[self.me], land.at[(1 - self.y) * 2 + self.c]
        to_y, to_c = self.copy(own, own, self.y_peer), self.copy(own, own, self.c_peer)
        on = self.copy(there, there, self.c_peer)
        to_y.start()
        to_c.start()

        def near(block, i):
            @pl.when(i == 1)
            def _():
                to_c.wait_recv()

            consume(block, i, 0)

        def far(block, i):
            @pl.when(i == 1)
            def _():
                on.wait_recv()

            consume(block, i, 1)

        if between is not None:
            between()
        self.pair(0, 0, near)
        to_y.wait_recv()
        on.start()
        self.pair(1, 0, far)
        for copy in (to_y, to_c, on):
            copy.wait_send()


class LineGather:
    def __init__(self, depth, own_ref, land, z_send, z_recv, x_send, x_recv):
        self.z, self.x, y, c = place()
        self.depth, self.own, self.land = depth, own_ref, land
        self.sems = z_send, z_recv, x_send, x_recv
        self.ways = (device(self.z + 1, self.x, y, c), device(self.z - 1, self.x, y, c))
        self.x_peer = device(self.z, 1 - self.x, y, c)

    def peers(self):
        z, x = self.z, self.x
        along = [device((z + k) % self.depth, x, self.x_peer[1] // 2, self.x_peer[1] % 2) for k in range(1, self.depth)]
        return along + [self.x_peer]

    def block(self, stream, source):
        rows = self.own.shape[1]
        first = pl.multiple_of((source * 2 + self.x) * rows, rows)
        return self.land.at[stream, pl.ds(first, rows), :]

    def along(self, stream, source, way, own=False):
        block = self.block(stream, source)
        number = stream * self.depth + source
        src = self.own.at[stream] if own else block
        z_send, z_recv = self.sems[:2]
        return remote(src, block, z_send.at[number * 2 + way], z_recv.at[number], self.ways[way])

    def across(self, stream, source, own=False):
        block = self.block(stream, source)
        number = stream * self.depth + source
        src = self.own.at[stream] if own else block
        return remote(src, block, self.sems[2].at[number], self.sems[3].at[number], self.x_peer)

    def moves_on(self, way):
        return self.z < self.depth - 1 if way == 0 else self.z > 0

    def start(self):
        for stream in range(2):
            for way in range(2):

                @pl.when(self.moves_on(way))
                def _():
                    self.along(stream, self.z, way, True).start()

            self.across(stream, self.z, True).start()
            rows = self.own.shape[1]
            first = pl.multiple_of((self.z * 2 + self.x) * rows, rows)
            self.land[stream, pl.ds(first, rows), :] = self.own[stream]

    def serve(self, stream, distance):
        for way in range(2):
            source = self.z - distance if way == 0 else self.z + distance

            @pl.when(source >= 0 if way == 0 else source < self.depth)
            def _():
                self.along(stream, source, way).wait_recv()

                @pl.when(self.moves_on(way))
                def _():
                    self.along(stream, source, way).start()

                self.across(stream, source).start()

    def finish(self, stream):
        for source in range(self.depth):
            self.across(stream, source).wait_recv()

    def drain(self):
        for stream in range(2):
            for source in range(self.depth):
                self.across(stream, source).wait_send()

                @pl.when((source <= self.z) & self.moves_on(0))
                def _():
                    self.along(stream, source, 0).wait_send()

                @pl.when((source >= self.z) & self.moves_on(1))
                def _():
                    self.along(stream, source, 1).wait_send()


class GroupSum:
    def __init__(self, group, number):
        self.group = group
        keep, mine, theirs, mixed, arrived = group.sums
        self.keep = [keep.at[0], keep.at[1]]
        self.mine = [mine.at[number, 0], mine.at[number, 1]]
        self.theirs = [theirs.at[number, 0], theirs.at[number, 1]]
        self.mixed, self.arrived = mixed.at[number], arrived.at[number]
        self.to_core = [group.copy(self.mine[i], self.theirs[i], group.c_peer) for i in range(2)]
        self.to_across = group.copy(self.mixed, self.arrived, group.y_peer)

    def add(self, part, i, side):
        @pl.when(i == 0)
        def _():
            self.keep[side][...] = part

        @pl.when(i == 1)
        def _():
            self.mine[side][...] = part.astype(BF)
            self.to_core[side].start()

    def pass_on(self):
        self.to_core[1].wait_recv()
        self.mixed[...] = (self.keep[1][...] + self.theirs[1][...].astype(F32)).astype(BF)
        self.to_across.start()

    def finish(self):
        self.to_core[0].wait_recv()
        total = self.keep[0][...] + self.theirs[0][...].astype(F32)
        self.to_across.wait_recv()
        total = total + self.arrived[...].astype(F32)
        for copy in self.to_core + [self.to_across]:
            copy.wait_send()
        return total


def group_scratch(rows, width):
    return [
        VMEM((2, rows, width), F32),
        VMEM((2, 2, rows, width), BF),
        VMEM((2, 2, rows, width), BF),
        VMEM((2, rows, width), BF),
        VMEM((2, rows, width), BF),
        pltpu.SemaphoreType.DMA((12,)),
        pltpu.SemaphoreType.DMA((12,)),
    ]


def flat(values):
    return values.reshape(-1, values.shape[-1])


def head_mask(head, columns, value):
    lane = lax.broadcasted_iota(jnp.int32, (1, columns), 1)
    return jnp.where(lane // HD == head, value, 0.0).astype(BF)


def score_bias(block, length_row, seq_len):
    shape = (seq_len, length_row.shape[1])
    key = lax.broadcasted_iota(jnp.int32, shape, 0)
    query = lax.broadcasted_iota(jnp.int32, shape, 1) + block * length_row.shape[1]
    allowed = (key <= query) & (key.astype(F32) < length_row)
    return jnp.where(allowed, 0.0, -1e30)


def columns_of(values, heads):
    return jnp.transpose(values.astype(F32)).astype(BF).reshape(heads, HD, -1)


def forward_kernel(
    depth, start_ref, gains_ref, length_ref, own_mlp_ref, attn_hbm,
    mlp_hbm, normed_one_hbm, members_hbm, attended_hbm, logs_ref, middle_ref, normed_two_hbm, pre_hbm, act_hbm,
    last_ref, hidden_ref,
    weights, attn, normed_one, members, value_cols, attended, att_cols, bias, normed_two, pre, act,
    load_sem, store_sem, z_send, z_recv, x_send, x_recv, *scratch
):
    group = Group(scratch[5], scratch[6], scratch[:5])
    line = LineGather(depth, own_mlp_ref, weights, z_send, z_recv, x_send, x_recv)
    load = pltpu.make_async_copy(attn_hbm, attn, load_sem.at[0])
    load.start()
    greet([group.y_peer, group.c_peer] + line.peers())
    line.start()
    normed_one[group.me] = layer_norm(start_ref[...], gains_ref[0:1], gains_ref[1:2]).astype(BF)
    blocks, rows, unused = normed_one.shape
    cols = members.shape[3]
    heads = cols // HD
    stores = []

    def store(src, dst):
        stores.append(pltpu.make_async_copy(src, dst, store_sem.at[len(stores)]))
        stores[-1].start()

    def project(block, i, side):
        out = dot_nn(normed_one[block], attn[:, : 3 * cols])
        for m in range(3):
            members[m, block] = out[:, m * cols : (m + 1) * cols].astype(BF)

    load.wait()
    group.gather(normed_one, project, lambda: line.serve(0, 1))
    line.serve(1, 1)
    store(normed_one, normed_one_hbm)
    store(members, members_hbm)
    value_cols[...] = columns_of(flat(members[2]), heads)
    sums = GroupSum(group, 0)

    def attend(block, i, side):
        bias[...] = score_bias(block, length_ref[...], blocks * rows)

        def head(h, carry):
            queries = members[0, block] * head_mask(h, cols, HD ** (-0.5))
            scores = contract_cols(flat(members[1]), queries) + bias[...]
            top = jnp.max(scores, axis=0, keepdims=True)
            expo = jnp.exp(scores - top)
            total = jnp.sum(expo, axis=0, keepdims=True)
            probs = (expo * (1.0 / total)).astype(BF)
            att_cols[h] = dot_nn(value_cols[h], probs)
            logs_ref[h, block] = top + jnp.log(total)
            return carry

        lax.fori_loop(0, heads, head, 0)
        rows_out = jnp.transpose(flat(att_cols[...])).astype(BF)
        attended[block] = rows_out
        sums.add(contract_cols(rows_out, attn[:, 3 * cols :]), i, side)

    group.pair(1, 1, lambda block, i: attend(block, i, 1))
    sums.pass_on()
    for stream in range(2):
        line.serve(stream, 2)
    group.pair(0, 1, lambda block, i: attend(block, i, 0))
    for stream in range(2):
        line.serve(stream, 3)
    store(attended, attended_hbm)
    middle = start_ref[...] + sums.finish()
    middle_ref[...] = middle
    normed_two[group.me] = layer_norm(middle, gains_ref[2:3], gains_ref[3:4]).astype(BF)
    again = GroupSum(group, 1)

    def feed(block, i, side):
        units = dot_nn(normed_two[block], weights[0])
        pre[block] = units
        active = gelu_tanh(units).astype(BF)
        act[block] = active
        again.add(contract_cols(active, weights[1]), i, side)

    def weights_here():
        for stream in range(2):
            line.finish(stream)
        store(weights, mlp_hbm)

    group.gather(normed_two, feed, weights_here)
    again.pass_on()
    store(normed_two, normed_two_hbm)
    store(pre, pre_hbm)
    store(act, act_hbm)
    last = middle_ref[...] + again.finish()
    last_ref[...] = last
    hidden_ref[...] = layer_norm(last, gains_ref[4:5], gains_ref[5:6]).astype(BF)
    line.drain()
    for copy in stores:
        copy.wait()


def forward_call(depth, start_rows, gains, length, attn, own_mlp):
    rows, width = start_rows.shape
    hidden_units = own_mlp.shape[2]
    line_sems = [pltpu.SemaphoreType.DMA((n * depth,)) for n in (4, 2, 2, 2)]
    cols = hidden_units // 4
    heads = cols // HD
    gathered = (4, rows, width)
    units = (4, rows, hidden_units)

    def shape(dims, kind):
        return jax.ShapeDtypeStruct(dims, kind)

    return pl.pallas_call(
        functools.partial(forward_kernel, depth),
        out_shape=(
            shape((2, width, hidden_units), BF),
            shape(gathered, BF),
            shape((3, 4, rows, cols), BF),
            shape((4, rows, cols), BF),
            shape((heads, 4, 1, rows), F32),
            shape((rows, width), F32),
            shape(gathered, BF),
            shape(units, F32),
            shape(units, BF),
            shape((rows, width), F32),
            shape((rows, width), BF),
        ),
        in_specs=[vspec(), vspec(), vspec(), vspec(), aspec()],
        out_specs=(
            aspec(), aspec(), aspec(), aspec(), vspec(), vspec(), aspec(), aspec(), aspec(), vspec(), vspec(),
        ),
        scratch_shapes=[
            VMEM((2, width, hidden_units), BF),
            VMEM((width, hidden_units), BF),
            VMEM(gathered, BF),
            VMEM((3, 4, rows, cols), BF),
            VMEM((heads, HD, 4 * rows), BF),
            VMEM((4, rows, cols), BF),
            VMEM((heads, HD, rows), F32),
            VMEM((4 * rows, rows), F32),
            VMEM(gathered, BF),
            VMEM(units, F32),
            VMEM(units, BF),
            pltpu.SemaphoreType.DMA((1,)),
            pltpu.SemaphoreType.DMA((7,)),
        ]
        + line_sems
        + group_scratch(rows, width),
        compiler_params=comm_params(7),
        name="layer_forward",
    )(start_rows, gains, length, own_mlp, attn)


def norm_back(values, gain_row, cotangent):
    centered = values - jnp.mean(values, axis=-1, keepdims=True)
    scale = lax.rsqrt(jnp.mean(centered * centered, axis=-1, keepdims=True) + 1e-05)
    normed = centered * scale
    weighted = cotangent * gain_row
    first = jnp.mean(weighted, axis=-1, keepdims=True)
    second = jnp.mean(weighted * normed, axis=-1, keepdims=True)
    grad = (weighted - first - normed * second) * scale
    gain = jnp.sum(cotangent * normed, axis=0, keepdims=True)
    return grad, gain, jnp.sum(cotangent, axis=0, keepdims=True)


def gelu_slope(values):
    root, cube = 0.7978845608028654, 0.044715
    square = values * values
    bent = jnp.tanh(root * (values + cube * values * square))
    return 0.5 * (1.0 + bent) + 0.5 * values * (1.0 - bent * bent) * root * (1.0 + 3.0 * cube * square)


def backward_kernel(
    grad_ref, start_ref, middle_ref, last_ref, gains_ref, length_ref, logs_ref,
    weights_hbm, attn_hbm, normed_one_hbm, members_hbm, attended_hbm, normed_two_hbm, pre_hbm, act_hbm,
    out_ref, norms_ref, weight_grads_hbm,
    weights, normed_one, members, attended, normed_two, pre, act,
    grad_last, grad_low, grad_pre, key_cols, query_cols, bias, key_grad, value_grad, grad_mid, grad_att, member_grads,
    weight_grads, load_sem, store_sem, *scratch
):
    group = Group(scratch[5], scratch[6], scratch[:5])
    sources = (
        (weights_hbm.at[1], weights.at[1]),
        (pre_hbm, pre),
        (weights_hbm.at[0], weights.at[0]),
        (act_hbm, act),
        (normed_two_hbm, normed_two),
        (attn_hbm, weights.at[2]),
        (members_hbm, members),
        (normed_one_hbm, normed_one),
        (attended_hbm, attended),
    )
    loads = [
        pltpu.make_async_copy(src, dst, load_sem.at[n]) for n, (src, dst) in enumerate(sources)
    ]
    for copy in loads:
        copy.start()
    blocks, rows, width = grad_low.shape
    cols = attended.shape[2]
    heads = cols // HD
    grad, gain, shift = norm_back(last_ref[...], gains_ref[4:5], grad_ref[...])
    grad_last[...] = grad
    norms_ref[4:5] = gain
    norms_ref[5:6] = shift
    grad_low[group.me] = grad.astype(BF)
    greet([group.y_peer, group.c_peer])
    sums = GroupSum(group, 0)

    def feed(block, i, side):
        active = dot_nn(grad_low[block], weights[1])
        low = (active * gelu_slope(pre[block])).astype(BF)
        grad_pre[block] = low
        sums.add(contract_cols(low, weights[0]), i, side)

    for copy in loads[:3]:
        copy.wait()
    group.gather(grad_low, feed)
    sums.pass_on()
    for copy in loads[3:]:
        copy.wait()

    def chunk(ref, j):
        return flat(ref[:, :, pl.ds(pl.multiple_of(j * rows, rows), rows)])

    def place_of(j):
        return pl.ds(pl.multiple_of(j * rows, rows), rows)

    def mlp_grads(j, carry):
        weight_grads[0, place_of(j), :] = contract_rows(chunk(normed_two, j), flat(grad_pre[...])).astype(BF)
        weight_grads[1, place_of(j), :] = contract_rows(chunk(grad_low, j), flat(act[...])).astype(BF)
        return carry

    lax.fori_loop(0, width // rows, mlp_grads, 0)
    grad, gain, shift = norm_back(middle_ref[...], gains_ref[2:3], sums.finish())
    norms_ref[2:3] = gain
    norms_ref[3:4] = shift
    grad = grad + grad_last[...]
    grad_last[...] = grad
    grad_mid[group.me] = grad.astype(BF)
    key_cols[...] = columns_of(flat(members[1]), heads)
    key_grad[...] = jnp.zeros(key_grad.shape, F32)
    value_grad[...] = jnp.zeros(value_grad.shape, F32)

    def attend(block, i, side):
        grad_att[block] = dot_nn(grad_mid[block], weights[2, :, 3 * cols :]).astype(BF)
        bias[...] = score_bias(block, length_ref[...], blocks * rows)

        def head(h, carry):
            queries = members[0, block] * head_mask(h, cols, HD ** (-0.5))
            grads = grad_att[block] * head_mask(h, cols, 1.0)
            scores = contract_cols(flat(members[1]), queries) + bias[...]
            probs = jnp.exp(scores - logs_ref[h, block])
            grad_probs = contract_cols(flat(members[2]), grads)
            inner = jnp.sum(grad_probs * probs, axis=0, keepdims=True)
            grad_scores = (probs * (grad_probs - inner)).astype(BF)
            key_grad[...] += dot_nn(grad_scores, queries)
            value_grad[...] += dot_nn(probs.astype(BF), grads)
            query_cols[h] = dot_nn(key_cols[h], grad_scores)
            return carry

        lax.fori_loop(0, heads, head, 0)
        turned = jnp.transpose(flat(query_cols[...])) * HD ** (-0.5)
        member_grads[block, :, :cols] = turned.astype(BF)

    group.gather(grad_mid, attend)
    split = (blocks, rows, cols)
    member_grads[:, :, cols : 2 * cols] = key_grad[...].astype(BF).reshape(split)
    member_grads[:, :, 2 * cols :] = value_grad[...].astype(BF).reshape(split)
    again = GroupSum(group, 1)

    def back(block, i, side):
        again.add(contract_cols(member_grads[block], weights[2, :, : 3 * cols]), i, side)

    group.pair(1, 1, lambda block, i: back(block, i, 1))
    again.pass_on()
    group.pair(0, 1, lambda block, i: back(block, i, 0))

    def attn_grads(j, carry):
        weight_grads[2, place_of(j), : 3 * cols] = contract_rows(
            chunk(normed_one, j), flat(member_grads[...])
        ).astype(BF)
        weight_grads[2, place_of(j), 3 * cols :] = contract_rows(
            chunk(grad_mid, j), flat(attended[...])
        ).astype(BF)
        return carry

    lax.fori_loop(0, width // rows, attn_grads, 0)
    store = pltpu.make_async_copy(weight_grads, weight_grads_hbm, store_sem.at[0])
    store.start()
    grad, gain, shift = norm_back(start_ref[...], gains_ref[0:1], again.finish())
    norms_ref[0:1] = gain
    norms_ref[1:2] = shift
    out_ref[...] = grad_last[...] + grad
    store.wait()


def backward_call(grad_hidden, start_rows, middle, last_rows, gains, length, logs, mlp, attn, kept):
    rows, width = start_rows.shape
    hidden_units = mlp.shape[2]
    cols = hidden_units // 4
    heads = cols // HD
    gathered = (4, rows, width)
    units = (4, rows, hidden_units)
    stack = (3, width, hidden_units)
    return pl.pallas_call(
        backward_kernel,
        out_shape=(
            jax.ShapeDtypeStruct((rows, width), F32),
            jax.ShapeDtypeStruct((6, width), F32),
            jax.ShapeDtypeStruct(stack, BF),
        ),
        in_specs=[vspec()] * 7 + [aspec()] * 8,
        out_specs=(vspec(), vspec(), aspec()),
        scratch_shapes=[
            VMEM(stack, BF),
            VMEM(gathered, BF),
            VMEM((3, 4, rows, cols), BF),
            VMEM((4, rows, cols), BF),
            VMEM(gathered, BF),
            VMEM(units, F32),
            VMEM(units, BF),
            VMEM((rows, width), F32),
            VMEM(gathered, BF),
            VMEM(units, BF),
            VMEM((heads, HD, 4 * rows), BF),
            VMEM((heads, HD, rows), F32),
            VMEM((4 * rows, rows), F32),
            VMEM((4 * rows, cols), F32),
            VMEM((4 * rows, cols), F32),
            VMEM(gathered, BF),
            VMEM((4, rows, cols), BF),
            VMEM((4, rows, 3 * cols), BF),
            VMEM(stack, BF),
            pltpu.SemaphoreType.DMA((9,)),
            pltpu.SemaphoreType.DMA((1,)),
        ]
        + group_scratch(rows, width),
        compiler_params=comm_params(8),
        name="layer_backward",
    )(grad_hidden, start_rows, middle, last_rows, gains, length, logs, mlp, attn, *kept)


def small_gather_kernel(depth, ints_ref, norms_ref, ints_out, norms_out, ss, rs, ns, nr):
    z, x, y, c = place()
    dp = lax.axis_index("dp")
    mp = lax.axis_index("mp")
    count = 2 * depth
    peers = [((dp + k) % count, mp) for k in range(1, count)]
    greet(peers)
    ints_out[dp] = ints_ref[...]
    norms_out[dp] = norms_ref[...]
    copies = []
    for k, peer in enumerate(peers):
        copies.append(remote(ints_ref, ints_out.at[dp], ss.at[k], rs.at[k], peer))
        copies.append(remote(norms_ref, norms_out.at[dp], ns.at[k], nr.at[k], peer))
    for copy in copies:
        copy.start()
    for copy in copies:
        copy.wait()


def small_gather(depth, ints, norms):
    count = 2 * depth
    return pl.pallas_call(
        functools.partial(small_gather_kernel, depth),
        out_shape=(
            jax.ShapeDtypeStruct((count, *ints.shape), ints.dtype),
            jax.ShapeDtypeStruct((count, *norms.shape), norms.dtype),
        ),
        in_specs=[vspec(), vspec()],
        out_specs=(vspec(), vspec()),
        scratch_shapes=[pltpu.SemaphoreType.DMA((count - 1,))] * 4,
        compiler_params=comm_params(5, 8),
        name="small_gather",
    )(ints, norms)


def scalar_sum_kernel(depth, repeats, own_ref, share_ref, spots_ref, norms_ref, out_ref, snap, got, ss, rs):
    z, x, y, c = place()
    peers = [device(z, flip(x, n // 4), flip(y, n // 2 % 2), flip(c, n % 2)) for n in range(1, 8)]
    z_peers = [device((z + k) % depth, x, y, c) for k in range(1, depth)]
    share = share_ref[...].astype(F32)
    copied = jnp.sum(spots_ref[...] * spots_ref[...]) + jnp.sum(norms_ref[...] * norms_ref[...])
    squares = jnp.sum(share * share) + copied * (1.0 / repeats)
    row = lax.broadcasted_iota(jnp.int32, own_ref.shape, 0)
    snap[0] = own_ref[...] + jnp.where(row == 0, squares, 0.0)
    greet(peers + z_peers)
    me = x * 4 + y * 2 + c
    copies = [
        remote(snap.at[0], got.at[me], ss.at[n], rs.at[n], peer) for n, peer in enumerate(peers)
    ]
    for copy in copies:
        copy.start()
    got[me] = snap[0]
    for copy in copies:
        copy.wait()
    total = got[0]
    for n in range(1, 8):
        total = total + got[n]
    snap[1] = total
    copies = [
        remote(snap.at[1], got.at[8 + z], ss.at[7 + k], rs.at[7 + k], peer)
        for k, peer in enumerate(z_peers)
    ]
    for copy in copies:
        copy.start()
    got[8 + z] = snap[1]
    for copy in copies:
        copy.wait()
    total = got[8]
    for k in range(1, depth):
        total = total + got[8 + k]
    out_ref[...] = total


def scalar_sum(depth, repeats, values, share, spots, norms):
    return pl.pallas_call(
        functools.partial(scalar_sum_kernel, depth, repeats),
        out_shape=jax.ShapeDtypeStruct(values.shape, F32),
        in_specs=[vspec()] * 4,
        out_specs=vspec(),
        scratch_shapes=[
            VMEM((2, *values.shape), F32),
            VMEM((8 + depth, *values.shape), F32),
            pltpu.SemaphoreType.DMA((6 + depth,)),
            pltpu.SemaphoreType.DMA((6 + depth,)),
        ],
        compiler_params=comm_params(6, 16),
        name="scalar_sum",
    )(values, share, spots, norms)


class KernelMoves:
    def __init__(self, depth):
        self.depth = depth

    def small(self, token_ids, target_ids, mask, norms):
        packed = jnp.concatenate([v.reshape(-1, 128) for v in (token_ids, target_ids, mask)], axis=0)
        each = packed.shape[0] // 3
        low = jnp.pad(norms.astype(BF), ((0, 16 - norms.shape[0]), (0, 0)))
        ints, norms_all = small_gather(self.depth, packed, low)
        norms_all = jnp.transpose(norms_all, (1, 0, 2)).reshape(16, -1)[: norms.shape[0]]
        return [ints[:, i * each : (i + 1) * each].reshape(-1) for i in range(3)] + [norms_all]

    def embed(self, table_low, local_ids, rows, positions, first_row):
        ids = local_ids.astype(F32).reshape(-1, 1, rows)
        return embed_call(self.depth, table_low, ids, positions.astype(BF))

    def weights(self, attn_in, attn_out, mlp_in, mlp_out):
        attn = jnp.concatenate([attn_in[0], attn_in[1], attn_in[2], attn_out], axis=1)
        gathered = lax.all_gather(attn.astype(BF), "dp", axis=0, tiled=True)
        return gathered, jnp.stack([mlp_in, mlp_out]).astype(BF)

    def forward(self, start_rows, gains, length, weights):
        row = jnp.full((1, start_rows.shape[0]), length.astype(F32))
        attn, own_mlp = weights
        mlp, normed_one, members, attended, logs, middle, normed_two, pre, act, last_rows, hidden = (
            forward_call(self.depth, start_rows, gains, row, attn, own_mlp)
        )
        kept = (normed_one, members, attended, normed_two, pre, act)
        return hidden, (start_rows, middle, last_rows, gains, row, logs, mlp, attn, kept)

    def backward(self, grad_hidden, saved):
        grad_start, norms_grad, grads = backward_call(grad_hidden, *saved)
        low = lax.psum_scatter(grads, "dp", scatter_dimension=1, tiled=True)
        share = low.astype(F32)
        cols = share.shape[2] // 4
        attn = jnp.stack([share[2, :, i * cols : (i + 1) * cols] for i in range(4)])
        return grad_start, norms_grad, attn, share[:2], low

    def head(self, hidden, table_low, targets, weights, vocab_size):
        rows = hidden.shape[0]
        targets = targets.astype(F32).reshape(-1, 1, rows)
        weights = weights.reshape(-1, 1, rows)
        hidden_all, expo, top, total, picked = logits_call(
            self.depth, vocab_size, hidden, table_low, targets
        )
        grad_hidden, grads = grads_call(
            self.depth, vocab_size, table_low, targets, weights, top, total, expo
        )
        weights = weights.reshape(-1)
        first = (lax.axis_index("dp") * lax.axis_size("mp") + lax.axis_index("mp")) * rows
        own_logs = lax.dynamic_slice(total.reshape(-1), (first,), (rows,))
        log_sum = jnp.sum(own_logs * lax.dynamic_slice(weights, (first,), (rows,)))
        loss_part = log_sum - jnp.sum(picked.reshape(-1) * weights)
        return grad_hidden, (grads, hidden_all), loss_part

    def scatter(self, grad_start, norms_grad, local_ids, table_grad, span):
        rows = grad_start.shape[0]
        count = norms_grad.shape[0]
        rest = jnp.pad(norms_grad, ((0, 16 - count), (0, 0)))
        sent = jnp.concatenate([grad_start, rest], axis=0).astype(BF)
        ids = local_ids.astype(F32).reshape(-1, 1, rows)
        grads, hidden_all = table_grad
        table_grad, positions_grad, rest, square = scatter_call(
            self.depth, sent, ids, grads, hidden_all, span
        )
        dp = lax.axis_index("dp")
        part = rest.shape[1] // lax.axis_size("dp")
        norms_part = lax.dynamic_slice(rest, (0, dp * part), (16, part))[:count]
        return table_grad, positions_grad, norms_part, square[0, 0]

    def total(self, table_square, loss_part, share, spots, norms):
        row = jnp.concatenate([jnp.full((1, 128), v, F32) for v in (table_square, loss_part)], axis=0)
        row = jnp.pad(row, ((0, 6), (0, 0)))
        summed = scalar_sum(self.depth, lax.axis_size("mp"), row, share, spots, norms)
        return summed[0, 0], summed[1, 0]


class PlainMoves:
    parts = 4

    def split(self, values, rows):
        piece = rows // self.parts
        return jnp.swapaxes(values.reshape(-1, self.parts, piece), 0, 1).reshape(self.parts, -1)

    def small(self, token_ids, target_ids, mask, norms):
        found = [lax.all_gather(v.reshape(-1), "dp", tiled=True) for v in (token_ids, target_ids, mask)]
        return found + [lax.all_gather(norms.astype(BF), "dp", axis=1, tiled=True)]

    def embed(self, table_low, local_ids, rows, positions, first_row):
        positions_all = lax.all_gather(positions.astype(BF), "dp", axis=0, tiled=True)
        own_positions = lax.dynamic_slice(positions_all, (first_row, 0), (rows, positions.shape[1]))

        def one(ids):
            looked = jnp.take(table_low, jnp.maximum(ids, 0), axis=0)
            looked = jnp.where(ids[:, None] >= 0, looked, jnp.zeros((), BF))
            return lax.psum_scatter(looked, ("dp", "mp"), tiled=True)

        embedded = lax.map(one, self.split(local_ids, rows)).reshape(rows, -1)
        return embedded.astype(F32) + own_positions.astype(F32)

    def gather_group(self, own):
        return lax.all_gather(own, "mp", tiled=True)

    def sum_group(self, parts):
        return lax.psum_scatter(parts, "mp", tiled=True)

    def weights(self, attn_in, attn_out, mlp_in, mlp_out):
        attn_pack = jnp.concatenate([attn_in, attn_out[None]], axis=0).astype(BF)
        mlp_pack = jnp.stack([mlp_in, mlp_out]).astype(BF)
        attn_all = lax.all_gather(attn_pack, "dp", axis=1, tiled=True)
        mlp_all = lax.all_gather(mlp_pack, "dp", axis=1, tiled=True)
        return attn_all, mlp_all

    def forward(self, start_rows, gains, length, weights):
        attn_all, mlp_all = weights
        normed_one = self.gather_group(layer_norm(start_rows, gains[0], gains[1]).astype(BF))
        seq_len = normed_one.shape[0]
        head_shape = (seq_len, attn_all.shape[2] // HD, HD)
        queries, keys, values = (dot_nn(normed_one, attn_all[i]).astype(BF) for i in range(3))
        heads = [v.reshape(head_shape) for v in (queries, keys, values)]
        attended, log_total = attend_forward(*heads, length)
        attended = attended.reshape(seq_len, -1)
        middle = start_rows + self.sum_group(contract_cols(attended, attn_all[3]))
        normed_two = self.gather_group(layer_norm(middle, gains[2], gains[3]).astype(BF))
        pre_gelu = dot_nn(normed_two, mlp_all[0])
        activated = gelu_tanh(pre_gelu).astype(BF)
        last_rows = middle + self.sum_group(contract_cols(activated, mlp_all[1]))
        hidden = layer_norm(last_rows, gains[4], gains[5]).astype(BF)
        return hidden, (
            start_rows, middle, last_rows, gains, length, weights, normed_one, heads, attended, log_total,
            normed_two, pre_gelu, activated,
        )

    def backward(self, grad_hidden, saved):
        (
            start_rows, middle, last_rows, gains, length, weights, normed_one, heads, attended, log_total,
            normed_two, pre_gelu, activated,
        ) = saved
        attn_all, mlp_all = weights
        grad_last, gain_three, shift_three = norm_back(last_rows, gains[4], grad_hidden)
        grad_last_low = self.gather_group(grad_last.astype(BF))
        mlp_out_grad = contract_rows(grad_last_low, activated)
        grad_activated = dot_nn(grad_last_low, mlp_all[1])
        grad_pre = (grad_activated * gelu_slope(pre_gelu)).astype(BF)
        mlp_in_grad = contract_rows(normed_two, grad_pre)
        grad_normed_two = self.sum_group(contract_cols(grad_pre, mlp_all[0]))
        mlp_share = lax.psum_scatter(
            jnp.stack([mlp_in_grad, mlp_out_grad]).astype(BF), "dp", scatter_dimension=1, tiled=True
        ).astype(F32)
        grad_from_two, gain_two, shift_two = norm_back(middle, gains[2], grad_normed_two)
        grad_middle = grad_last + grad_from_two
        grad_middle_low = self.gather_group(grad_middle.astype(BF))
        attn_out_grad = contract_rows(grad_middle_low, attended)
        grad_attended = dot_nn(grad_middle_low, attn_all[3]).astype(BF).reshape(heads[0].shape)
        members = [
            v.reshape(attended.shape)
            for v in attend_backward(*heads, length, log_total, grad_attended)
        ]
        attn_grads = [contract_rows(normed_one, v) for v in members] + [attn_out_grad]
        grad_normed_one = self.sum_group(
            sum(contract_cols(members[i], attn_all[i]) for i in range(3))
        )
        attn_share = lax.psum_scatter(
            jnp.stack(attn_grads).astype(BF), "dp", scatter_dimension=1, tiled=True
        ).astype(F32)
        grad_from_one, gain_one, shift_one = norm_back(start_rows, gains[0], grad_normed_one)
        rows_of = (gain_one, shift_one, gain_two, shift_two, gain_three, shift_three)
        shares = (attn_share, mlp_share)
        return grad_middle + grad_from_one, jnp.concatenate(rows_of), attn_share, mlp_share, shares

    def head(self, hidden, table_low, targets, weights, vocab_size):
        rows, width = hidden.shape
        shard = table_low.shape[0]

        def one(carried, packed):
            own, ids, weight = packed
            table_grad, loss_part = carried
            hidden_all = lax.all_gather(own, ("dp", "mp"), tiled=True)
            logits = contract_cols(hidden_all, table_low)
            top = lax.pmax(jnp.max(logits, axis=1), ("dp", "mp"))
            onehot = jnp.arange(shard)[None, :] == ids[:, None]
            picked = jnp.sum(logits * jnp.where(onehot, 1.0 - smoothing + even, even), axis=1)
            total = lax.psum(jnp.sum(jnp.exp(logits - top[:, None]), axis=1), ("dp", "mp"))
            total = top + jnp.log(total)
            grads = jnp.exp(logits - total[:, None]) - jnp.where(onehot, 1.0 - smoothing, 0.0)
            grads = ((grads - even) * weight[:, None]).astype(BF)
            partial = dot_nn(grads, table_low).astype(BF)
            grad_hidden = lax.psum_scatter(partial, ("dp", "mp"), tiled=True).astype(F32)
            table_grad = table_grad + contract_rows(grads, hidden_all)
            return (table_grad, loss_part + jnp.sum((total / devices - picked) * weight)), grad_hidden

        even = smoothing / vocab_size
        devices = lax.axis_size("dp") * lax.axis_size("mp")
        first = (jnp.zeros((shard, width), F32), jnp.zeros((), F32))
        own = hidden.reshape(self.parts, rows // self.parts, width)
        (table_grad, loss_part), grad_hidden = lax.scan(
            one, first, (own, self.split(targets, rows), self.split(weights, rows))
        )
        return grad_hidden.reshape(rows, width), table_grad, loss_part

    def scatter(self, grad_start, norms_grad, local_ids, table_grad, span):
        shard = table_grad.shape[0]
        rows, width = grad_start.shape

        def one(carried, packed):
            own, ids = packed
            everything = lax.all_gather(own, ("dp", "mp"), tiled=True).astype(F32)
            safe = jnp.where(ids >= 0, ids, shard)
            return carried + jax.ops.segment_sum(everything, safe, num_segments=shard), None

        own = grad_start.astype(BF).reshape(self.parts, rows // self.parts, width)
        table_grad, unused = lax.scan(one, table_grad, (own, self.split(local_ids, rows)))
        spread = jnp.zeros((lax.axis_size("mp") * rows, width), F32)
        spread = lax.dynamic_update_slice(spread, grad_start, (lax.axis_index("mp") * rows, 0))
        positions_grad = lax.psum(lax.psum_scatter(spread, "dp", tiled=True), "mp")
        norms_part = lax.psum(
            lax.psum_scatter(norms_grad, "dp", scatter_dimension=1, tiled=True), "mp"
        )
        return table_grad, positions_grad, norms_part, jnp.sum(table_grad * table_grad)

    def total(self, table_square, loss_part, share, spots, norms):
        squares = table_square + sum(jnp.sum(v * v) for v in share)
        squares = squares + (jnp.sum(spots * spots) + jnp.sum(norms * norms)) / lax.axis_size("mp")
        return lax.psum((squares, loss_part), ("dp", "mp"))


def attend_scores(queries, keys, length):
    scores = jnp.einsum("qhe,khe->hqk", queries, keys, preferred_element_type=F32) * HD ** (-0.5)
    place_at = jnp.arange(queries.shape[0])
    allowed = (place_at[None, :] <= place_at[:, None]) & (place_at[None, :] < length)
    return jnp.where(allowed[None], scores, -1e30)


def attend_forward(queries, keys, values, length):
    scores = attend_scores(queries, keys, length)
    top = jnp.max(scores, axis=-1, keepdims=True)
    log_total = jnp.log(jnp.sum(jnp.exp(scores - top), axis=-1, keepdims=True)) + top
    probs = jnp.exp(scores - log_total).astype(BF)
    attended = jnp.einsum("hqk,khe->qhe", probs, values, preferred_element_type=F32)
    return attended.astype(BF), log_total


def attend_backward(queries, keys, values, length, log_total, grad):
    probs = jnp.exp(attend_scores(queries, keys, length) - log_total)
    grad_values = jnp.einsum("hqk,qhe->khe", probs.astype(BF), grad, preferred_element_type=F32)
    grad_probs = jnp.einsum("qhe,khe->hqk", grad, values, preferred_element_type=F32)
    inner = jnp.sum(grad_probs * probs, axis=-1, keepdims=True)
    grad_scores = (probs * (grad_probs - inner)).astype(BF)
    scale = HD ** (-0.5)
    grad_queries = jnp.einsum("hqk,khe->qhe", grad_scores, keys, preferred_element_type=F32) * scale
    grad_keys = jnp.einsum("hqk,qhe->khe", grad_scores, queries, preferred_element_type=F32) * scale
    return grad_queries.astype(BF), grad_keys.astype(BF), grad_values.astype(BF)


def local(
    moves,
    token_ids,
    target_ids,
    loss_mask,
    lengths,
    step_count,
    *weights,
):
    masters, firsts, seconds = weights[:7], weights[7:14], weights[14:]
    table, positions, attn_in, attn_out, mlp_in, mlp_out, norms = masters
    shard = table.shape[0]
    width = table.shape[1]
    dp, mp = lax.axis_index("dp"), lax.axis_index("mp")
    dp_count, mp_count = lax.axis_size("dp"), lax.axis_size("mp")
    vocab_size = shard * dp_count * mp_count
    seq_len = token_ids.shape[1]
    rows = token_ids.size // mp_count
    table_low = table.astype(BF)
    ids_all, targets_all, mask_all, norms_all = moves.small(token_ids, target_ids, loss_mask, norms)
    gains = norms_all.astype(F32)
    mask_all = mask_all.astype(F32)
    token_total = jnp.sum(mask_all)
    row_weights = mask_all / token_total
    base = (dp * mp_count + mp) * shard

    def local_of(ids):
        inside = (ids >= base) & (ids < base + shard)
        return jnp.where(inside, ids - base, -1)

    local_ids, local_targets = local_of(ids_all), local_of(targets_all)
    layer_weights = moves.weights(attn_in, attn_out, mlp_in, mlp_out)

    first_row = (mp * rows) % seq_len
    start_rows = moves.embed(table_low, local_ids, rows, positions, first_row)
    hidden, saved = moves.forward(start_rows, gains, lengths[0], layer_weights)

    grad_hidden, table_grad, loss_part = moves.head(
        hidden, table_low, local_targets, row_weights, vocab_size
    )
    grad_start, norms_grad, attn_share, mlp_share, all_shares = moves.backward(grad_hidden, saved)
    table_grad, positions_grad, norms_part, table_square = moves.scatter(
        grad_start, norms_grad, local_ids, table_grad, positions.shape[0]
    )
    shares = (
        table_grad,
        positions_grad,
        attn_share[:3],
        attn_share[3],
        mlp_share[0],
        mlp_share[1],
        norms_part,
    )
    total_square, loss = moves.total(table_square, loss_part, all_shares, positions_grad, norms_part)
    grad_norm = jnp.sqrt(total_square)
    factor = jnp.minimum(1.0, clip_norm / (grad_norm + 1e-06))
    step_float = step_count[0].astype(F32)
    updated = [
        adam_update(
            masters[i],
            firsts[i],
            seconds[i],
            factor * shares[i],
            learn_rates[i],
            decay_rates[i],
            step_float,
        )
        for i in range(7)
    ]
    return (loss, grad_norm) + tuple(updated[i][part] for part in range(3) for i in range(7))


def fits_kernels(mesh):
    if mesh.shape["mp"] != 4 or mesh.shape["dp"] != 8:
        return False
    for (dp, mp), item in zip(
        ((i, j) for i in range(8) for j in range(4)), mesh.devices.reshape(-1)
    ):
        coords = getattr(item, "coords", None)
        if coords is not None and (tuple(coords), item.core_on_chip) != (
            (dp % 2, mp // 2, dp // 2),
            mp % 2,
        ):
            return False
    return True


def solution(mesh):
    table, rows, heads, grid, norms = (
        P(("dp", "mp"), None),
        P("dp", None),
        P(None, "dp", "mp"),
        P("dp", "mp"),
        P(None, "dp"),
    )
    each = (table, rows, heads, grid, grid, grid, norms)
    in_specs = (rows, rows, rows, P("dp"), P()) + each * 3
    out_specs = (P(), P()) + each * 3
    moves = KernelMoves(mesh.shape["dp"] // 2) if fits_kernels(mesh) else PlainMoves()
    return jax.shard_map(
        functools.partial(local, moves),
        mesh=mesh,
        in_specs=in_specs,
        out_specs=out_specs,
        check_vma=False,
    )
```
